32 devices in a mesh: mode: 2 (over y), col: 16 (over z, x, core).
Axes of the slice: x: 2, y: 2, z: 4, core: 2. Of those that a mesh axis runs over, the one named last changes fastest.
Arguments:
- tensor: float32 [512, 16, 4096], P('mode', 'col'), may hold values from -15 to 15
- start_basis: float32 [512, 128], replicated, may hold values from -6 to 6
Outputs:
- factor: float32 [512, 512], replicated
- basis: float32 [512, 128], replicated
- core: float32 [128, 16, 4096], P(None, 'col', 'mode')
The draws below stay inside these ranges and needn't reach their ends.
All inputs are finite; a program needn't handle non-finite values.
Results may differ from the reference program's by a relative error of at most 0.00018.
Values sent between devices are 32-bit elements; how exact they have to be, the bound alone decides.
A program may use at most 64 MiB of HBM per device.

```python
import math
import jax
import jax.numpy as jnp
from jax import lax

I1 = 512
RANK = 128
J_LEN = 4096
POWER = 2
I2_LEN = 16


def draw_tensor(key, part):
    scale_key = jax.random.fold_in(key, 11)
    value_key = jax.random.fold_in(key, 23)
    scales = jnp.exp(jax.random.uniform(scale_key, (I1, 1, 1), jnp.float32, 0.0, math.log(2.0)))
    values = jnp.clip(jax.random.normal(value_key, (I1, I2_LEN, J_LEN), jnp.float32), -6.0, 6.0)
    return (scales * values).astype(jnp.float32)


def centred(rng, dims, width, reach, held_as=jnp.bfloat16):
    drawn = jax.random.normal(rng, dims, jnp.float32) * width
    return jnp.minimum(jnp.maximum(drawn, -reach), reach).astype(held_as)


def setup_inputs(seed: int = 0) -> dict:
    arg_keys = jax.random.split(jax.random.key(seed), 3)
    return {
        "tensor": draw_tensor(jax.random.fold_in(arg_keys[2], 71), 0),
        "start_basis": centred(arg_keys[1], (I1, RANK), 1.0, 6.0, jnp.float32),
    }


def lower_chol(matrix):
    return jnp.linalg.cholesky(matrix)

def orthonormal(image):
    small = lower_chol(jnp.dot(image.T.astype(jnp.float32), image.astype(jnp.float32), precision=lax.Precision.HIGHEST, preferred_element_type=jnp.float32))
    return jax.scipy.linalg.solve_triangular(small, image.T, lower=True).T

def reference(tensor, start_basis):
    unfolded = tensor.reshape(I1, -1)
    columns = unfolded.shape[1]
    gram = jnp.dot(unfolded.astype(jnp.float32), unfolded.T.astype(jnp.float32), precision=lax.Precision.HIGHEST, preferred_element_type=jnp.float32)
    factor = lower_chol(gram / columns)
    basis = start_basis
    for step in range(POWER):
        inner = jnp.dot(factor.T.astype(jnp.float32), basis.astype(jnp.float32), precision=lax.Precision.HIGHEST, preferred_element_type=jnp.float32)
        image = jnp.dot(factor.astype(jnp.float32), inner.astype(jnp.float32), precision=lax.Precision.HIGHEST, preferred_element_type=jnp.float32)
        basis = orthonormal(image)
    core = jnp.dot(basis.T.astype(jnp.float32), unfolded.astype(jnp.float32), precision=lax.Precision.HIGHEST, preferred_element_type=jnp.float32)
    return (factor, basis, core.reshape(RANK, I2_LEN, J_LEN))
```

```python
import functools

import jax
import jax.numpy as jnp
from jax import lax
from jax.experimental import pallas as pl
from jax.experimental.pallas import tpu as pltpu
from jax.sharding import PartitionSpec as P

POWER = 2
BLOCK = 128
PANEL = 8
CHUNK = 512
MESH = pl.DeviceIdType.MESH


def halves(value):
    high = value.astype(jnp.bfloat16)
    low = (value - high.astype(jnp.float32)).astype(jnp.bfloat16)
    return high, low


def contract(left, right, dims):
    return lax.dot_general(left, right, (dims, ((), ())), preferred_element_type=jnp.float32)


def exact(left, right, dims):
    return lax.dot_general(
        left, right, (dims, ((), ())), precision=lax.Precision.HIGHEST,
        preferred_element_type=jnp.float32,
    )


NN = ((1,), (0,))
NT = ((1,), (1,))
TN = ((0,), (0,))


def split3(value):
    high = value.astype(jnp.bfloat16).astype(jnp.float32)
    rest = value - high
    middle = rest.astype(jnp.bfloat16).astype(jnp.float32)
    return high, middle, rest - middle


def eliminate_panel(aug, j):
    size, width = aug.shape
    first = PANEL * j
    rows = [aug[first + t : first + t + 1, :] for t in range(PANEL)]
    entry = {}
    for t in range(PANEL):
        for s in range(t, PANEL):
            value = rows[t][:, first + s : first + s + 1]
            entry[s, t] = jnp.broadcast_to(value, (1, size))
    pivots = []
    for t in range(PANEL):
        pivot = entry[t, t]
        pivots.append(pivot)
        inverse = 1.0 / pivot
        for s in range(t + 1, PANEL):
            ratio = entry[s, t] * inverse
            for u in range(s, PANEL):
                entry[u, s] = entry[u, s] - ratio * entry[u, t]
            rows[s] = rows[s] - jnp.concatenate([ratio] * (width // size), axis=1) * rows[t]
    done = []
    for t in range(PANEL):
        scale = lax.rsqrt(pivots[t])
        done.append(rows[t] * jnp.concatenate([scale] * (width // size), axis=1))
    panel = jnp.concatenate(done, axis=0)
    aug[first : first + PANEL, :] = panel
    below = first + PANEL
    if below < size:
        high, middle, low = split3(panel)
        left = jnp.concatenate([high, high, middle, high, low, middle], axis=0).astype(jnp.bfloat16)
        right = jnp.concatenate([high, middle, high, low, high, middle], axis=0).astype(jnp.bfloat16)
        aug[below:size, :] = aug[below:size, :] - contract(left[:, below:size], right, TN)


def eliminate(augs):
    for j in range(BLOCK // PANEL):
        for aug in augs:
            eliminate_panel(aug, j)


def load_augmented(aug, matrix):
    size = matrix.shape[0]
    row = lax.broadcasted_iota(jnp.int32, (size, size), 0)
    column = lax.broadcasted_iota(jnp.int32, (size, size), 1)
    aug[:, 0:size] = matrix
    aug[:, size : 2 * size] = jnp.where(row == column, 1.0, 0.0).astype(jnp.float32)


def lower_blocks(blocks):
    return [(i, k) for i in range(blocks) for k in range(i + 1)]


def stages_of(modes, cols):
    stages, stride = [], 1
    first = 2 if cols % 2 == 0 else 1
    if first > 1:
        stages.append((1, first, False))
        stride = first
    second = 2 if (cols // stride) % 2 == 0 else 1
    stages.append((stride, second, True))
    stride *= second
    if cols // stride > 1:
        stages.append((stride, cols // stride, False))
    return stages


def round_up(value, unit):
    return -(-value // unit) * unit


def layout_of(size, modes, cols):
    pairs = lower_blocks(size // BLOCK)
    rows = size // modes
    inner = []
    if rows % BLOCK == 0 and modes > 1:
        inner = lower_blocks(rows // BLOCK)
    per = rows // BLOCK
    extent = round_up(len(inner) * BLOCK, 8 * cols)
    where = {}
    for m in range(modes):
        for n, (i, k) in enumerate(inner):
            where[m * per + i, m * per + k] = m * extent + n * BLOCK
    outer = [pair for pair in pairs if pair not in where]
    for n, pair in enumerate(outer):
        where[pair] = modes * extent + n * BLOCK
    return where, inner, extent, outer, round_up(len(outer) * BLOCK, 8 * modes * cols)


def members_of(stages, modes):
    return [count * (modes if with_mode else 1) for _, count, with_mode in stages]


def gather_kernel(modes, cols, x_ref, flat_ref, total_ref, local, acc_in, acc_out, main, cross, *rest):
    mode, col = lax.axis_index("mode"), lax.axis_index("col")
    all_stages = stages_of(modes, cols)
    col_stages = [(stride, count, False) for stride, count, _ in all_stages]
    n = len(all_stages)
    slots_in, slots_out = rest[:n], rest[n : 2 * n]
    local_sem, piece_send, piece_recv, swap_send, swap_recv, in_sems, out_sems, share_in, share_out = rest[2 * n :]
    rows, depth, length = x_ref.shape
    size = rows * modes
    width = length // modes
    chunk = min(CHUNK, width)
    per = width // chunk
    chunks = depth * per
    where, inner, in_extent, outer, out_extent = layout_of(size, modes, cols)

    def position(stage):
        stride, count, with_mode = stage
        place = lax.rem(lax.div(col, stride), count)
        return place * modes + mode if with_mode else place

    def members(stage):
        return stage[1] * (modes if stage[2] else 1)

    def peer(stage, offset):
        stride, count, with_mode = stage
        other = lax.rem(position(stage) + offset, members(stage))
        place = lax.div(other, modes) if with_mode else other
        there = col + (place - lax.rem(lax.div(col, stride), count)) * stride
        return other, (lax.rem(other, modes) if with_mode else mode, there)

    partners = [(lax.rem(mode + d, modes), col) for d in range(1, modes)]
    greeted = []
    for stage in all_stages:
        greeted += [peer(stage, d)[1] for d in range(1, members(stage))]
    barrier = pltpu.get_barrier_semaphore()
    for device in greeted:
        pl.semaphore_signal(barrier, inc=1, device_id=device, device_id_type=MESH)
    pl.semaphore_wait(barrier, len(greeted))

    own_rows = pl.ds(pl.multiple_of(mode * rows, rows), rows)

    def spans(c):
        layer, part = lax.div(c, per), lax.rem(c, per)
        return layer, part * chunk, pl.multiple_of(layer * width + part * chunk, chunk)

    def piece(c, d):
        layer, start, target = spans(c)
        source = pl.multiple_of(lax.rem(mode + d, modes) * width + start, chunk)
        return pltpu.make_async_remote_copy(
            src_ref=x_ref.at[:, layer, pl.ds(source, chunk)],
            dst_ref=flat_ref.at[own_rows, pl.ds(target, chunk)],
            send_sem=piece_send.at[d - 1, c],
            recv_sem=piece_recv.at[d - 1, c],
            device_id=partners[d - 1],
            device_id_type=MESH,
        )

    def load(c):
        layer, part = lax.div(c, per * modes), lax.rem(c, per * modes)
        source = pl.multiple_of(part * chunk, chunk)
        target = pl.multiple_of(layer * length + part * chunk, chunk)
        return pltpu.make_async_copy(
            x_ref.at[:, layer, pl.ds(source, chunk)], local.at[:, pl.ds(target, chunk)], local_sem.at[c]
        ), target

    def begin(c, carry):
        for d in range(1, modes):
            piece(c, d).start()
        return carry

    def begin_load(c, carry):
        load(c)[0].start()
        return carry

    early = max(chunks // 2, 1)
    lax.fori_loop(0, early, begin, 0)
    lax.fori_loop(0, chunks * modes, begin_load, 0)

    main[...] = jnp.zeros_like(main)
    cross[...] = jnp.zeros_like(cross)

    def accumulate_in(c, carry):
        copy, target = load(c)
        copy.wait()
        if inner:
            high, low = halves(local[:, pl.ds(target, chunk)])
            main[0:rows, 0:rows] += contract(high, high, NT)
            cross[0:rows, 0:rows] += contract(high, low, NT)
        return carry

    lax.fori_loop(0, chunks * modes, accumulate_in, 0)
    for layer in range(depth):
        source = pl.multiple_of(layer * length + mode * width, chunk)
        flat_ref[own_rows, layer * width : (layer + 1) * width] = local[:, pl.ds(source, width)]

    def pack(acc, pairs, extent):
        for at, (i, k) in enumerate(pairs):
            tall, wide = slice(i * BLOCK, (i + 1) * BLOCK), slice(k * BLOCK, (k + 1) * BLOCK)
            acc[at * BLOCK : (at + 1) * BLOCK, :] = main[tall, wide] + (cross[tall, wide] + cross[wide, tall].T)
        used = len(pairs) * BLOCK
        if used < extent:
            acc[used:, :] = jnp.zeros((extent - used, BLOCK), jnp.float32)

    def scatter_sum(stages, acc, extent, slots, sems, target):
        base, bases = 0, []
        for g, stage in enumerate(stages):
            count = members(stage)
            part = extent // count
            copies = []
            for d in range(1, count):
                other, device = peer(stage, d)
                copy = pltpu.make_async_remote_copy(
                    src_ref=acc.at[pl.ds(pl.multiple_of(base + other * part, 8), part), :],
                    dst_ref=slots[g].at[d - 1],
                    send_sem=sems.at[0, g, d - 1],
                    recv_sem=sems.at[1, g, d - 1],
                    device_id=device,
                    device_id_type=MESH,
                )
                copy.start()
                copies.append(copy)
            base = base + position(stage) * part
            extent = part
            bases.append((base, part))
            for copy in copies:
                copy.wait()
            mine = pl.ds(pl.multiple_of(base, 8), part)
            added = acc[mine, :]
            for d in range(1, count):
                added = added + slots[g][d - 1]
            if g < len(stages) - 1:
                acc[mine, :] = added
            else:
                total_ref[pl.ds(pl.multiple_of(target + base, 8), part), :] = added
        return bases

    def share(stages, bases, targets, sems):
        for g in reversed(range(len(stages))):
            stage = stages[g]
            base, part = bases[g]
            copies = []
            for d in range(1, members(stage)):
                for t, target in enumerate(targets):
                    mine = pl.ds(pl.multiple_of(target + base, 8), part)
                    copy = pltpu.make_async_remote_copy(
                        src_ref=total_ref.at[mine, :],
                        dst_ref=total_ref.at[mine, :],
                        send_sem=sems.at[0, g, (d - 1) * len(targets) + t],
                        recv_sem=sems.at[1, g, (d - 1) * len(targets) + t],
                        device_id=peer(stage, d)[1],
                        device_id_type=MESH,
                    )
                    copy.start()
                    copies.append(copy)
            for copy in copies:
                copy.wait()

    def accumulate_out(c, carry):
        for d in range(1, modes):
            piece(c, d).wait_recv()
        high, low = halves(flat_ref[:, pl.ds(spans(c)[2], chunk)])
        if inner:
            for m in range(1, modes):
                tall, wide = slice(m * rows, (m + 1) * rows), slice(0, m * rows)
                main[tall, wide] += contract(high[tall, :], high[wide, :], NT) + contract(low[tall, :], high[wide, :], NT)
                cross[tall, wide] += contract(high[tall, :], low[wide, :], NT)
        else:
            main[...] += contract(high, high, NT)
            cross[...] += contract(high, low, NT)
        return carry

    swaps = []
    if inner:
        pack(acc_in, inner, in_extent)
        main[...] = jnp.zeros_like(main)
        cross[...] = jnp.zeros_like(cross)
        bases = scatter_sum(col_stages, acc_in, in_extent, slots_in, in_sems, mode * in_extent)
        base, part = bases[-1]
        mine = pl.ds(pl.multiple_of(mode * in_extent + base, 8), part)
        for d in range(1, modes):
            swap = pltpu.make_async_remote_copy(
                src_ref=total_ref.at[mine, :],
                dst_ref=total_ref.at[mine, :],
                send_sem=swap_send.at[d - 1],
                recv_sem=swap_recv.at[d - 1],
                device_id=partners[d - 1],
                device_id_type=MESH,
            )
            swap.start()
            swaps.append(swap)
    lax.fori_loop(early, chunks, begin, 0)
    lax.fori_loop(0, early, accumulate_out, 0)
    if inner:
        for swap in swaps:
            swap.wait()
        share(col_stages, bases, [m * in_extent for m in range(modes)], share_in)
    lax.fori_loop(early, chunks, accumulate_out, 0)

    pack(acc_out, outer, out_extent)
    bases = scatter_sum(all_stages, acc_out, out_extent, slots_out, out_sems, modes * in_extent)
    share(all_stages, bases, [modes * in_extent], share_out)

    def end(c, carry):
        for d in range(1, modes):
            piece(c, d).wait_send()
        return carry

    lax.fori_loop(0, chunks, end, 0)


def gather(tensor):
    modes, cols = lax.axis_size("mode"), lax.axis_size("col")
    rows, depth, length = tensor.shape
    size = rows * modes
    width = length // modes
    chunks = depth * (width // min(CHUNK, width))
    stages = stages_of(modes, cols)
    _, inner, in_extent, _, out_extent = layout_of(size, modes, cols)
    in_extent = max(in_extent, 8 * cols)
    slots_in, slots_out, extent_in, extent, most = [], [], in_extent, out_extent, 1
    for stride, count, with_mode in stages:
        extent_in = extent_in // count
        slots_in.append(pltpu.VMEM((max(count - 1, 1), extent_in, BLOCK), jnp.float32))
        count = count * (modes if with_mode else 1)
        extent = extent // count
        slots_out.append(pltpu.VMEM((max(count - 1, 1), extent, BLOCK), jnp.float32))
        most = max(most, count - 1)
    dma = pltpu.SemaphoreType.DMA
    vmem = pl.BlockSpec(memory_space=pltpu.VMEM)
    packed = (modes * in_extent if inner else 0) + out_extent
    return pl.pallas_call(
        functools.partial(gather_kernel, modes, cols),
        out_shape=(
            jax.ShapeDtypeStruct((size, depth * width), jnp.float32),
            jax.ShapeDtypeStruct((packed, BLOCK), jnp.float32),
        ),
        in_specs=[pl.BlockSpec(memory_space=pl.ANY)],
        out_specs=(vmem, vmem),
        scratch_shapes=[
            pltpu.VMEM((rows, depth * length), jnp.float32),
            pltpu.VMEM((in_extent, BLOCK), jnp.float32),
            pltpu.VMEM((out_extent, BLOCK), jnp.float32),
            pltpu.VMEM((size, size), jnp.float32),
            pltpu.VMEM((size, size), jnp.float32),
            *slots_in,
            *slots_out,
            dma((chunks * modes,)),
            *[dma((max(modes - 1, 1), chunks))] * 2,
            *[dma((max(modes - 1, 1),))] * 2,
            *[dma((2, len(stages), most))] * 2,
            dma((2, len(stages), most * modes)),
            dma((2, len(stages), most)),
        ],
        compiler_params=pltpu.CompilerParams(collective_id=0, has_side_effects=True),
        name="gather",
    )(tensor)


def linear_kernel(columns, where, packed_ref, start_ref, flat_ref, factor_ref, basis_ref, core_ref, gram, work, image, aug_f, aug_b, core, core_sem):
    size, rank = start_ref.shape
    blocks = size // BLOCK
    row = lax.broadcasted_iota(jnp.int32, (BLOCK, BLOCK), 0)
    column = lax.broadcasted_iota(jnp.int32, (BLOCK, BLOCK), 1)
    scale = 1.0 / columns
    for (i, k), at in where.items():
        scaled = packed_ref[at : at + BLOCK, :] * scale
        gram[i * BLOCK : (i + 1) * BLOCK, k * BLOCK : (k + 1) * BLOCK] = scaled
        work[i * BLOCK : (i + 1) * BLOCK, k * BLOCK : (k + 1) * BLOCK] = scaled
        if i != k:
            gram[k * BLOCK : (k + 1) * BLOCK, i * BLOCK : (i + 1) * BLOCK] = scaled.T

    for step in range(max(blocks, POWER)):
        augs = []
        if step < blocks:
            at = step * BLOCK
            load_augmented(aug_f, work[at : at + BLOCK, at : at + BLOCK])
            augs.append(aug_f)
        if step < POWER:
            source = start_ref if step == 0 else basis_ref
            image[...] = exact(gram[...], source[...], NN)
            load_augmented(aug_b, exact(image[...], image[...], TN))
            augs.append(aug_b)
        eliminate(augs)
        if step < POWER:
            basis_ref[...] = exact(image[...], aug_b[:, rank : 2 * rank], NT)
        if step < blocks:
            upper = jnp.where(row <= column, aug_f[:, 0:BLOCK], 0.0)
            factor_ref[at : at + BLOCK, at : at + BLOCK] = upper.T
            if step > 0:
                factor_ref[0:at, at : at + BLOCK] = jnp.zeros((at, BLOCK), jnp.float32)
            below = at + BLOCK
            if below < size:
                inverse = aug_f[:, BLOCK : 2 * BLOCK]
                left = exact(work[below:size, at : at + BLOCK], inverse, NT)
                factor_ref[below:size, at : at + BLOCK] = left
                work[below:size, below:size] = work[below:size, below:size] - exact(left, left, NT)

    high, low = halves(basis_ref[...])
    depth, length = core_ref.shape[1:]
    width = min(CHUNK, length)
    copies = []
    for start in range(0, depth * length, width):
        part = slice(start, start + width)
        flat_high, flat_low = halves(flat_ref[:, part])
        core[:, part] = contract(high, flat_high, TN) + contract(high, flat_low, TN) + contract(low, flat_high, TN)
        layer, offset = divmod(start, length)
        copy = pltpu.make_async_copy(
            core.at[:, part], core_ref.at[:, layer, offset : offset + width], core_sem.at[len(copies)]
        )
        copy.start()
        copies.append(copy)
    for copy in copies:
        copy.wait()


def linear(columns, depth, packed, start_basis, flat):
    size, rank = start_basis.shape
    length = flat.shape[1] // depth
    where = layout_of(size, lax.axis_size("mode"), lax.axis_size("col"))[0]
    vmem = pl.BlockSpec(memory_space=pltpu.VMEM)
    return pl.pallas_call(
        functools.partial(linear_kernel, columns, where),
        out_shape=(
            jax.ShapeDtypeStruct((size, size), jnp.float32),
            jax.ShapeDtypeStruct((size, rank), jnp.float32),
            jax.ShapeDtypeStruct((rank, depth, length), jnp.float32),
        ),
        in_specs=[vmem] * 3,
        out_specs=(vmem, vmem, pl.BlockSpec(memory_space=pl.ANY)),
        scratch_shapes=[
            pltpu.VMEM((size, size), jnp.float32),
            pltpu.VMEM((size, size), jnp.float32),
            pltpu.VMEM((size, rank), jnp.float32),
            pltpu.VMEM((BLOCK, 2 * BLOCK), jnp.float32),
            pltpu.VMEM((rank, 2 * rank), jnp.float32),
            pltpu.VMEM((rank, flat.shape[1]), jnp.float32),
            pltpu.SemaphoreType.DMA((flat.shape[1] // min(CHUNK, length),)),
        ],
        name="linear",
    )(packed, start_basis, flat)


def fast_case(modes, cols, shape):
    rows, depth, length = shape
    return modes == 2 and depth == 1 and rows % (2 * BLOCK) == 0 and cols % 2 == 0 and cols > 2 and length % (2 * BLOCK) == 0


STRIPS = 8
LATE = 2
EARLY = 3
SEMAPHORES = 240


def fast_layout(rows, cols):
    per = rows // BLOCK
    strip = rows // STRIPS
    first = rows - LATE * strip
    inner = lower_blocks(per)
    unit = 8 * cols
    extents = [round_up(len(inner) * BLOCK, unit), round_up(first * per, unit), round_up((rows - first) * per, unit)]
    starts, at = [], 0
    for extent in extents:
        starts.append(at)
        at += 2 * extent
    return per, strip, first, inner, extents, starts, at


def fast_gather_kernel(cols, columns, x_ref, recv_out, total_ref, lead_ref, inverse_ref, local, recv, own_high, own_low, main, cross, work, aug, acc_in, acc_a, acc_b, *rest):
    slots, sems = rest[:-1], rest[-1]
    mode, col = lax.axis_index("mode"), lax.axis_index("col")
    other_mode = 1 - mode
    rows, _, length = x_ref.shape
    width = length // 2
    chips = cols // 2
    per, strip, first, inner, extents, starts, _ = fast_layout(rows, cols)
    core, chip = lax.rem(col, 2), lax.div(col, 2)
    counter = [0]
    pending = []

    def sem():
        counter[0] += 1
        return sems.at[counter[0] - 1]

    def push(source, target, device):
        copy = pltpu.make_async_remote_copy(
            src_ref=source, dst_ref=target, send_sem=sem(), recv_sem=sem(), device_id=device, device_id_type=MESH
        )
        copy.start()
        pending.append(copy)
        return copy

    sibling = (mode, chip * 2 + 1 - core)
    partner = (other_mode, col)
    plane = []
    for d in range(1, chips):
        place = lax.rem(chip + d, chips)
        plane.append((place, (mode, place * 2 + core)))
    across = [(other_mode, lax.rem(chip + d, chips) * 2 + core) for d in range(chips)]

    greeted = [sibling] + [device for _, device in plane] + across
    barrier = pltpu.get_barrier_semaphore()
    for device in greeted:
        pl.semaphore_signal(barrier, inc=1, device_id=device, device_id_type=MESH)
    pl.semaphore_wait(barrier, len(greeted))

    pieces = []
    away = pl.ds(pl.multiple_of(other_mode * width, width), width)

    def send_piece(k):
        span = slice(k * strip, (k + 1) * strip)
        pieces.append(push(x_ref.at[span, 0, away], recv.at[span, :], partner))

    for k in range(EARLY):
        send_piece(k)

    loads = []
    part = length // 4
    for c in range(4):
        span = slice(c * part, (c + 1) * part)
        copy = pltpu.make_async_copy(x_ref.at[:, 0, span], local.at[:, span], sem())
        copy.start()
        loads.append(copy)
    for c in range(4):
        loads[c].wait()
        high, low = halves(local[:, c * part : (c + 1) * part])
        if c == 0:
            main[...] = contract(high, high, NT)
            cross[...] = contract(high, low, NT)
        else:
            main[...] += contract(high, high, NT)
            cross[...] += contract(high, low, NT)

    for at, (i, k) in enumerate(inner):
        tall, wide = slice(i * BLOCK, (i + 1) * BLOCK), slice(k * BLOCK, (k + 1) * BLOCK)
        acc_in[at * BLOCK : (at + 1) * BLOCK, :] = main[tall, wide] + (cross[tall, wide] + cross[wide, tall].T)

    def fill(acc, used):
        if used < acc.shape[0]:
            acc[used:, :] = jnp.zeros((acc.shape[0] - used, BLOCK), jnp.float32)

    def rows_at(base, count):
        return pl.ds(pl.multiple_of(base, 8), count)

    def core_send(acc, slot):
        half = acc.shape[0] // 2
        return push(acc.at[rows_at((1 - core) * half, half), :], slot.at[...], sibling)

    def core_add(acc, slot, copy):
        half = acc.shape[0] // 2
        copy.wait_recv()
        mine = rows_at(core * half, half)
        acc[mine, :] = acc[mine, :] + slot[...]

    def plane_send(acc, slot):
        half = acc.shape[0] // 2
        share = half // chips
        copies = []
        for d, (place, device) in enumerate(plane):
            copies.append(push(acc.at[rows_at(core * half + place * share, share), :], slot.at[d], device))
        return copies

    def plane_add(acc, slot, copies, start):
        half = acc.shape[0] // 2
        share = half // chips
        base = core * half + chip * share
        for copy in copies:
            copy.wait_recv()
        added = acc[rows_at(base, share), :]
        for d in range(chips - 1):
            added = added + slot[d]
        total_ref[rows_at(start + mode * acc.shape[0] + base, share), :] = added

    def swap(acc, start):
        half = acc.shape[0] // 2
        share = half // chips
        mine = rows_at(start + mode * acc.shape[0] + core * half + chip * share, share)
        return push(total_ref.at[mine, :], total_ref.at[mine, :], partner)

    def plane_share(acc, start):
        half = acc.shape[0] // 2
        share = half // chips
        copies = []
        for _, device in plane:
            for m in range(2):
                mine = rows_at(start + m * acc.shape[0] + core * half + chip * share, share)
                copies.append(push(total_ref.at[mine, :], total_ref.at[mine, :], device))
        return copies

    def direct_share(acc, start):
        half = acc.shape[0] // 2
        share = half // chips
        mine = rows_at(start + mode * acc.shape[0] + core * half + chip * share, share)
        devices = [device for _, device in plane] + across
        return [push(total_ref.at[mine, :], total_ref.at[mine, :], device) for device in devices]

    def core_share(acc, start):
        half = acc.shape[0] // 2
        copies = []
        for m in range(2):
            mine = rows_at(start + m * acc.shape[0] + core * half, half)
            copies.append(push(total_ref.at[mine, :], total_ref.at[mine, :], sibling))
        return copies

    def arrive(copies):
        for copy in copies:
            copy.wait_recv()

    outgoing = []

    def strips(begin, end, acc, offset, tall):
        arrive(pieces[begin:end])
        span = slice(begin * strip, end * strip)
        copy = pltpu.make_async_copy(recv.at[span, :], recv_out.at[span, :], sem())
        copy.start()
        outgoing.append(copy)
        high, low = halves(recv[span, :])
        value = contract(high, own_high[...], NT) + (contract(high, own_low[...], NT) + contract(low, own_high[...], NT))
        for c in range(per):
            at = c * tall + begin * strip - offset
            acc[at : at + (end - begin) * strip, :] = value[:, c * BLOCK : (c + 1) * BLOCK]

    fill(acc_in, len(inner) * BLOCK)
    copy = core_send(acc_in, slots[0])
    mine = local[:, pl.ds(pl.multiple_of(mode * width, width), width)]
    high, low = halves(mine)
    own_high[...] = high
    own_low[...] = low
    core_add(acc_in, slots[0], copy)
    copies = plane_send(acc_in, slots[1])
    plane_add(acc_in, slots[1], copies, starts[0])
    copy = swap(acc_in, starts[0])
    for k in range(EARLY, STRIPS):
        send_piece(k)
    strips(0, 2, acc_a, 0, first)
    arrive([copy])
    arrive(plane_share(acc_in, starts[0]))
    arrive(core_share(acc_in, starts[0]))

    scale = 1.0 / columns
    for at, (i, k) in enumerate(inner):
        tall, wide = slice(i * BLOCK, (i + 1) * BLOCK), slice(k * BLOCK, (k + 1) * BLOCK)
        work[tall, wide] = total_ref[starts[0] + at * BLOCK : starts[0] + (at + 1) * BLOCK, :] * scale
    lead_ref[...] = jnp.zeros_like(lead_ref)
    inverse_ref[...] = jnp.zeros_like(inverse_ref)
    row = lax.broadcasted_iota(jnp.int32, (BLOCK, BLOCK), 0)
    column = lax.broadcasted_iota(jnp.int32, (BLOCK, BLOCK), 1)
    for step in range(per):
        at, below = step * BLOCK, (step + 1) * BLOCK
        load_augmented(aug, work[at:below, at:below])
        eliminate([aug])
        lead_ref[at:below, at:below] = jnp.where(row <= column, aug[:, 0:BLOCK], 0.0).T
        inverse = aug[:, BLOCK : 2 * BLOCK]
        inverse_ref[at:below, at:below] = inverse
        if step > 0:
            inverse_ref[at:below, 0:at] = -exact(inverse, exact(lead_ref[at:below, 0:at], inverse_ref[0:at, 0:at], NN), NN)
        if below < rows:
            left = exact(work[below:rows, at:below], inverse, NT)
            lead_ref[below:rows, at:below] = left
            work[below:rows, below:rows] = work[below:rows, below:rows] - exact(left, left, NT)
        if step == 0:
            strips(2, 4, acc_a, 0, first)
    strips(4, STRIPS - LATE, acc_a, 0, first)
    fill(acc_a, first * per)
    core_add(acc_a, slots[2], core_send(acc_a, slots[2]))
    copies = plane_send(acc_a, slots[3])
    for k in range(STRIPS - LATE, STRIPS - 1):
        strips(k, k + 1, acc_b, first, rows - first)
    plane_add(acc_a, slots[3], copies, starts[1])
    copy_a = swap(acc_a, starts[1])
    strips(STRIPS - 1, STRIPS, acc_b, first, rows - first)
    fill(acc_b, (rows - first) * per)
    core_add(acc_b, slots[4], core_send(acc_b, slots[4]))
    copies = plane_send(acc_b, slots[5])
    arrive([copy_a])
    copies_a = plane_share(acc_a, starts[1])
    plane_add(acc_b, slots[5], copies, starts[2])
    copies = direct_share(acc_b, starts[2])
    arrive(copies_a)
    copies_a = core_share(acc_a, starts[1])
    arrive(copies)
    copies = core_share(acc_b, starts[2])
    arrive(copies_a)
    arrive(copies)
    for copy in pending:
        copy.wait_send()
    for copy in outgoing:
        copy.wait()


def fast_gather(tensor, columns):
    cols = lax.axis_size("col")
    rows, _, length = tensor.shape
    width = length // 2
    chips = cols // 2
    _, _, _, _, extents, _, packed = fast_layout(rows, cols)
    slots = []
    for extent in extents:
        slots.append(pltpu.VMEM((extent // 2, BLOCK), jnp.float32))
        slots.append(pltpu.VMEM((chips - 1, extent // cols, BLOCK), jnp.float32))
    vmem = pl.BlockSpec(memory_space=pltpu.VMEM)
    return pl.pallas_call(
        functools.partial(fast_gather_kernel, cols, columns),
        out_shape=(
            jax.ShapeDtypeStruct((rows, width), jnp.float32),
            jax.ShapeDtypeStruct((packed, BLOCK), jnp.float32),
            jax.ShapeDtypeStruct((rows, rows), jnp.float32),
            jax.ShapeDtypeStruct((rows, rows), jnp.float32),
        ),
        in_specs=[pl.BlockSpec(memory_space=pl.ANY)],
        out_specs=(pl.BlockSpec(memory_space=pl.ANY), vmem, vmem, vmem),
        scratch_shapes=[
            pltpu.VMEM((rows, length), jnp.float32),
            pltpu.VMEM((rows, width), jnp.float32),
            pltpu.VMEM((rows, width), jnp.bfloat16),
            pltpu.VMEM((rows, width), jnp.bfloat16),
            pltpu.VMEM((rows, rows), jnp.float32),
            pltpu.VMEM((rows, rows), jnp.float32),
            pltpu.VMEM((rows, rows), jnp.float32),
            pltpu.VMEM((BLOCK, 2 * BLOCK), jnp.float32),
            *[pltpu.VMEM((extent, BLOCK), jnp.float32) for extent in extents],
            *slots,
            pltpu.SemaphoreType.DMA((SEMAPHORES,)),
        ],
        compiler_params=pltpu.CompilerParams(collective_id=0, has_side_effects=True),
        name="fast_gather",
    )(tensor)


def fast_linear_kernel(cols, columns, total_ref, lead_ref, inverse_ref, start_ref, x_ref, recv_ref, factor_ref, basis_ref, core_ref, gram, work, image, aug_f, aug_b, flat, core, flat_sem, core_sem):
    mode = lax.axis_index("mode")
    size, rank = start_ref.shape
    rows = size // 2
    width = recv_ref.shape[1]
    per, _, first, inner, extents, starts, _ = fast_layout(rows, cols)
    own = pl.ds(pl.multiple_of(mode * rows, rows), rows)
    away = pl.ds(pl.multiple_of((1 - mode) * rows, rows), rows)
    half = pl.ds(pl.multiple_of(mode * width, width), width)
    loads = [
        pltpu.make_async_copy(x_ref.at[:, 0, half], flat.at[own, :], flat_sem.at[0]),
        pltpu.make_async_copy(recv_ref, flat.at[away, :], flat_sem.at[1]),
    ]
    for load in loads:
        load.start()

    scale = 1.0 / columns
    for m in range(2):
        for at, (i, k) in enumerate(inner):
            begin = starts[0] + m * extents[0] + at * BLOCK
            block = total_ref[begin : begin + BLOCK, :] * scale
            tall = slice(m * rows + i * BLOCK, m * rows + (i + 1) * BLOCK)
            wide = slice(m * rows + k * BLOCK, m * rows + (k + 1) * BLOCK)
            gram[tall, wide] = block
            if i != k:
                gram[wide, tall] = block.T
    pair = []
    for m in range(2):
        blocks = []
        for c in range(per):
            a = starts[1] + m * extents[1] + c * first
            b = starts[2] + m * extents[2] + c * (rows - first)
            blocks.append(jnp.concatenate([total_ref[a : a + first, :], total_ref[b : b + rows - first, :]], axis=0))
        pair.append(jnp.concatenate(blocks, axis=1))
    lower = (pair[0] + pair[1].T) * scale
    gram[rows:size, 0:rows] = lower
    gram[0:rows, rows:size] = lower.T

    row = lax.broadcasted_iota(jnp.int32, (BLOCK, BLOCK), 0)
    column = lax.broadcasted_iota(jnp.int32, (BLOCK, BLOCK), 1)
    factor_ref[0:rows, 0:rows] = lead_ref[...]
    factor_ref[0:rows, rows:size] = jnp.zeros((rows, rows), jnp.float32)
    left = exact(lower, inverse_ref[...], NT)
    factor_ref[rows:size, 0:rows] = left
    work[...] = gram[rows:size, rows:size] - exact(left, left, NT)

    for step in range(max(per, POWER)):
        augs = []
        at, below = step * BLOCK, (step + 1) * BLOCK
        if step < POWER:
            source = start_ref if step == 0 else basis_ref
            image[...] = exact(gram[...], source[...], NN)
            load_augmented(aug_b, exact(image[...], image[...], TN))
            augs.append(aug_b)
        if step < per:
            load_augmented(aug_f, work[at:below, at:below])
            augs.append(aug_f)
        eliminate(augs)
        if step < POWER:
            basis_ref[...] = exact(image[...], aug_b[:, rank : 2 * rank], NT)
        if step < per:
            upper = jnp.where(row <= column, aug_f[:, 0:BLOCK], 0.0)
            factor_ref[rows + at : rows + below, rows + at : rows + below] = upper.T
            if step > 0:
                factor_ref[rows : rows + at, rows + at : rows + below] = jnp.zeros((at, BLOCK), jnp.float32)
            if below < rows:
                left = exact(work[below:rows, at:below], aug_f[:, BLOCK : 2 * BLOCK], NT)
                factor_ref[rows + below : size, rows + at : rows + below] = left
                work[below:rows, below:rows] = work[below:rows, below:rows] - exact(left, left, NT)

    for load in loads:
        load.wait()
    high, low = halves(basis_ref[...])
    piece = min(CHUNK, width)
    copies = []
    for start in range(0, width, piece):
        part = slice(start, start + piece)
        flat_high, flat_low = halves(flat[:, part])
        core[:, part] = contract(high, flat_high, TN) + contract(high, flat_low, TN) + contract(low, flat_high, TN)
        copy = pltpu.make_async_copy(core.at[:, part], core_ref.at[:, 0, part], core_sem.at[len(copies)])
        copy.start()
        copies.append(copy)
    for copy in copies:
        copy.wait()


def fast_linear(columns, total, lead, inverse, start_basis, tensor, recv):
    size, rank = start_basis.shape
    rows, width = recv.shape
    vmem = pl.BlockSpec(memory_space=pltpu.VMEM)
    anywhere = pl.BlockSpec(memory_space=pl.ANY)
    return pl.pallas_call(
        functools.partial(fast_linear_kernel, lax.axis_size("col"), columns),
        out_shape=(
            jax.ShapeDtypeStruct((size, size), jnp.float32),
            jax.ShapeDtypeStruct((size, rank), jnp.float32),
            jax.ShapeDtypeStruct((rank, 1, width), jnp.float32),
        ),
        in_specs=[vmem, vmem, vmem, vmem, anywhere, anywhere],
        out_specs=(vmem, vmem, anywhere),
        scratch_shapes=[
            pltpu.VMEM((size, size), jnp.float32),
            pltpu.VMEM((rows, rows), jnp.float32),
            pltpu.VMEM((size, rank), jnp.float32),
            pltpu.VMEM((BLOCK, 2 * BLOCK), jnp.float32),
            pltpu.VMEM((rank, 2 * rank), jnp.float32),
            pltpu.VMEM((size, width), jnp.float32),
            pltpu.VMEM((rank, width), jnp.float32),
            pltpu.SemaphoreType.DMA((2,)),
            pltpu.SemaphoreType.DMA((width // min(CHUNK, width),)),
        ],
        name="fast_linear",
    )(total, lead, inverse, start_basis, tensor, recv)


def per_device(tensor, start_basis):
    modes, cols = lax.axis_size("mode"), lax.axis_size("col")
    depth = tensor.shape[1]
    columns = depth * tensor.shape[2] * cols
    if fast_case(modes, cols, tensor.shape):
        recv, total, lead, inverse = fast_gather(tensor, columns)
        return fast_linear(columns, total, lead, inverse, start_basis, tensor, recv)
    flat, packed = gather(tensor)
    return linear(columns, depth, packed, start_basis, flat)


def solution(mesh):
    in_specs = (P("mode", "col", None), P())
    out_specs = (P(), P(), P(None, "col", "mode"))
    return jax.shard_map(
        per_device, mesh=mesh, in_specs=in_specs, out_specs=out_specs, check_vma=False
    )
```

```python
import functools

import jax
import jax.numpy as jnp
from jax import lax
from jax.experimental import pallas as pl
from jax.experimental.pallas import tpu as pltpu
from jax.sharding import PartitionSpec as P

POWER = 2
BLOCK = 128
PANEL = 8
CHUNK = 512
MESH = pl.DeviceIdType.MESH


def halves(value):
    high = value.astype(jnp.bfloat16)
    low = (value - high.astype(jnp.float32)).astype(jnp.bfloat16)
    return high, low


def contract(left, right, dims):
    return lax.dot_general(left, right, (dims, ((), ())), preferred_element_type=jnp.float32)


def exact(left, right, dims):
    return lax.dot_general(
        left, right, (dims, ((), ())), precision=lax.Precision.HIGHEST,
        preferred_element_type=jnp.float32,
    )


NN = ((1,), (0,))
NT = ((1,), (1,))
TN = ((0,), (0,))


def split3(value):
    high = value.astype(jnp.bfloat16).astype(jnp.float32)
    rest = value - high
    middle = rest.astype(jnp.bfloat16).astype(jnp.float32)
    return high, middle, rest - middle


def spread(tile, lane):
    return jnp.broadcast_to(tile[:, lane : lane + 1], tile.shape)


def eliminate_panel(aug, j):
    parts, size, _ = aug.shape
    first = PANEL * j
    after = first + PANEL
    below = after + PANEL
    rows = [[aug[p, pl.ds(first + t, PANEL, stride=0), :] for p in range(parts)] for t in range(PANEL)]
    entry = {}
    for s in range(PANEL):
        for t in range(s + 1):
            entry[s, t] = spread(rows[t][0], first + s)
    if after < size:
        following = [aug[p, after:below, :] for p in range(parts)]
        column = [spread(following[0], first + t) for t in range(PANEL)]
    for t in range(PANEL):
        inverse = 1.0 / entry[t, t]
        for s in range(t + 1, PANEL):
            ratio = entry[s, t] * inverse
            for u in range(s, PANEL):
                entry[u, s] = entry[u, s] - ratio * entry[u, t]
            rows[s] = [a - ratio * b for a, b in zip(rows[s], rows[t])]
        scale = lax.rsqrt(entry[t, t])
        for p in range(parts):
            aug[p, first + t : first + t + 1, :] = (rows[t][p] * scale)[0:1]
        if after < size:
            ratio = column[t] * inverse
            for u in range(t + 1, PANEL):
                column[u] = column[u] - ratio * entry[u, t]
            following = [a - ratio * b for a, b in zip(following, rows[t])]
    if after < size:
        for p in range(parts):
            aug[p, after:below, :] = following[p]
    if below < size:
        rights = []
        for p in range(parts):
            high, middle, low = split3(aug[p, first:after, :])
            if p == 0:
                left = jnp.concatenate([high, high, middle, high, low, middle], axis=0).astype(jnp.bfloat16)
            rights.append(jnp.concatenate([high, middle, high, low, high, middle], axis=0).astype(jnp.bfloat16))
        update = contract(left, jnp.concatenate(rights, axis=1), TN)
        for p in range(parts):
            aug[p, below:size, :] = aug[p, below:size, :] - update[below:size, p * size : (p + 1) * size]


def eliminate(augs):
    for j in range(BLOCK // PANEL):
        for aug in augs:
            eliminate_panel(aug, j)


def load_augmented(aug, matrix):
    size = matrix.shape[0]
    aug[0] = matrix
    if aug.shape[0] > 1:
        row = lax.broadcasted_iota(jnp.int32, (size, size), 0)
        column = lax.broadcasted_iota(jnp.int32, (size, size), 1)
        aug[1] = jnp.where(row == column, 1.0, 0.0).astype(jnp.float32)


def lower_blocks(blocks):
    return [(i, k) for i in range(blocks) for k in range(i + 1)]


def stages_of(modes, cols):
    stages, stride = [], 1
    first = 2 if cols % 2 == 0 else 1
    if first > 1:
        stages.append((1, first, False))
        stride = first
    second = 2 if (cols // stride) % 2 == 0 else 1
    stages.append((stride, second, True))
    stride *= second
    if cols // stride > 1:
        stages.append((stride, cols // stride, False))
    return stages


def round_up(value, unit):
    return -(-value // unit) * unit


def layout_of(size, modes, cols):
    pairs = lower_blocks(size // BLOCK)
    rows = size // modes
    inner = []
    if rows % BLOCK == 0 and modes > 1:
        inner = lower_blocks(rows // BLOCK)
    per = rows // BLOCK
    extent = round_up(len(inner) * BLOCK, 8 * cols)
    where = {}
    for m in range(modes):
        for n, (i, k) in enumerate(inner):
            where[m * per + i, m * per + k] = m * extent + n * BLOCK
    outer = [pair for pair in pairs if pair not in where]
    for n, pair in enumerate(outer):
        where[pair] = modes * extent + n * BLOCK
    return where, inner, extent, outer, round_up(len(outer) * BLOCK, 8 * modes * cols)


def members_of(stages, modes):
    return [count * (modes if with_mode else 1) for _, count, with_mode in stages]


def gather_kernel(modes, cols, x_ref, flat_ref, total_ref, local, acc_in, acc_out, main, cross, *rest):
    mode, col = lax.axis_index("mode"), lax.axis_index("col")
    all_stages = stages_of(modes, cols)
    col_stages = [(stride, count, False) for stride, count, _ in all_stages]
    n = len(all_stages)
    slots_in, slots_out = rest[:n], rest[n : 2 * n]
    local_sem, piece_send, piece_recv, swap_send, swap_recv, in_sems, out_sems, share_in, share_out = rest[2 * n :]
    rows, depth, length = x_ref.shape
    size = rows * modes
    width = length // modes
    chunk = min(CHUNK, width)
    per = width // chunk
    chunks = depth * per
    where, inner, in_extent, outer, out_extent = layout_of(size, modes, cols)

    def position(stage):
        stride, count, with_mode = stage
        place = lax.rem(lax.div(col, stride), count)
        return place * modes + mode if with_mode else place

    def members(stage):
        return stage[1] * (modes if stage[2] else 1)

    def peer(stage, offset):
        stride, count, with_mode = stage
        other = lax.rem(position(stage) + offset, members(stage))
        place = lax.div(other, modes) if with_mode else other
        there = col + (place - lax.rem(lax.div(col, stride), count)) * stride
        return other, (lax.rem(other, modes) if with_mode else mode, there)

    partners = [(lax.rem(mode + d, modes), col) for d in range(1, modes)]
    greeted = []
    for stage in all_stages:
        greeted += [peer(stage, d)[1] for d in range(1, members(stage))]
    barrier = pltpu.get_barrier_semaphore()
    for device in greeted:
        pl.semaphore_signal(barrier, inc=1, device_id=device, device_id_type=MESH)
    pl.semaphore_wait(barrier, len(greeted))

    own_rows = pl.ds(pl.multiple_of(mode * rows, rows), rows)

    def spans(c):
        layer, part = lax.div(c, per), lax.rem(c, per)
        return layer, part * chunk, pl.multiple_of(layer * width + part * chunk, chunk)

    def piece(c, d):
        layer, start, target = spans(c)
        source = pl.multiple_of(lax.rem(mode + d, modes) * width + start, chunk)
        return pltpu.make_async_remote_copy(
            src_ref=x_ref.at[:, layer, pl.ds(source, chunk)],
            dst_ref=flat_ref.at[own_rows, pl.ds(target, chunk)],
            send_sem=piece_send.at[d - 1, c],
            recv_sem=piece_recv.at[d - 1, c],
            device_id=partners[d - 1],
            device_id_type=MESH,
        )

    def load(c):
        layer, part = lax.div(c, per * modes), lax.rem(c, per * modes)
        source = pl.multiple_of(part * chunk, chunk)
        target = pl.multiple_of(layer * length + part * chunk, chunk)
        return pltpu.make_async_copy(
            x_ref.at[:, layer, pl.ds(source, chunk)], local.at[:, pl.ds(target, chunk)], local_sem.at[c]
        ), target

    def begin(c, carry):
        for d in range(1, modes):
            piece(c, d).start()
        return carry

    def begin_load(c, carry):
        load(c)[0].start()
        return carry

    early = max(chunks // 2, 1)
    lax.fori_loop(0, early, begin, 0)
    lax.fori_loop(0, chunks * modes, begin_load, 0)

    main[...] = jnp.zeros_like(main)
    cross[...] = jnp.zeros_like(cross)

    def accumulate_in(c, carry):
        copy, target = load(c)
        copy.wait()
        if inner:
            high, low = halves(local[:, pl.ds(target, chunk)])
            main[0:rows, 0:rows] += contract(high, high, NT)
            cross[0:rows, 0:rows] += contract(high, low, NT)
        return carry

    lax.fori_loop(0, chunks * modes, accumulate_in, 0)
    for layer in range(depth):
        source = pl.multiple_of(layer * length + mode * width, chunk)
        flat_ref[own_rows, layer * width : (layer + 1) * width] = local[:, pl.ds(source, width)]

    def pack(acc, pairs, extent):
        for at, (i, k) in enumerate(pairs):
            tall, wide = slice(i * BLOCK, (i + 1) * BLOCK), slice(k * BLOCK, (k + 1) * BLOCK)
            acc[at * BLOCK : (at + 1) * BLOCK, :] = main[tall, wide] + (cross[tall, wide] + cross[wide, tall].T)
        used = len(pairs) * BLOCK
        if used < extent:
            acc[used:, :] = jnp.zeros((extent - used, BLOCK), jnp.float32)

    def scatter_sum(stages, acc, extent, slots, sems, target):
        base, bases = 0, []
        for g, stage in enumerate(stages):
            count = members(stage)
            part = extent // count
            copies = []
            for d in range(1, count):
                other, device = peer(stage, d)
                copy = pltpu.make_async_remote_copy(
                    src_ref=acc.at[pl.ds(pl.multiple_of(base + other * part, 8), part), :],
                    dst_ref=slots[g].at[d - 1],
                    send_sem=sems.at[0, g, d - 1],
                    recv_sem=sems.at[1, g, d - 1],
                    device_id=device,
                    device_id_type=MESH,
                )
                copy.start()
                copies.append(copy)
            base = base + position(stage) * part
            extent = part
            bases.append((base, part))
            for copy in copies:
                copy.wait()
            mine = pl.ds(pl.multiple_of(base, 8), part)
            added = acc[mine, :]
            for d in range(1, count):
                added = added + slots[g][d - 1]
            if g < len(stages) - 1:
                acc[mine, :] = added
            else:
                total_ref[pl.ds(pl.multiple_of(target + base, 8), part), :] = added
        return bases

    def share(stages, bases, targets, sems):
        for g in reversed(range(len(stages))):
            stage = stages[g]
            base, part = bases[g]
            copies = []
            for d in range(1, members(stage)):
                for t, target in enumerate(targets):
                    mine = pl.ds(pl.multiple_of(target + base, 8), part)
                    copy = pltpu.make_async_remote_copy(
                        src_ref=total_ref.at[mine, :],
                        dst_ref=total_ref.at[mine, :],
                        send_sem=sems.at[0, g, (d - 1) * len(targets) + t],
                        recv_sem=sems.at[1, g, (d - 1) * len(targets) + t],
                        device_id=peer(stage, d)[1],
                        device_id_type=MESH,
                    )
                    copy.start()
                    copies.append(copy)
            for copy in copies:
                copy.wait()

    def accumulate_out(c, carry):
        for d in range(1, modes):
            piece(c, d).wait_recv()
        high, low = halves(flat_ref[:, pl.ds(spans(c)[2], chunk)])
        if inner:
            for m in range(1, modes):
                tall, wide = slice(m * rows, (m + 1) * rows), slice(0, m * rows)
                main[tall, wide] += contract(high[tall, :], high[wide, :], NT) + contract(low[tall, :], high[wide, :], NT)
                cross[tall, wide] += contract(high[tall, :], low[wide, :], NT)
        else:
            main[...] += contract(high, high, NT)
            cross[...] += contract(high, low, NT)
        return carry

    swaps = []
    if inner:
        pack(acc_in, inner, in_extent)
        main[...] = jnp.zeros_like(main)
        cross[...] = jnp.zeros_like(cross)
        bases = scatter_sum(col_stages, acc_in, in_extent, slots_in, in_sems, mode * in_extent)
        base, part = bases[-1]
        mine = pl.ds(pl.multiple_of(mode * in_extent + base, 8), part)
        for d in range(1, modes):
            swap = pltpu.make_async_remote_copy(
                src_ref=total_ref.at[mine, :],
                dst_ref=total_ref.at[mine, :],
                send_sem=swap_send.at[d - 1],
                recv_sem=swap_recv.at[d - 1],
                device_id=partners[d - 1],
                device_id_type=MESH,
            )
            swap.start()
            swaps.append(swap)
    lax.fori_loop(early, chunks, begin, 0)
    lax.fori_loop(0, early, accumulate_out, 0)
    if inner:
        for swap in swaps:
            swap.wait()
        share(col_stages, bases, [m * in_extent for m in range(modes)], share_in)
    lax.fori_loop(early, chunks, accumulate_out, 0)

    pack(acc_out, outer, out_extent)
    bases = scatter_sum(all_stages, acc_out, out_extent, slots_out, out_sems, modes * in_extent)
    share(all_stages, bases, [modes * in_extent], share_out)

    def end(c, carry):
        for d in range(1, modes):
            piece(c, d).wait_send()
        return carry

    lax.fori_loop(0, chunks, end, 0)


def gather(tensor):
    modes, cols = lax.axis_size("mode"), lax.axis_size("col")
    rows, depth, length = tensor.shape
    size = rows * modes
    width = length // modes
    chunks = depth * (width // min(CHUNK, width))
    stages = stages_of(modes, cols)
    _, inner, in_extent, _, out_extent = layout_of(size, modes, cols)
    in_extent = max(in_extent, 8 * cols)
    slots_in, slots_out, extent_in, extent, most = [], [], in_extent, out_extent, 1
    for stride, count, with_mode in stages:
        extent_in = extent_in // count
        slots_in.append(pltpu.VMEM((max(count - 1, 1), extent_in, BLOCK), jnp.float32))
        count = count * (modes if with_mode else 1)
        extent = extent // count
        slots_out.append(pltpu.VMEM((max(count - 1, 1), extent, BLOCK), jnp.float32))
        most = max(most, count - 1)
    dma = pltpu.SemaphoreType.DMA
    vmem = pl.BlockSpec(memory_space=pltpu.VMEM)
    packed = (modes * in_extent if inner else 0) + out_extent
    return pl.pallas_call(
        functools.partial(gather_kernel, modes, cols),
        out_shape=(
            jax.ShapeDtypeStruct((size, depth * width), jnp.float32),
            jax.ShapeDtypeStruct((packed, BLOCK), jnp.float32),
        ),
        in_specs=[pl.BlockSpec(memory_space=pl.ANY)],
        out_specs=(vmem, vmem),
        scratch_shapes=[
            pltpu.VMEM((rows, depth * length), jnp.float32),
            pltpu.VMEM((in_extent, BLOCK), jnp.float32),
            pltpu.VMEM((out_extent, BLOCK), jnp.float32),
            pltpu.VMEM((size, size), jnp.float32),
            pltpu.VMEM((size, size), jnp.float32),
            *slots_in,
            *slots_out,
            dma((chunks * modes,)),
            *[dma((max(modes - 1, 1), chunks))] * 2,
            *[dma((max(modes - 1, 1),))] * 2,
            *[dma((2, len(stages), most))] * 2,
            dma((2, len(stages), most * modes)),
            dma((2, len(stages), most)),
        ],
        compiler_params=pltpu.CompilerParams(collective_id=0, has_side_effects=True),
        name="gather",
    )(tensor)


def linear_kernel(columns, where, packed_ref, start_ref, flat_ref, factor_ref, basis_ref, core_ref, gram, work, image, aug_f, aug_b, core, core_sem):
    size, rank = start_ref.shape
    blocks = size // BLOCK
    row = lax.broadcasted_iota(jnp.int32, (BLOCK, BLOCK), 0)
    column = lax.broadcasted_iota(jnp.int32, (BLOCK, BLOCK), 1)
    scale = 1.0 / columns
    for (i, k), at in where.items():
        scaled = packed_ref[at : at + BLOCK, :] * scale
        gram[i * BLOCK : (i + 1) * BLOCK, k * BLOCK : (k + 1) * BLOCK] = scaled
        work[i * BLOCK : (i + 1) * BLOCK, k * BLOCK : (k + 1) * BLOCK] = scaled
        if i != k:
            gram[k * BLOCK : (k + 1) * BLOCK, i * BLOCK : (i + 1) * BLOCK] = scaled.T

    for step in range(max(blocks, POWER)):
        augs = []
        if step < blocks:
            at = step * BLOCK
            load_augmented(aug_f, work[at : at + BLOCK, at : at + BLOCK])
            augs.append(aug_f)
        if step < POWER:
            source = start_ref if step == 0 else basis_ref
            image[...] = exact(gram[...], source[...], NN)
            load_augmented(aug_b, exact(image[...], image[...], TN))
            augs.append(aug_b)
        eliminate(augs)
        if step < POWER:
            basis_ref[...] = exact(image[...], aug_b[1], NT)
        if step < blocks:
            upper = jnp.where(row <= column, aug_f[0], 0.0)
            factor_ref[at : at + BLOCK, at : at + BLOCK] = upper.T
            if step > 0:
                factor_ref[0:at, at : at + BLOCK] = jnp.zeros((at, BLOCK), jnp.float32)
            below = at + BLOCK
            if below < size:
                inverse = aug_f[1]
                left = exact(work[below:size, at : at + BLOCK], inverse, NT)
                factor_ref[below:size, at : at + BLOCK] = left
                work[below:size, below:size] = work[below:size, below:size] - exact(left, left, NT)

    high, low = halves(basis_ref[...])
    depth, length = core_ref.shape[1:]
    width = min(CHUNK, length)
    copies = []
    for start in range(0, depth * length, width):
        part = slice(start, start + width)
        flat_high, flat_low = halves(flat_ref[:, part])
        core[:, part] = contract(high, flat_high, TN) + contract(high, flat_low, TN) + contract(low, flat_high, TN)
        layer, offset = divmod(start, length)
        copy = pltpu.make_async_copy(
            core.at[:, part], core_ref.at[:, layer, offset : offset + width], core_sem.at[len(copies)]
        )
        copy.start()
        copies.append(copy)
    for copy in copies:
        copy.wait()


def linear(columns, depth, packed, start_basis, flat):
    size, rank = start_basis.shape
    length = flat.shape[1] // depth
    where = layout_of(size, lax.axis_size("mode"), lax.axis_size("col"))[0]
    vmem = pl.BlockSpec(memory_space=pltpu.VMEM)
    return pl.pallas_call(
        functools.partial(linear_kernel, columns, where),
        out_shape=(
            jax.ShapeDtypeStruct((size, size), jnp.float32),
            jax.ShapeDtypeStruct((size, rank), jnp.float32),
            jax.ShapeDtypeStruct((rank, depth, length), jnp.float32),
        ),
        in_specs=[vmem] * 3,
        out_specs=(vmem, vmem, pl.BlockSpec(memory_space=pl.ANY)),
        scratch_shapes=[
            pltpu.VMEM((size, size), jnp.float32),
            pltpu.VMEM((size, size), jnp.float32),
            pltpu.VMEM((size, rank), jnp.float32),
            pltpu.VMEM((2, BLOCK, BLOCK), jnp.float32),
            pltpu.VMEM((2, rank, rank), jnp.float32),
            pltpu.VMEM((rank, flat.shape[1]), jnp.float32),
            pltpu.SemaphoreType.DMA((flat.shape[1] // min(CHUNK, length),)),
        ],
        name="linear",
    )(packed, start_basis, flat)


def fast_case(modes, cols, shape):
    rows, depth, length = shape
    return modes == 2 and depth == 1 and rows % (2 * BLOCK) == 0 and cols % 4 == 0 and length % (2 * BLOCK) == 0


STRIPS = 8
LATE = 4
EARLY = 3
HELD = 2
PIECES = STRIPS + 2


def fast_cuts(strip):
    return sorted([k * strip for k in range(STRIPS + 1)] + [2 * strip + strip // 2, 6 * strip + strip // 2])


def fast_layout(rows, cols):
    per = rows // BLOCK
    strip = rows // STRIPS
    first = rows - LATE * strip
    inner = lower_blocks(per)
    unit = 8 * cols
    extents = [round_up(len(inner) * BLOCK, unit), round_up(first * per, unit), round_up((rows - first) * per, unit)]
    starts, at = [], 0
    for extent in extents:
        starts.append(at)
        at += 2 * extent
    return per, strip, first, inner, extents, starts, at


def fast_gather_kernel(cols, columns, x_ref, recv_out, early_out, lead_out, inverse_out, late_ref, local, recv, early_ref, lead_ref, inverse_ref, own_high, own_low, main, cross, work, aug, acc_in, acc_a, acc_b, *rest):
    slots, sems, hello = rest[:-2], rest[-2], rest[-1]
    mode, col = lax.axis_index("mode"), lax.axis_index("col")
    other_mode = 1 - mode
    rows, _, length = x_ref.shape
    width = length // 2
    chips = cols // 2
    per, strip, first, inner, extents, starts, _ = fast_layout(rows, cols)
    core, chip = lax.rem(col, 2), lax.div(col, 2)
    names = {}
    pending = {}

    def sem(*name):
        return sems.at[names.setdefault(name, len(names))]

    def drain(*kinds):
        for name in [name for name in pending if name[0] in kinds]:
            pending.pop(name).wait_send()

    def push(source, target, device, *name):
        if name in pending:
            pending.pop(name).wait_send()
        copy = pltpu.make_async_remote_copy(
            src_ref=source, dst_ref=target, send_sem=sem("send", *name), recv_sem=sem("recv", *name),
            device_id=device, device_id_type=MESH,
        )
        copy.start()
        pending[name] = copy
        return copy

    sibling = (mode, chip * 2 + 1 - core)
    partner = (other_mode, col)
    plane = []
    for d in range(1, chips):
        place = lax.rem(chip + d, chips)
        plane.append((place, (mode, place * 2 + core)))

    line = chips // 2
    place = lax.div(chip, 2)
    beside = (mode, (place * 2 + 1 - lax.rem(chip, 2)) * 2 + core)
    above, under = (mode, col + 4), (mode, col - 4)
    has_above, has_under = place < line - 1, place > 0

    def hail(semaphore, device):
        pl.semaphore_signal(semaphore, inc=1, device_id=device, device_id_type=MESH)

    barrier = pltpu.get_barrier_semaphore()
    for device in (partner, sibling, beside):
        hail(barrier, device)
    pl.when(has_above)(lambda: hail(barrier, above))
    pl.when(has_under)(lambda: hail(barrier, under))
    pl.semaphore_wait(barrier, 3 + has_above.astype(jnp.int32) + has_under.astype(jnp.int32))

    def meet_line():
        pl.when(has_under)(lambda: pl.semaphore_wait(hello.at[0], 1))
        pl.when(has_above)(lambda: hail(hello.at[0], above))
        pl.when(has_above)(lambda: pl.semaphore_wait(hello.at[1], 1))
        pl.when(has_under)(lambda: hail(hello.at[1], under))
        hail(hello.at[2], beside)

    def meet_beside():
        pl.semaphore_wait(hello.at[2], 1)

    pieces = []
    away = pl.ds(pl.multiple_of(other_mode * width, width), width)

    cuts = fast_cuts(strip)

    def send_piece(k):
        span = slice(cuts[k], cuts[k + 1])
        pieces.append(push(x_ref.at[span, 0, away], recv.at[span, :], partner, "piece", k))
        del pending["piece", k]

    for k in range(EARLY):
        send_piece(k)

    loads = []
    part = length // 4
    for c in range(4):
        span = slice(c * part, (c + 1) * part)
        copy = pltpu.make_async_copy(x_ref.at[:, 0, span], local.at[:, span], sem("local", c))
        copy.start()
        loads.append(copy)
    for c in range(4):
        if c == 1:
            meet_line()
        loads[c].wait()
        high, low = halves(local[:, c * part : (c + 1) * part])
        if c == 0:
            main[...] = contract(high, high, NT)
            cross[...] = contract(high, low, NT)
        else:
            main[...] += contract(high, high, NT)
            cross[...] += contract(high, low, NT)

    for at, (i, k) in enumerate(inner):
        tall, wide = slice(i * BLOCK, (i + 1) * BLOCK), slice(k * BLOCK, (k + 1) * BLOCK)
        acc_in[at * BLOCK : (at + 1) * BLOCK, :] = main[tall, wide] + (cross[tall, wide] + cross[wide, tall].T)

    def fill(acc, used):
        if used < acc.shape[0]:
            acc[used:, :] = jnp.zeros((acc.shape[0] - used, BLOCK), jnp.float32)

    def rows_at(base, count):
        return pl.ds(pl.multiple_of(base, 8), count)

    def core_send(acc, slot):
        half = acc.shape[0] // 2
        return push(acc.at[rows_at((1 - core) * half, half), :], slot.at[...], sibling, "core")

    def core_add(acc, slot, copy):
        half = acc.shape[0] // 2
        copy.wait_recv()
        mine = rows_at(core * half, half)
        acc[mine, :] = acc[mine, :] + slot[...]

    def plane_send(acc, slot):
        half = acc.shape[0] // 2
        share = half // chips
        copies = []
        for d, (place, device) in enumerate(plane):
            copies.append(push(acc.at[rows_at(core * half + place * share, share), :], slot.at[d], device, "plane", d))
        return copies

    def plane_add(acc, slot, copies, total, start):
        half = acc.shape[0] // 2
        share = half // chips
        base = core * half + chip * share
        for copy in copies:
            copy.wait_recv()
        added = acc[rows_at(base, share), :]
        for d in range(chips - 1):
            added = added + slot[d]
        total[rows_at(start + mode * acc.shape[0] + base, share), :] = added

    def swap(acc, total, start, phase):
        half = acc.shape[0] // 2
        share = half // chips
        mine = rows_at(start + mode * acc.shape[0] + core * half + chip * share, share)
        return push(total.at[mine, :], total.at[mine, :], partner, "swap", phase)

    def plane_share(acc, total, start, modes):
        half = acc.shape[0] // 2
        share = half // chips
        copies = []
        for d, (_, device) in enumerate(plane):
            for at, m in modes:
                mine = rows_at(start + m * acc.shape[0] + core * half + chip * share, share)
                copies.append(push(total.at[mine, :], total.at[mine, :], device, "share", d, at))
        return copies

    def core_share(acc, total, start):
        half = acc.shape[0] // 2
        copies = []
        for m in range(2):
            mine = rows_at(start + m * acc.shape[0] + core * half, half)
            copies.append(push(total.at[mine, :], total.at[mine, :], sibling, "both", m))
        return copies

    def arrive(copies):
        for copy in copies:
            copy.wait_recv()

    outgoing = {}
    leaving = [0]
    both = [(0, 0), (1, 1)]

    def leave(source, target):
        lane = leaving[0] % len(loads)
        leaving[0] += 1
        if lane in outgoing:
            outgoing.pop(lane).wait()
        copy = pltpu.make_async_copy(source, target, sem("local", lane))
        copy.start()
        outgoing[lane] = copy

    def strips(begin, end, acc, offset, tall):
        span = slice(begin * strip, end * strip)
        arrive(pieces[cuts.index(begin * strip) : cuts.index(end * strip)])
        leave(recv.at[span, :], recv_out.at[span, :])
        high, low = halves(recv[span, :])
        both = contract(own_high[...], jnp.concatenate([high, low], axis=0), NT)
        count = high.shape[0]
        value = both[:, 0:count] + (both[:, count:] + contract(own_low[...], high, NT))
        value = value.T
        for c in range(per):
            at = c * tall + begin * strip - offset
            acc[at : at + (end - begin) * strip, :] = value[:, c * BLOCK : (c + 1) * BLOCK]

    fill(acc_in, len(inner) * BLOCK)
    meet_beside()
    copy = core_send(acc_in, slots[0])
    mine = local[:, pl.ds(pl.multiple_of(mode * width, width), width)]
    high, low = halves(mine)
    own_high[...] = high
    own_low[...] = low
    core_add(acc_in, slots[0], copy)
    copies = plane_send(acc_in, slots[1])
    plane_add(acc_in, slots[1], copies, early_ref, starts[0])
    copy = swap(acc_in, early_ref, starts[0], 0)
    for k in range(EARLY, PIECES - HELD):
        send_piece(k)
    strips(0, 1, acc_a, 0, first)
    arrive([copy])
    copies = plane_share(acc_in, early_ref, starts[0], both)
    drain("core", "plane", "swap")
    strips(1, 2, acc_a, 0, first)
    arrive(copies)
    arrive(core_share(acc_in, early_ref, starts[0]))

    scale = 1.0 / columns
    for at, (i, k) in enumerate(inner):
        tall, wide = slice(i * BLOCK, (i + 1) * BLOCK), slice(k * BLOCK, (k + 1) * BLOCK)
        work[tall, wide] = early_ref[starts[0] + at * BLOCK : starts[0] + (at + 1) * BLOCK, :] * scale
    lead_ref[...] = jnp.zeros_like(lead_ref)
    inverse_ref[...] = jnp.zeros_like(inverse_ref)
    row = lax.broadcasted_iota(jnp.int32, (BLOCK, BLOCK), 0)
    column = lax.broadcasted_iota(jnp.int32, (BLOCK, BLOCK), 1)
    for step in range(per):
        at, below = step * BLOCK, (step + 1) * BLOCK
        load_augmented(aug, work[at:below, at:below])
        eliminate([aug])
        lead_ref[at:below, at:below] = jnp.where(row <= column, aug[0], 0.0).T
        inverse = aug[1]
        inverse_ref[at:below, at:below] = inverse
        if step > 0:
            inverse_ref[at:below, 0:at] = -exact(inverse, exact(lead_ref[at:below, 0:at], inverse_ref[0:at, 0:at], NN), NN)
        if below < rows:
            left = exact(work[below:rows, at:below], inverse, NT)
            lead_ref[below:rows, at:below] = left
            work[below:rows, below:rows] = work[below:rows, below:rows] - exact(left, left, NT)
        if step == 0:
            strips(2, STRIPS - LATE, acc_a, 0, first)
            fill(acc_a, first * per)
            core_add(acc_a, slots[2], core_send(acc_a, slots[2]))
            copies = plane_send(acc_a, slots[3])
    plane_add(acc_a, slots[3], copies, early_ref, starts[1])
    copy = swap(acc_a, early_ref, starts[1], 1)
    for k in range(PIECES - HELD, PIECES):
        send_piece(k)
    leave(lead_ref, lead_out)
    leave(inverse_ref, inverse_out)
    strips(STRIPS - LATE, STRIPS - 2, acc_b, first, rows - first)
    arrive([copy])
    copies = plane_share(acc_a, early_ref, starts[1], both)
    drain("core", "plane", "swap", "both")
    for copy in pieces[:-HELD]:
        copy.wait_send()
    strips(STRIPS - 2, STRIPS - 1, acc_b, first, rows - first)
    arrive(copies)
    copies = core_share(acc_a, early_ref, starts[1])
    drain("share")
    arrive(copies)
    leave(early_ref, early_out)
    strips(STRIPS - 1, STRIPS, acc_b, first, rows - first)
    fill(acc_b, (rows - first) * per)
    core_add(acc_b, slots[4], core_send(acc_b, slots[4]))
    plane_add(acc_b, slots[5], plane_send(acc_b, slots[5]), late_ref, 0)
    copy = swap(acc_b, late_ref, 0, 2)
    copies = plane_share(acc_b, late_ref, 0, [(0, mode)])
    drain("core", "plane", "both")
    arrive([copy])
    copies += plane_share(acc_b, late_ref, 0, [(1, other_mode)])
    drain("swap")
    for copy in pieces[-HELD:]:
        copy.wait_send()
    for copy in outgoing.values():
        copy.wait()
    arrive(copies)
    copies = core_share(acc_b, late_ref, 0)
    drain("share")
    arrive(copies)
    drain("both")


def fast_gather(tensor, columns):
    cols = lax.axis_size("col")
    rows, _, length = tensor.shape
    width = length // 2
    chips = cols // 2
    _, _, _, _, extents, starts, _ = fast_layout(rows, cols)
    slots = []
    for extent in extents:
        slots.append(pltpu.VMEM((extent // 2, BLOCK), jnp.float32))
        slots.append(pltpu.VMEM((chips - 1, extent // cols, BLOCK), jnp.float32))
    vmem = pl.BlockSpec(memory_space=pltpu.VMEM)
    anywhere = pl.BlockSpec(memory_space=pl.ANY)
    return pl.pallas_call(
        functools.partial(fast_gather_kernel, cols, columns),
        out_shape=(
            jax.ShapeDtypeStruct((rows, width), jnp.float32),
            jax.ShapeDtypeStruct((starts[2], BLOCK), jnp.float32),
            jax.ShapeDtypeStruct((rows, rows), jnp.float32),
            jax.ShapeDtypeStruct((rows, rows), jnp.float32),
            jax.ShapeDtypeStruct((2 * extents[2], BLOCK), jnp.float32),
        ),
        in_specs=[anywhere],
        out_specs=(anywhere, anywhere, anywhere, anywhere, vmem),
        scratch_shapes=[
            pltpu.VMEM((rows, length), jnp.float32),
            pltpu.VMEM((rows, width), jnp.float32),
            pltpu.VMEM((starts[2], BLOCK), jnp.float32),
            pltpu.VMEM((rows, rows), jnp.float32),
            pltpu.VMEM((rows, rows), jnp.float32),
            pltpu.VMEM((rows, width), jnp.bfloat16),
            pltpu.VMEM((rows, width), jnp.bfloat16),
            pltpu.VMEM((rows, rows), jnp.float32),
            pltpu.VMEM((rows, rows), jnp.float32),
            pltpu.VMEM((rows, rows), jnp.float32),
            pltpu.VMEM((2, BLOCK, BLOCK), jnp.float32),
            *[pltpu.VMEM((extent, BLOCK), jnp.float32) for extent in extents],
            *slots,
            pltpu.SemaphoreType.DMA((2 * PIECES + 16 + 6 * (chips - 1),)),
            pltpu.SemaphoreType.REGULAR((3,)),
        ],
        compiler_params=pltpu.CompilerParams(collective_id=0, has_side_effects=True),
        name="fast_gather",
    )(tensor)


def fast_linear_kernel(cols, columns, early_ref, late_ref, lead_ref, inverse_ref, start_ref, x_ref, recv_ref, factor_ref, basis_ref, core_ref, gram, work, image, aug_f, aug_last, aug_b, flat, core, flat_sem, core_sem):
    mode = lax.axis_index("mode")
    size, rank = start_ref.shape
    rows = size // 2
    width = recv_ref.shape[1]
    per, _, first, inner, extents, starts, _ = fast_layout(rows, cols)
    own = pl.ds(pl.multiple_of(mode * rows, rows), rows)
    away = pl.ds(pl.multiple_of((1 - mode) * rows, rows), rows)
    half = pl.ds(pl.multiple_of(mode * width, width), width)
    loads = [
        pltpu.make_async_copy(x_ref.at[:, 0, half], flat.at[own, :], flat_sem.at[0]),
        pltpu.make_async_copy(recv_ref, flat.at[away, :], flat_sem.at[1]),
        pltpu.make_async_copy(lead_ref, factor_ref.at[0:rows, 0:rows], flat_sem.at[2]),
    ]
    for load in loads:
        load.start()

    scale = 1.0 / columns
    for m in range(2):
        for at, (i, k) in enumerate(inner):
            begin = starts[0] + m * extents[0] + at * BLOCK
            block = early_ref[begin : begin + BLOCK, :] * scale
            tall = slice(m * rows + i * BLOCK, m * rows + (i + 1) * BLOCK)
            wide = slice(m * rows + k * BLOCK, m * rows + (k + 1) * BLOCK)
            gram[tall, wide] = block
            if i != k:
                gram[wide, tall] = block.T
    pair = []
    for m in range(2):
        blocks = []
        for c in range(per):
            a = starts[1] + m * extents[1] + c * first
            b = m * extents[2] + c * (rows - first)
            blocks.append(jnp.concatenate([early_ref[a : a + first, :], late_ref[b : b + rows - first, :]], axis=0))
        pair.append(jnp.concatenate(blocks, axis=1))
    lower = (pair[0] + pair[1].T) * scale
    gram[rows:size, 0:rows] = lower
    gram[0:rows, rows:size] = lower.T

    row = lax.broadcasted_iota(jnp.int32, (BLOCK, BLOCK), 0)
    column = lax.broadcasted_iota(jnp.int32, (BLOCK, BLOCK), 1)
    factor_ref[0:rows, rows:size] = jnp.zeros((rows, rows), jnp.float32)
    left = exact(lower, inverse_ref[...], NT)
    factor_ref[rows:size, 0:rows] = left
    work[...] = gram[rows:size, rows:size] - exact(left, left, NT)

    for step in range(max(per, POWER)):
        augs = []
        at, below = step * BLOCK, (step + 1) * BLOCK
        if step < POWER:
            source = start_ref if step == 0 else basis_ref
            image[...] = exact(gram[...], source[...], NN)
            load_augmented(aug_b, exact(image[...], image[...], TN))
            augs.append(aug_b)
        if step < per:
            block = aug_f if below < rows else aug_last
            load_augmented(block, work[at:below, at:below])
            augs.append(block)
        eliminate(augs)
        if step < POWER:
            basis_ref[...] = exact(image[...], aug_b[1], NT)
        if step < per:
            upper = jnp.where(row <= column, block[0], 0.0)
            factor_ref[rows + at : rows + below, rows + at : rows + below] = upper.T
            if step > 0:
                factor_ref[rows : rows + at, rows + at : rows + below] = jnp.zeros((at, BLOCK), jnp.float32)
            if below < rows:
                left = exact(work[below:rows, at:below], aug_f[1], NT)
                factor_ref[rows + below : size, rows + at : rows + below] = left
                work[below:rows, below:rows] = work[below:rows, below:rows] - exact(left, left, NT)

    for load in loads:
        load.wait()
    high, low = halves(basis_ref[...])
    piece = min(CHUNK, width)
    copies = []
    for start in range(0, width, piece):
        part = slice(start, start + piece)
        flat_high, flat_low = halves(flat[:, part])
        core[:, part] = contract(high, flat_high, TN) + contract(high, flat_low, TN) + contract(low, flat_high, TN)
        copy = pltpu.make_async_copy(core.at[:, part], core_ref.at[:, 0, part], core_sem.at[len(copies)])
        copy.start()
        copies.append(copy)
    for copy in copies:
        copy.wait()


def fast_linear(columns, early, late, lead, inverse, start_basis, tensor, recv):
    size, rank = start_basis.shape
    rows, width = recv.shape
    vmem = pl.BlockSpec(memory_space=pltpu.VMEM)
    anywhere = pl.BlockSpec(memory_space=pl.ANY)
    return pl.pallas_call(
        functools.partial(fast_linear_kernel, lax.axis_size("col"), columns),
        out_shape=(
            jax.ShapeDtypeStruct((size, size), jnp.float32),
            jax.ShapeDtypeStruct((size, rank), jnp.float32),
            jax.ShapeDtypeStruct((rank, 1, width), jnp.float32),
        ),
        in_specs=[vmem, vmem, anywhere, vmem, vmem, anywhere, anywhere],
        out_specs=(vmem, vmem, anywhere),
        scratch_shapes=[
            pltpu.VMEM((size, size), jnp.float32),
            pltpu.VMEM((rows, rows), jnp.float32),
            pltpu.VMEM((size, rank), jnp.float32),
            pltpu.VMEM((2, BLOCK, BLOCK), jnp.float32),
            pltpu.VMEM((1, BLOCK, BLOCK), jnp.float32),
            pltpu.VMEM((2, rank, rank), jnp.float32),
            pltpu.VMEM((size, width), jnp.float32),
            pltpu.VMEM((rank, width), jnp.float32),
            pltpu.SemaphoreType.DMA((3,)),
            pltpu.SemaphoreType.DMA((width // min(CHUNK, width),)),
        ],
        name="fast_linear",
    )(early, late, lead, inverse, start_basis, tensor, recv)


def per_device(tensor, start_basis):
    modes, cols = lax.axis_size("mode"), lax.axis_size("col")
    depth = tensor.shape[1]
    columns = depth * tensor.shape[2] * cols
    if fast_case(modes, cols, tensor.shape):
        recv, early, lead, inverse, late = fast_gather(tensor, columns)
        return fast_linear(columns, early, late, lead, inverse, start_basis, tensor, recv)
    flat, packed = gather(tensor)
    return linear(columns, depth, packed, start_basis, flat)


def solution(mesh):
    in_specs = (P("mode", "col", None), P())
    out_specs = (P(), P(), P(None, "col", "mode"))
    return jax.shard_map(
        per_device, mesh=mesh, in_specs=in_specs, out_specs=out_specs, check_vma=False
    )
```

```python
import functools

import jax
import jax.numpy as jnp
from jax import lax
from jax.experimental import pallas as pl
from jax.experimental.pallas import tpu as pltpu
from jax.sharding import PartitionSpec as P

POWER = 2
BLOCK = 128
PANEL = 8
CHUNK = 512
MESH = pl.DeviceIdType.MESH


def halves(value):
    high = value.astype(jnp.bfloat16)
    low = (value - high.astype(jnp.float32)).astype(jnp.bfloat16)
    return high, low


def contract(left, right, dims):
    return lax.dot_general(left, right, (dims, ((), ())), preferred_element_type=jnp.float32)


def exact(left, right, dims):
    return lax.dot_general(
        left, right, (dims, ((), ())), precision=lax.Precision.HIGHEST,
        preferred_element_type=jnp.float32,
    )


NN = ((1,), (0,))
NT = ((1,), (1,))
TN = ((0,), (0,))


def thirds(value):
    high = value.astype(jnp.bfloat16)
    rest = value - high.astype(jnp.float32)
    middle = rest.astype(jnp.bfloat16)
    low = (rest - middle.astype(jnp.float32)).astype(jnp.bfloat16)
    return high, middle, low


def six_terms(left, right, dims):
    high, middle, low = right
    beside, along = (1, 0) if dims == NN else (0, 1)
    wide = jnp.concatenate([high, middle], axis=beside)
    first = contract(
        jnp.concatenate([left[0], left[1]], axis=1), jnp.concatenate([wide, wide], axis=along), dims
    )
    second = contract(
        jnp.concatenate([left[2], left[0]], axis=1), jnp.concatenate([high, low], axis=along), dims
    )
    count = second.shape[1]
    return first[:, 0:count] + (first[:, count:] + second)


def self_product(parts):
    high, middle, low = parts
    pair = jnp.concatenate([high, middle], axis=1)
    product = contract(pair, pair, TN)
    small = contract(high, low, TN)
    count = small.shape[0]
    rest = (product[0:count, count:] + product[count:, 0:count]) + (product[count:, count:] + (small + small.T))
    return product[0:count, 0:count] + rest


def split3(value):
    high = value.astype(jnp.bfloat16).astype(jnp.float32)
    rest = value - high
    middle = rest.astype(jnp.bfloat16).astype(jnp.float32)
    return high, middle, rest - middle


def spread(tile, lane):
    return jnp.broadcast_to(tile[:, lane : lane + 1], tile.shape)


def eliminate_panel(aug, j):
    parts, size, _ = aug.shape
    first = PANEL * j
    after = first + PANEL
    below = after + PANEL
    rows = [[aug[p, pl.ds(first + t, PANEL, stride=0), :] for p in range(parts)] for t in range(PANEL)]
    entry = {}
    for s in range(PANEL):
        for t in range(s + 1):
            entry[s, t] = spread(rows[t][0], first + s)
    if after < size:
        following = [aug[p, after:below, :] for p in range(parts)]
        column = [spread(following[0], first + t) for t in range(PANEL)]
    for t in range(PANEL):
        inverse = 1.0 / entry[t, t]
        for s in range(t + 1, PANEL):
            ratio = entry[s, t] * inverse
            for u in range(s, PANEL):
                entry[u, s] = entry[u, s] - ratio * entry[u, t]
            rows[s] = [a - ratio * b for a, b in zip(rows[s], rows[t])]
        scale = lax.rsqrt(entry[t, t])
        for p in range(parts):
            aug[p, first + t : first + t + 1, :] = (rows[t][p] * scale)[0:1]
        if after < size:
            ratio = column[t] * inverse
            for u in range(t + 1, PANEL):
                column[u] = column[u] - ratio * entry[u, t]
            following = [a - ratio * b for a, b in zip(following, rows[t])]
    if after < size:
        for p in range(parts):
            aug[p, after:below, :] = following[p]
    if below < size:
        rights = []
        for p in range(parts):
            high, middle, low = split3(aug[p, first:after, :])
            if p == 0:
                left = jnp.concatenate([high, high, middle, high, low, middle], axis=0).astype(jnp.bfloat16)
            rights.append(jnp.concatenate([high, middle, high, low, high, middle], axis=0).astype(jnp.bfloat16))
        update = contract(left, jnp.concatenate(rights, axis=1), TN)
        for p in range(parts):
            aug[p, below:size, :] = aug[p, below:size, :] - update[below:size, p * size : (p + 1) * size]


def eliminate(augs):
    for j in range(BLOCK // PANEL):
        for aug in augs:
            eliminate_panel(aug, j)


def load_augmented(aug, matrix):
    size = matrix.shape[0]
    aug[0] = matrix
    if aug.shape[0] > 1:
        row = lax.broadcasted_iota(jnp.int32, (size, size), 0)
        column = lax.broadcasted_iota(jnp.int32, (size, size), 1)
        aug[1] = jnp.where(row == column, 1.0, 0.0).astype(jnp.float32)


def lower_blocks(blocks):
    return [(i, k) for i in range(blocks) for k in range(i + 1)]


def stages_of(modes, cols):
    stages, stride = [], 1
    first = 2 if cols % 2 == 0 else 1
    if first > 1:
        stages.append((1, first, False))
        stride = first
    second = 2 if (cols // stride) % 2 == 0 else 1
    stages.append((stride, second, True))
    stride *= second
    if cols // stride > 1:
        stages.append((stride, cols // stride, False))
    return stages


def round_up(value, unit):
    return -(-value // unit) * unit


def layout_of(size, modes, cols):
    pairs = lower_blocks(size // BLOCK)
    rows = size // modes
    inner = []
    if rows % BLOCK == 0 and modes > 1:
        inner = lower_blocks(rows // BLOCK)
    per = rows // BLOCK
    extent = round_up(len(inner) * BLOCK, 8 * cols)
    where = {}
    for m in range(modes):
        for n, (i, k) in enumerate(inner):
            where[m * per + i, m * per + k] = m * extent + n * BLOCK
    outer = [pair for pair in pairs if pair not in where]
    for n, pair in enumerate(outer):
        where[pair] = modes * extent + n * BLOCK
    return where, inner, extent, outer, round_up(len(outer) * BLOCK, 8 * modes * cols)


def members_of(stages, modes):
    return [count * (modes if with_mode else 1) for _, count, with_mode in stages]


def gather_kernel(modes, cols, x_ref, flat_ref, total_ref, local, acc_in, acc_out, main, cross, *rest):
    mode, col = lax.axis_index("mode"), lax.axis_index("col")
    all_stages = stages_of(modes, cols)
    col_stages = [(stride, count, False) for stride, count, _ in all_stages]
    n = len(all_stages)
    slots_in, slots_out = rest[:n], rest[n : 2 * n]
    local_sem, piece_send, piece_recv, swap_send, swap_recv, in_sems, out_sems, share_in, share_out = rest[2 * n :]
    rows, depth, length = x_ref.shape
    size = rows * modes
    width = length // modes
    chunk = min(CHUNK, width)
    per = width // chunk
    chunks = depth * per
    where, inner, in_extent, outer, out_extent = layout_of(size, modes, cols)

    def position(stage):
        stride, count, with_mode = stage
        place = lax.rem(lax.div(col, stride), count)
        return place * modes + mode if with_mode else place

    def members(stage):
        return stage[1] * (modes if stage[2] else 1)

    def peer(stage, offset):
        stride, count, with_mode = stage
        other = lax.rem(position(stage) + offset, members(stage))
        place = lax.div(other, modes) if with_mode else other
        there = col + (place - lax.rem(lax.div(col, stride), count)) * stride
        return other, (lax.rem(other, modes) if with_mode else mode, there)

    partners = [(lax.rem(mode + d, modes), col) for d in range(1, modes)]
    greeted = []
    for stage in all_stages:
        greeted += [peer(stage, d)[1] for d in range(1, members(stage))]
    barrier = pltpu.get_barrier_semaphore()
    for device in greeted:
        pl.semaphore_signal(barrier, inc=1, device_id=device, device_id_type=MESH)
    pl.semaphore_wait(barrier, len(greeted))

    own_rows = pl.ds(pl.multiple_of(mode * rows, rows), rows)

    def spans(c):
        layer, part = lax.div(c, per), lax.rem(c, per)
        return layer, part * chunk, pl.multiple_of(layer * width + part * chunk, chunk)

    def piece(c, d):
        layer, start, target = spans(c)
        source = pl.multiple_of(lax.rem(mode + d, modes) * width + start, chunk)
        return pltpu.make_async_remote_copy(
            src_ref=x_ref.at[:, layer, pl.ds(source, chunk)],
            dst_ref=flat_ref.at[own_rows, pl.ds(target, chunk)],
            send_sem=piece_send.at[d - 1, c],
            recv_sem=piece_recv.at[d - 1, c],
            device_id=partners[d - 1],
            device_id_type=MESH,
        )

    def load(c):
        layer, part = lax.div(c, per * modes), lax.rem(c, per * modes)
        source = pl.multiple_of(part * chunk, chunk)
        target = pl.multiple_of(layer * length + part * chunk, chunk)
        return pltpu.make_async_copy(
            x_ref.at[:, layer, pl.ds(source, chunk)], local.at[:, pl.ds(target, chunk)], local_sem.at[c]
        ), target

    def begin(c, carry):
        for d in range(1, modes):
            piece(c, d).start()
        return carry

    def begin_load(c, carry):
        load(c)[0].start()
        return carry

    early = max(chunks // 2, 1)
    lax.fori_loop(0, early, begin, 0)
    lax.fori_loop(0, chunks * modes, begin_load, 0)

    main[...] = jnp.zeros_like(main)
    cross[...] = jnp.zeros_like(cross)

    def accumulate_in(c, carry):
        copy, target = load(c)
        copy.wait()
        if inner:
            high, low = halves(local[:, pl.ds(target, chunk)])
            main[0:rows, 0:rows] += contract(high, high, NT)
            cross[0:rows, 0:rows] += contract(high, low, NT)
        return carry

    lax.fori_loop(0, chunks * modes, accumulate_in, 0)
    for layer in range(depth):
        source = pl.multiple_of(layer * length + mode * width, chunk)
        flat_ref[own_rows, layer * width : (layer + 1) * width] = local[:, pl.ds(source, width)]

    def pack(acc, pairs, extent):
        for at, (i, k) in enumerate(pairs):
            tall, wide = slice(i * BLOCK, (i + 1) * BLOCK), slice(k * BLOCK, (k + 1) * BLOCK)
            acc[at * BLOCK : (at + 1) * BLOCK, :] = main[tall, wide] + (cross[tall, wide] + cross[wide, tall].T)
        used = len(pairs) * BLOCK
        if used < extent:
            acc[used:, :] = jnp.zeros((extent - used, BLOCK), jnp.float32)

    def scatter_sum(stages, acc, extent, slots, sems, target):
        base, bases = 0, []
        for g, stage in enumerate(stages):
            count = members(stage)
            part = extent // count
            copies = []
            for d in range(1, count):
                other, device = peer(stage, d)
                copy = pltpu.make_async_remote_copy(
                    src_ref=acc.at[pl.ds(pl.multiple_of(base + other * part, 8), part), :],
                    dst_ref=slots[g].at[d - 1],
                    send_sem=sems.at[0, g, d - 1],
                    recv_sem=sems.at[1, g, d - 1],
                    device_id=device,
                    device_id_type=MESH,
                )
                copy.start()
                copies.append(copy)
            base = base + position(stage) * part
            extent = part
            bases.append((base, part))
            for copy in copies:
                copy.wait()
            mine = pl.ds(pl.multiple_of(base, 8), part)
            added = acc[mine, :]
            for d in range(1, count):
                added = added + slots[g][d - 1]
            if g < len(stages) - 1:
                acc[mine, :] = added
            else:
                total_ref[pl.ds(pl.multiple_of(target + base, 8), part), :] = added
        return bases

    def share(stages, bases, targets, sems):
        for g in reversed(range(len(stages))):
            stage = stages[g]
            base, part = bases[g]
            copies = []
            for d in range(1, members(stage)):
                for t, target in enumerate(targets):
                    mine = pl.ds(pl.multiple_of(target + base, 8), part)
                    copy = pltpu.make_async_remote_copy(
                        src_ref=total_ref.at[mine, :],
                        dst_ref=total_ref.at[mine, :],
                        send_sem=sems.at[0, g, (d - 1) * len(targets) + t],
                        recv_sem=sems.at[1, g, (d - 1) * len(targets) + t],
                        device_id=peer(stage, d)[1],
                        device_id_type=MESH,
                    )
                    copy.start()
                    copies.append(copy)
            for copy in copies:
                copy.wait()

    def accumulate_out(c, carry):
        for d in range(1, modes):
            piece(c, d).wait_recv()
        high, low = halves(flat_ref[:, pl.ds(spans(c)[2], chunk)])
        if inner:
            for m in range(1, modes):
                tall, wide = slice(m * rows, (m + 1) * rows), slice(0, m * rows)
                main[tall, wide] += contract(high[tall, :], high[wide, :], NT) + contract(low[tall, :], high[wide, :], NT)
                cross[tall, wide] += contract(high[tall, :], low[wide, :], NT)
        else:
            main[...] += contract(high, high, NT)
            cross[...] += contract(high, low, NT)
        return carry

    swaps = []
    if inner:
        pack(acc_in, inner, in_extent)
        main[...] = jnp.zeros_like(main)
        cross[...] = jnp.zeros_like(cross)
        bases = scatter_sum(col_stages, acc_in, in_extent, slots_in, in_sems, mode * in_extent)
        base, part = bases[-1]
        mine = pl.ds(pl.multiple_of(mode * in_extent + base, 8), part)
        for d in range(1, modes):
            swap = pltpu.make_async_remote_copy(
                src_ref=total_ref.at[mine, :],
                dst_ref=total_ref.at[mine, :],
                send_sem=swap_send.at[d - 1],
                recv_sem=swap_recv.at[d - 1],
                device_id=partners[d - 1],
                device_id_type=MESH,
            )
            swap.start()
            swaps.append(swap)
    lax.fori_loop(early, chunks, begin, 0)
    lax.fori_loop(0, early, accumulate_out, 0)
    if inner:
        for swap in swaps:
            swap.wait()
        share(col_stages, bases, [m * in_extent for m in range(modes)], share_in)
    lax.fori_loop(early, chunks, accumulate_out, 0)

    pack(acc_out, outer, out_extent)
    bases = scatter_sum(all_stages, acc_out, out_extent, slots_out, out_sems, modes * in_extent)
    share(all_stages, bases, [modes * in_extent], share_out)

    def end(c, carry):
        for d in range(1, modes):
            piece(c, d).wait_send()
        return carry

    lax.fori_loop(0, chunks, end, 0)


def gather(tensor):
    modes, cols = lax.axis_size("mode"), lax.axis_size("col")
    rows, depth, length = tensor.shape
    size = rows * modes
    width = length // modes
    chunks = depth * (width // min(CHUNK, width))
    stages = stages_of(modes, cols)
    _, inner, in_extent, _, out_extent = layout_of(size, modes, cols)
    in_extent = max(in_extent, 8 * cols)
    slots_in, slots_out, extent_in, extent, most = [], [], in_extent, out_extent, 1
    for stride, count, with_mode in stages:
        extent_in = extent_in // count
        slots_in.append(pltpu.VMEM((max(count - 1, 1), extent_in, BLOCK), jnp.float32))
        count = count * (modes if with_mode else 1)
        extent = extent // count
        slots_out.append(pltpu.VMEM((max(count - 1, 1), extent, BLOCK), jnp.float32))
        most = max(most, count - 1)
    dma = pltpu.SemaphoreType.DMA
    vmem = pl.BlockSpec(memory_space=pltpu.VMEM)
    packed = (modes * in_extent if inner else 0) + out_extent
    return pl.pallas_call(
        functools.partial(gather_kernel, modes, cols),
        out_shape=(
            jax.ShapeDtypeStruct((size, depth * width), jnp.float32),
            jax.ShapeDtypeStruct((packed, BLOCK), jnp.float32),
        ),
        in_specs=[pl.BlockSpec(memory_space=pl.ANY)],
        out_specs=(vmem, vmem),
        scratch_shapes=[
            pltpu.VMEM((rows, depth * length), jnp.float32),
            pltpu.VMEM((in_extent, BLOCK), jnp.float32),
            pltpu.VMEM((out_extent, BLOCK), jnp.float32),
            pltpu.VMEM((size, size), jnp.float32),
            pltpu.VMEM((size, size), jnp.float32),
            *slots_in,
            *slots_out,
            dma((chunks * modes,)),
            *[dma((max(modes - 1, 1), chunks))] * 2,
            *[dma((max(modes - 1, 1),))] * 2,
            *[dma((2, len(stages), most))] * 2,
            dma((2, len(stages), most * modes)),
            dma((2, len(stages), most)),
        ],
        compiler_params=pltpu.CompilerParams(collective_id=0, has_side_effects=True),
        name="gather",
    )(tensor)


def linear_kernel(columns, where, packed_ref, start_ref, flat_ref, factor_ref, basis_ref, core_ref, gram, work, image, aug_f, aug_b, core, core_sem):
    size, rank = start_ref.shape
    blocks = size // BLOCK
    row = lax.broadcasted_iota(jnp.int32, (BLOCK, BLOCK), 0)
    column = lax.broadcasted_iota(jnp.int32, (BLOCK, BLOCK), 1)
    scale = 1.0 / columns
    for (i, k), at in where.items():
        scaled = packed_ref[at : at + BLOCK, :] * scale
        gram[i * BLOCK : (i + 1) * BLOCK, k * BLOCK : (k + 1) * BLOCK] = scaled
        work[i * BLOCK : (i + 1) * BLOCK, k * BLOCK : (k + 1) * BLOCK] = scaled
        if i != k:
            gram[k * BLOCK : (k + 1) * BLOCK, i * BLOCK : (i + 1) * BLOCK] = scaled.T

    for step in range(max(blocks, POWER)):
        augs = []
        if step < blocks:
            at = step * BLOCK
            load_augmented(aug_f, work[at : at + BLOCK, at : at + BLOCK])
            augs.append(aug_f)
        if step < POWER:
            source = start_ref if step == 0 else basis_ref
            image[...] = exact(gram[...], source[...], NN)
            load_augmented(aug_b, exact(image[...], image[...], TN))
            augs.append(aug_b)
        eliminate(augs)
        if step < POWER:
            basis_ref[...] = exact(image[...], aug_b[1], NT)
        if step < blocks:
            upper = jnp.where(row <= column, aug_f[0], 0.0)
            factor_ref[at : at + BLOCK, at : at + BLOCK] = upper.T
            if step > 0:
                factor_ref[0:at, at : at + BLOCK] = jnp.zeros((at, BLOCK), jnp.float32)
            below = at + BLOCK
            if below < size:
                inverse = aug_f[1]
                left = exact(work[below:size, at : at + BLOCK], inverse, NT)
                factor_ref[below:size, at : at + BLOCK] = left
                work[below:size, below:size] = work[below:size, below:size] - exact(left, left, NT)

    high, low = halves(basis_ref[...])
    depth, length = core_ref.shape[1:]
    width = min(CHUNK, length)
    copies = []
    for start in range(0, depth * length, width):
        part = slice(start, start + width)
        flat_high, flat_low = halves(flat_ref[:, part])
        core[:, part] = contract(high, flat_high, TN) + contract(high, flat_low, TN) + contract(low, flat_high, TN)
        layer, offset = divmod(start, length)
        copy = pltpu.make_async_copy(
            core.at[:, part], core_ref.at[:, layer, offset : offset + width], core_sem.at[len(copies)]
        )
        copy.start()
        copies.append(copy)
    for copy in copies:
        copy.wait()


def linear(columns, depth, packed, start_basis, flat):
    size, rank = start_basis.shape
    length = flat.shape[1] // depth
    where = layout_of(size, lax.axis_size("mode"), lax.axis_size("col"))[0]
    vmem = pl.BlockSpec(memory_space=pltpu.VMEM)
    return pl.pallas_call(
        functools.partial(linear_kernel, columns, where),
        out_shape=(
            jax.ShapeDtypeStruct((size, size), jnp.float32),
            jax.ShapeDtypeStruct((size, rank), jnp.float32),
            jax.ShapeDtypeStruct((rank, depth, length), jnp.float32),
        ),
        in_specs=[vmem] * 3,
        out_specs=(vmem, vmem, pl.BlockSpec(memory_space=pl.ANY)),
        scratch_shapes=[
            pltpu.VMEM((size, size), jnp.float32),
            pltpu.VMEM((size, size), jnp.float32),
            pltpu.VMEM((size, rank), jnp.float32),
            pltpu.VMEM((2, BLOCK, BLOCK), jnp.float32),
            pltpu.VMEM((2, rank, rank), jnp.float32),
            pltpu.VMEM((rank, flat.shape[1]), jnp.float32),
            pltpu.SemaphoreType.DMA((flat.shape[1] // min(CHUNK, length),)),
        ],
        name="linear",
    )(packed, start_basis, flat)


def fast_case(modes, cols, shape):
    rows, depth, length = shape
    return modes == 2 and depth == 1 and rows % (2 * BLOCK) == 0 and cols % 4 == 0 and length % (2 * BLOCK) == 0


STRIPS = 8
LATE = 4
EARLY = 3
HELD = 2
PIECES = STRIPS + 2


def fast_cuts(strip):
    return sorted([k * strip for k in range(STRIPS + 1)] + [2 * strip + strip // 2, 6 * strip + strip // 2])


def fast_layout(rows, cols):
    per = rows // BLOCK
    strip = rows // STRIPS
    first = rows - LATE * strip
    inner = lower_blocks(per)
    unit = 8 * cols
    extents = [round_up(len(inner) * BLOCK, unit), round_up(first * per, unit), round_up((rows - first) * per, unit)]
    starts, at = [], 0
    for extent in extents:
        starts.append(at)
        at += 2 * extent
    return per, strip, first, inner, extents, starts, at


def fast_gather_kernel(cols, columns, x_ref, high_out, low_out, early_out, lead_out, inverse_out, late_ref, local, recv, early_ref, lead_ref, inverse_ref, own_high, own_low, other_high, other_low, main, cross, work, aug, acc_in, acc_a, acc_b, *rest):
    slots, sems, hello = rest[:-2], rest[-2], rest[-1]
    mode, col = lax.axis_index("mode"), lax.axis_index("col")
    other_mode = 1 - mode
    rows, _, length = x_ref.shape
    width = length // 2
    chips = cols // 2
    per, strip, first, inner, extents, starts, _ = fast_layout(rows, cols)
    core, chip = lax.rem(col, 2), lax.div(col, 2)
    names = {}
    pending = {}

    def sem(*name):
        return sems.at[names.setdefault(name, len(names))]

    def drain(*kinds):
        for name in [name for name in pending if name[0] in kinds]:
            pending.pop(name).wait_send()

    def push(source, target, device, *name):
        if name in pending:
            pending.pop(name).wait_send()
        copy = pltpu.make_async_remote_copy(
            src_ref=source, dst_ref=target, send_sem=sem("send", *name), recv_sem=sem("recv", *name),
            device_id=device, device_id_type=MESH,
        )
        copy.start()
        pending[name] = copy
        return copy

    sibling = (mode, chip * 2 + 1 - core)
    partner = (other_mode, col)
    plane = []
    for d in range(1, chips):
        place = lax.rem(chip + d, chips)
        plane.append((place, (mode, place * 2 + core)))

    line = chips // 2
    place = lax.div(chip, 2)
    beside = (mode, (place * 2 + 1 - lax.rem(chip, 2)) * 2 + core)
    above, under = (mode, col + 4), (mode, col - 4)
    has_above, has_under = place < line - 1, place > 0

    def hail(semaphore, device):
        pl.semaphore_signal(semaphore, inc=1, device_id=device, device_id_type=MESH)

    barrier = pltpu.get_barrier_semaphore()
    for device in (partner, sibling, beside):
        hail(barrier, device)
    pl.when(has_above)(lambda: hail(barrier, above))
    pl.when(has_under)(lambda: hail(barrier, under))
    pl.semaphore_wait(barrier, 3 + has_above.astype(jnp.int32) + has_under.astype(jnp.int32))

    def meet_line():
        pl.when(has_under)(lambda: pl.semaphore_wait(hello.at[0], 1))
        pl.when(has_above)(lambda: hail(hello.at[0], above))
        pl.when(has_above)(lambda: pl.semaphore_wait(hello.at[1], 1))
        pl.when(has_under)(lambda: hail(hello.at[1], under))
        hail(hello.at[2], beside)

    def meet_beside():
        pl.semaphore_wait(hello.at[2], 1)

    pieces = []
    away = pl.ds(pl.multiple_of(other_mode * width, width), width)

    cuts = fast_cuts(strip)

    def send_piece(k):
        span = slice(cuts[k], cuts[k + 1])
        pieces.append(push(x_ref.at[span, 0, away], recv.at[span, :], partner, "piece", k))
        del pending["piece", k]

    for k in range(EARLY):
        send_piece(k)

    loads = []
    part = length // 4
    for c in range(4):
        span = slice(c * part, (c + 1) * part)
        copy = pltpu.make_async_copy(x_ref.at[:, 0, span], local.at[:, span], sem("local", c))
        copy.start()
        loads.append(copy)
    for c in range(4):
        if c == 1:
            meet_line()
        loads[c].wait()
        high, low = halves(local[:, c * part : (c + 1) * part])
        if c == 0:
            main[...] = contract(high, high, NT)
            cross[...] = contract(high, low, NT)
        else:
            main[...] += contract(high, high, NT)
            cross[...] += contract(high, low, NT)

    for at, (i, k) in enumerate(inner):
        tall, wide = slice(i * BLOCK, (i + 1) * BLOCK), slice(k * BLOCK, (k + 1) * BLOCK)
        acc_in[at * BLOCK : (at + 1) * BLOCK, :] = main[tall, wide] + (cross[tall, wide] + cross[wide, tall].T)

    def fill(acc, used):
        if used < acc.shape[0]:
            acc[used:, :] = jnp.zeros((acc.shape[0] - used, BLOCK), jnp.float32)

    def rows_at(base, count):
        return pl.ds(pl.multiple_of(base, 8), count)

    def core_send(acc, slot):
        half = acc.shape[0] // 2
        return push(acc.at[rows_at((1 - core) * half, half), :], slot.at[...], sibling, "core")

    def core_add(acc, slot, copy):
        half = acc.shape[0] // 2
        copy.wait_recv()
        mine = rows_at(core * half, half)
        acc[mine, :] = acc[mine, :] + slot[...]

    def plane_send(acc, slot):
        half = acc.shape[0] // 2
        share = half // chips
        copies = []
        for d, (place, device) in enumerate(plane):
            copies.append(push(acc.at[rows_at(core * half + place * share, share), :], slot.at[d], device, "plane", d))
        return copies

    def plane_add(acc, slot, copies, total, start):
        half = acc.shape[0] // 2
        share = half // chips
        base = core * half + chip * share
        for copy in copies:
            copy.wait_recv()
        added = acc[rows_at(base, share), :]
        for d in range(chips - 1):
            added = added + slot[d]
        total[rows_at(start + mode * acc.shape[0] + base, share), :] = added

    def swap(acc, total, start, phase):
        half = acc.shape[0] // 2
        share = half // chips
        mine = rows_at(start + mode * acc.shape[0] + core * half + chip * share, share)
        return push(total.at[mine, :], total.at[mine, :], partner, "swap", phase)

    def plane_share(acc, total, start, modes):
        half = acc.shape[0] // 2
        share = half // chips
        copies = []
        for d, (_, device) in enumerate(plane):
            for at, m in modes:
                mine = rows_at(start + m * acc.shape[0] + core * half + chip * share, share)
                copies.append(push(total.at[mine, :], total.at[mine, :], device, "share", d, at))
        return copies

    def core_share(acc, total, start):
        half = acc.shape[0] // 2
        copies = []
        for m in range(2):
            mine = rows_at(start + m * acc.shape[0] + core * half, half)
            copies.append(push(total.at[mine, :], total.at[mine, :], sibling, "both", m))
        return copies

    def arrive(copies):
        for copy in copies:
            copy.wait_recv()

    outgoing = {}
    leaving = [0]
    both = [(0, 0), (1, 1)]

    def leave(source, target):
        lane = leaving[0] % len(loads)
        leaving[0] += 1
        if lane in outgoing:
            outgoing.pop(lane).wait()
        copy = pltpu.make_async_copy(source, target, sem("local", lane))
        copy.start()
        outgoing[lane] = copy

    def strips(begin, end, acc, offset, tall):
        span = slice(begin * strip, end * strip)
        arrive(pieces[cuts.index(begin * strip) : cuts.index(end * strip)])
        high, low = halves(recv[span, :])
        other_high[span, :] = high
        other_low[span, :] = low
        target = pl.ds(pl.multiple_of(other_mode * rows + begin * strip, strip), (end - begin) * strip)
        leave(other_high.at[span, :], high_out.at[target, :])
        leave(other_low.at[span, :], low_out.at[target, :])
        both = contract(own_high[...], jnp.concatenate([high, low], axis=0), NT)
        count = high.shape[0]
        value = both[:, 0:count] + (both[:, count:] + contract(own_low[...], high, NT))
        value = value.T
        for c in range(per):
            at = c * tall + begin * strip - offset
            acc[at : at + (end - begin) * strip, :] = value[:, c * BLOCK : (c + 1) * BLOCK]

    fill(acc_in, len(inner) * BLOCK)
    meet_beside()
    copy = core_send(acc_in, slots[0])
    mine = local[:, pl.ds(pl.multiple_of(mode * width, width), width)]
    high, low = halves(mine)
    own_high[...] = high
    own_low[...] = low
    core_add(acc_in, slots[0], copy)
    copies = plane_send(acc_in, slots[1])
    target = pl.ds(pl.multiple_of(mode * rows, rows), rows)
    leave(own_high, high_out.at[target, :])
    leave(own_low, low_out.at[target, :])
    plane_add(acc_in, slots[1], copies, early_ref, starts[0])
    copy = swap(acc_in, early_ref, starts[0], 0)
    for k in range(EARLY, PIECES - HELD):
        send_piece(k)
    strips(0, 1, acc_a, 0, first)
    arrive([copy])
    copies = plane_share(acc_in, early_ref, starts[0], both)
    drain("core", "plane", "swap")
    strips(1, 2, acc_a, 0, first)
    arrive(copies)
    arrive(core_share(acc_in, early_ref, starts[0]))

    scale = 1.0 / columns
    for at, (i, k) in enumerate(inner):
        tall, wide = slice(i * BLOCK, (i + 1) * BLOCK), slice(k * BLOCK, (k + 1) * BLOCK)
        work[tall, wide] = early_ref[starts[0] + at * BLOCK : starts[0] + (at + 1) * BLOCK, :] * scale
    lead_ref[...] = jnp.zeros_like(lead_ref)
    inverse_ref[...] = jnp.zeros_like(inverse_ref)
    row = lax.broadcasted_iota(jnp.int32, (BLOCK, BLOCK), 0)
    column = lax.broadcasted_iota(jnp.int32, (BLOCK, BLOCK), 1)
    for step in range(per):
        at, below = step * BLOCK, (step + 1) * BLOCK
        load_augmented(aug, work[at:below, at:below])
        eliminate([aug])
        lead_ref[at:below, at:below] = jnp.where(row <= column, aug[0], 0.0).T
        inverse = aug[1]
        inverse_ref[at:below, at:below] = inverse
        if step > 0:
            inverse_ref[at:below, 0:at] = -exact(inverse, exact(lead_ref[at:below, 0:at], inverse_ref[0:at, 0:at], NN), NN)
        if below < rows:
            left = exact(work[below:rows, at:below], inverse, NT)
            lead_ref[below:rows, at:below] = left
            work[below:rows, below:rows] = work[below:rows, below:rows] - exact(left, left, NT)
        if step == 0:
            strips(2, STRIPS - LATE, acc_a, 0, first)
            fill(acc_a, first * per)
            core_add(acc_a, slots[2], core_send(acc_a, slots[2]))
            copies = plane_send(acc_a, slots[3])
    plane_add(acc_a, slots[3], copies, early_ref, starts[1])
    copy = swap(acc_a, early_ref, starts[1], 1)
    for k in range(PIECES - HELD, PIECES):
        send_piece(k)
    leave(lead_ref, lead_out)
    leave(inverse_ref, inverse_out)
    strips(STRIPS - LATE, STRIPS - 2, acc_b, first, rows - first)
    arrive([copy])
    copies = plane_share(acc_a, early_ref, starts[1], both)
    drain("core", "plane", "swap", "both")
    for copy in pieces[:-HELD]:
        copy.wait_send()
    strips(STRIPS - 2, STRIPS - 1, acc_b, first, rows - first)
    arrive(copies)
    copies = core_share(acc_a, early_ref, starts[1])
    drain("share")
    arrive(copies)
    leave(early_ref, early_out)
    strips(STRIPS - 1, STRIPS, acc_b, first, rows - first)
    fill(acc_b, (rows - first) * per)
    core_add(acc_b, slots[4], core_send(acc_b, slots[4]))
    plane_add(acc_b, slots[5], plane_send(acc_b, slots[5]), late_ref, 0)
    copy = swap(acc_b, late_ref, 0, 2)
    copies = plane_share(acc_b, late_ref, 0, [(0, mode)])
    drain("core", "plane", "both")
    arrive([copy])
    copies += plane_share(acc_b, late_ref, 0, [(1, other_mode)])
    drain("swap")
    for copy in pieces[-HELD:]:
        copy.wait_send()
    for copy in outgoing.values():
        copy.wait()
    arrive(copies)
    copies = core_share(acc_b, late_ref, 0)
    drain("share")
    arrive(copies)
    drain("both")


def fast_gather(tensor, columns):
    cols = lax.axis_size("col")
    rows, _, length = tensor.shape
    width = length // 2
    chips = cols // 2
    _, _, _, _, extents, starts, _ = fast_layout(rows, cols)
    slots = []
    for extent in extents:
        slots.append(pltpu.VMEM((extent // 2, BLOCK), jnp.float32))
        slots.append(pltpu.VMEM((chips - 1, extent // cols, BLOCK), jnp.float32))
    vmem = pl.BlockSpec(memory_space=pltpu.VMEM)
    anywhere = pl.BlockSpec(memory_space=pl.ANY)
    return pl.pallas_call(
        functools.partial(fast_gather_kernel, cols, columns),
        out_shape=(
            jax.ShapeDtypeStruct((2 * rows, width), jnp.bfloat16),
            jax.ShapeDtypeStruct((2 * rows, width), jnp.bfloat16),
            jax.ShapeDtypeStruct((starts[2], BLOCK), jnp.float32),
            jax.ShapeDtypeStruct((rows, rows), jnp.float32),
            jax.ShapeDtypeStruct((rows, rows), jnp.float32),
            jax.ShapeDtypeStruct((2 * extents[2], BLOCK), jnp.float32),
        ),
        in_specs=[anywhere],
        out_specs=(anywhere, anywhere, anywhere, anywhere, anywhere, vmem),
        scratch_shapes=[
            pltpu.VMEM((rows, length), jnp.float32),
            pltpu.VMEM((rows, width), jnp.float32),
            pltpu.VMEM((starts[2], BLOCK), jnp.float32),
            pltpu.VMEM((rows, rows), jnp.float32),
            pltpu.VMEM((rows, rows), jnp.float32),
            *[pltpu.VMEM((rows, width), jnp.bfloat16)] * 4,
            pltpu.VMEM((rows, rows), jnp.float32),
            pltpu.VMEM((rows, rows), jnp.float32),
            pltpu.VMEM((rows, rows), jnp.float32),
            pltpu.VMEM((2, BLOCK, BLOCK), jnp.float32),
            *[pltpu.VMEM((extent, BLOCK), jnp.float32) for extent in extents],
            *slots,
            pltpu.SemaphoreType.DMA((2 * PIECES + 16 + 6 * (chips - 1),)),
            pltpu.SemaphoreType.REGULAR((3,)),
        ],
        compiler_params=pltpu.CompilerParams(collective_id=0, has_side_effects=True),
        name="fast_gather",
    )(tensor)


def fast_linear_kernel(cols, columns, early_ref, late_ref, lead_ref, inverse_ref, start_ref, high_ref, low_ref, factor_ref, basis_ref, core_ref, gram, split, work, aug_f, aug_last, aug_b, flat_high, flat_low, core, flat_sem, core_sem):
    size, rank = start_ref.shape
    rows = size // 2
    width = core_ref.shape[2]
    per, _, first, inner, extents, starts, _ = fast_layout(rows, cols)
    loads = [
        pltpu.make_async_copy(lead_ref, factor_ref.at[0:rows, 0:rows], flat_sem.at[0]),
        pltpu.make_async_copy(high_ref, flat_high, flat_sem.at[1]),
        pltpu.make_async_copy(low_ref, flat_low, flat_sem.at[2]),
    ]
    for load in loads:
        load.start()

    scale = 1.0 / columns
    for m in range(2):
        for at, (i, k) in enumerate(inner):
            begin = starts[0] + m * extents[0] + at * BLOCK
            block = early_ref[begin : begin + BLOCK, :] * scale
            tall = slice(m * rows + i * BLOCK, m * rows + (i + 1) * BLOCK)
            wide = slice(m * rows + k * BLOCK, m * rows + (k + 1) * BLOCK)
            gram[tall, wide] = block
            if i != k:
                gram[wide, tall] = block.T
    pair = []
    for m in range(2):
        blocks = []
        for c in range(per):
            a = starts[1] + m * extents[1] + c * first
            b = m * extents[2] + c * (rows - first)
            blocks.append(jnp.concatenate([early_ref[a : a + first, :], late_ref[b : b + rows - first, :]], axis=0))
        pair.append(jnp.concatenate(blocks, axis=1))
    lower = (pair[0] + pair[1].T) * scale
    gram[rows:size, 0:rows] = lower
    gram[0:rows, rows:size] = lower.T
    for p, part in enumerate(thirds(gram[...])):
        split[p] = part

    row = lax.broadcasted_iota(jnp.int32, (BLOCK, BLOCK), 0)
    column = lax.broadcasted_iota(jnp.int32, (BLOCK, BLOCK), 1)
    factor_ref[0:rows, rows:size] = jnp.zeros((rows, rows), jnp.float32)
    left = six_terms([split[p, rows:size, 0:rows] for p in range(3)], thirds(inverse_ref[...]), NT)
    factor_ref[rows:size, 0:rows] = left
    parts = thirds(left)
    work[...] = gram[rows:size, rows:size] - six_terms(parts, parts, NT)

    basis = start_ref[...]
    for step in range(max(per, POWER)):
        augs = []
        at, below = step * BLOCK, (step + 1) * BLOCK
        if step < POWER:
            image = thirds(six_terms([split[p] for p in range(3)], thirds(basis), NN))
            load_augmented(aug_b, self_product(image))
            augs.append(aug_b)
        if step < per:
            block = aug_f if below < rows else aug_last
            load_augmented(block, work[at:below, at:below])
            augs.append(block)
        eliminate(augs)
        if step < POWER:
            basis = six_terms(image, thirds(aug_b[1]), NT)
        if step < per:
            upper = jnp.where(row <= column, block[0], 0.0)
            factor_ref[rows + at : rows + below, rows + at : rows + below] = upper.T
            if step > 0:
                factor_ref[rows : rows + at, rows + at : rows + below] = jnp.zeros((at, BLOCK), jnp.float32)
            if below < rows:
                left = six_terms(thirds(work[below:rows, at:below]), thirds(aug_f[1]), NT)
                factor_ref[rows + below : size, rows + at : rows + below] = left
                parts = thirds(left)
                work[below:rows, below:rows] = work[below:rows, below:rows] - six_terms(parts, parts, NT)

    basis_ref[...] = basis
    for load in loads:
        load.wait()
    high, low = halves(basis)
    both = jnp.concatenate([high, low], axis=1)
    piece = min(CHUNK, width)
    copies = []
    for start in range(0, width, piece):
        part = slice(start, start + piece)
        product = contract(both, flat_high[:, part], TN)
        core[:, part] = product[0:rank] + (product[rank:] + contract(high, flat_low[:, part], TN))
        copy = pltpu.make_async_copy(core.at[:, part], core_ref.at[:, 0, part], core_sem.at[len(copies)])
        copy.start()
        copies.append(copy)
    for copy in copies:
        copy.wait()


def fast_linear(columns, early, late, lead, inverse, start_basis, high, low):
    size, rank = start_basis.shape
    rows, width = size // 2, high.shape[1]
    vmem = pl.BlockSpec(memory_space=pltpu.VMEM)
    anywhere = pl.BlockSpec(memory_space=pl.ANY)
    return pl.pallas_call(
        functools.partial(fast_linear_kernel, lax.axis_size("col"), columns),
        out_shape=(
            jax.ShapeDtypeStruct((size, size), jnp.float32),
            jax.ShapeDtypeStruct((size, rank), jnp.float32),
            jax.ShapeDtypeStruct((rank, 1, width), jnp.float32),
        ),
        in_specs=[vmem, vmem, anywhere, vmem, vmem, anywhere, anywhere],
        out_specs=(vmem, vmem, anywhere),
        scratch_shapes=[
            pltpu.VMEM((size, size), jnp.float32),
            pltpu.VMEM((3, size, size), jnp.bfloat16),
            pltpu.VMEM((rows, rows), jnp.float32),
            pltpu.VMEM((2, BLOCK, BLOCK), jnp.float32),
            pltpu.VMEM((1, BLOCK, BLOCK), jnp.float32),
            pltpu.VMEM((2, rank, rank), jnp.float32),
            pltpu.VMEM((size, width), jnp.bfloat16),
            pltpu.VMEM((size, width), jnp.bfloat16),
            pltpu.VMEM((rank, width), jnp.float32),
            pltpu.SemaphoreType.DMA((3,)),
            pltpu.SemaphoreType.DMA((width // min(CHUNK, width),)),
        ],
        name="fast_linear",
    )(early, late, lead, inverse, start_basis, high, low)


def per_device(tensor, start_basis):
    modes, cols = lax.axis_size("mode"), lax.axis_size("col")
    depth = tensor.shape[1]
    columns = depth * tensor.shape[2] * cols
    if fast_case(modes, cols, tensor.shape):
        high, low, early, lead, inverse, late = fast_gather(tensor, columns)
        return fast_linear(columns, early, late, lead, inverse, start_basis, high, low)
    flat, packed = gather(tensor)
    return linear(columns, depth, packed, start_basis, flat)


def solution(mesh):
    in_specs = (P("mode", "col", None), P())
    out_specs = (P(), P(), P(None, "col", "mode"))
    return jax.shard_map(
        per_device, mesh=mesh, in_specs=in_specs, out_specs=out_specs, check_vma=False
    )
```

```python
import functools
import itertools

import jax
import jax.numpy as jnp
from jax import lax
from jax.experimental import pallas as pl
from jax.experimental.pallas import tpu as pltpu
from jax.sharding import PartitionSpec as P

POWER = 2
BLOCK = 128
PANEL = 8
CHUNK = 512
MESH = pl.DeviceIdType.MESH


def halves(value):
    high = value.astype(jnp.bfloat16)
    low = (value - high.astype(jnp.float32)).astype(jnp.bfloat16)
    return high, low


def contract(left, right, dims):
    return lax.dot_general(left, right, (dims, ((), ())), preferred_element_type=jnp.float32)


def exact(left, right, dims):
    return lax.dot_general(
        left, right, (dims, ((), ())), precision=lax.Precision.HIGHEST,
        preferred_element_type=jnp.float32,
    )


NN = ((1,), (0,))
NT = ((1,), (1,))
TN = ((0,), (0,))


def thirds(value):
    high = value.astype(jnp.bfloat16)
    rest = value - high.astype(jnp.float32)
    middle = rest.astype(jnp.bfloat16)
    low = (rest - middle.astype(jnp.float32)).astype(jnp.bfloat16)
    return high, middle, low


def six_terms(left, right, dims):
    high, middle, low = right
    beside, along = (1, 0) if dims == NN else (0, 1)
    wide = jnp.concatenate([high, middle], axis=beside)
    first = contract(
        jnp.concatenate([left[0], left[1]], axis=1), jnp.concatenate([wide, wide], axis=along), dims
    )
    second = contract(
        jnp.concatenate([left[2], left[0]], axis=1), jnp.concatenate([high, low], axis=along), dims
    )
    count = second.shape[1]
    return first[:, 0:count] + (first[:, count:] + second)


def self_product(parts):
    high, middle, low = parts
    pair = jnp.concatenate([high, middle], axis=1)
    product = contract(pair, pair, TN)
    small = contract(high, low, TN)
    count = small.shape[0]
    rest = (product[0:count, count:] + product[count:, 0:count]) + (product[count:, count:] + (small + small.T))
    return product[0:count, 0:count] + rest


def split3(value):
    high = value.astype(jnp.bfloat16).astype(jnp.float32)
    rest = value - high
    middle = rest.astype(jnp.bfloat16).astype(jnp.float32)
    return high, middle, rest - middle


def spread(tile, lane):
    return jnp.broadcast_to(tile[:, lane : lane + 1], tile.shape)


def eliminate_panel(aug, j):
    parts, size, _ = aug.shape
    first = PANEL * j
    after = first + PANEL
    below = after + PANEL
    rows = [[aug[p, pl.ds(first + t, PANEL, stride=0), :] for p in range(parts)] for t in range(PANEL)]
    entry = {}
    for s in range(PANEL):
        for t in range(s + 1):
            entry[s, t] = spread(rows[t][0], first + s)
    if after < size:
        following = [aug[p, after:below, :] for p in range(parts)]
        column = [spread(following[0], first + t) for t in range(PANEL)]
    for t in range(PANEL):
        inverse = 1.0 / entry[t, t]
        for s in range(t + 1, PANEL):
            ratio = entry[s, t] * inverse
            for u in range(s, PANEL):
                entry[u, s] = entry[u, s] - ratio * entry[u, t]
            rows[s] = [a - ratio * b for a, b in zip(rows[s], rows[t])]
        scale = lax.rsqrt(entry[t, t])
        for p in range(parts):
            aug[p, first + t : first + t + 1, :] = (rows[t][p] * scale)[0:1]
        if after < size:
            ratio = column[t] * inverse
            for u in range(t + 1, PANEL):
                column[u] = column[u] - ratio * entry[u, t]
            following = [a - ratio * b for a, b in zip(following, rows[t])]
    if after < size:
        for p in range(parts):
            aug[p, after:below, :] = following[p]
    if below < size:
        rights = []
        for p in range(parts):
            high, middle, low = split3(aug[p, first:after, :])
            if p == 0:
                left = jnp.concatenate([high, high, middle, high, low, middle], axis=0).astype(jnp.bfloat16)
            rights.append(jnp.concatenate([high, middle, high, low, high, middle], axis=0).astype(jnp.bfloat16))
        update = contract(left, jnp.concatenate(rights, axis=1), TN)
        for p in range(parts):
            aug[p, below:size, :] = aug[p, below:size, :] - update[below:size, p * size : (p + 1) * size]


def eliminate(augs):
    for j in range(BLOCK // PANEL):
        for aug in augs:
            eliminate_panel(aug, j)


def load_augmented(aug, matrix):
    size = matrix.shape[0]
    aug[0] = matrix
    if aug.shape[0] > 1:
        row = lax.broadcasted_iota(jnp.int32, (size, size), 0)
        column = lax.broadcasted_iota(jnp.int32, (size, size), 1)
        aug[1] = jnp.where(row == column, 1.0, 0.0).astype(jnp.float32)


def lower_blocks(blocks):
    return [(i, k) for i in range(blocks) for k in range(i + 1)]


def stages_of(modes, cols):
    stages, stride = [], 1
    first = 2 if cols % 2 == 0 else 1
    if first > 1:
        stages.append((1, first, False))
        stride = first
    second = 2 if (cols // stride) % 2 == 0 else 1
    stages.append((stride, second, True))
    stride *= second
    if cols // stride > 1:
        stages.append((stride, cols // stride, False))
    return stages


def round_up(value, unit):
    return -(-value // unit) * unit


def layout_of(size, modes, cols):
    pairs = lower_blocks(size // BLOCK)
    rows = size // modes
    inner = []
    if rows % BLOCK == 0 and modes > 1:
        inner = lower_blocks(rows // BLOCK)
    per = rows // BLOCK
    extent = round_up(len(inner) * BLOCK, 8 * cols)
    where = {}
    for m in range(modes):
        for n, (i, k) in enumerate(inner):
            where[m * per + i, m * per + k] = m * extent + n * BLOCK
    outer = [pair for pair in pairs if pair not in where]
    for n, pair in enumerate(outer):
        where[pair] = modes * extent + n * BLOCK
    return where, inner, extent, outer, round_up(len(outer) * BLOCK, 8 * modes * cols)


def members_of(stages, modes):
    return [count * (modes if with_mode else 1) for _, count, with_mode in stages]


def gather_kernel(modes, cols, x_ref, flat_ref, total_ref, local, acc_in, acc_out, main, cross, *rest):
    mode, col = lax.axis_index("mode"), lax.axis_index("col")
    all_stages = stages_of(modes, cols)
    col_stages = [(stride, count, False) for stride, count, _ in all_stages]
    n = len(all_stages)
    slots_in, slots_out = rest[:n], rest[n : 2 * n]
    local_sem, piece_send, piece_recv, swap_send, swap_recv, in_sems, out_sems, share_in, share_out = rest[2 * n :]
    rows, depth, length = x_ref.shape
    size = rows * modes
    width = length // modes
    chunk = min(CHUNK, width)
    per = width // chunk
    chunks = depth * per
    where, inner, in_extent, outer, out_extent = layout_of(size, modes, cols)

    def position(stage):
        stride, count, with_mode = stage
        place = lax.rem(lax.div(col, stride), count)
        return place * modes + mode if with_mode else place

    def members(stage):
        return stage[1] * (modes if stage[2] else 1)

    def peer(stage, offset):
        stride, count, with_mode = stage
        other = lax.rem(position(stage) + offset, members(stage))
        place = lax.div(other, modes) if with_mode else other
        there = col + (place - lax.rem(lax.div(col, stride), count)) * stride
        return other, (lax.rem(other, modes) if with_mode else mode, there)

    partners = [(lax.rem(mode + d, modes), col) for d in range(1, modes)]
    greeted = []
    for stage in all_stages:
        greeted += [peer(stage, d)[1] for d in range(1, members(stage))]
    barrier = pltpu.get_barrier_semaphore()
    for device in greeted:
        pl.semaphore_signal(barrier, inc=1, device_id=device, device_id_type=MESH)
    pl.semaphore_wait(barrier, len(greeted))

    own_rows = pl.ds(pl.multiple_of(mode * rows, rows), rows)

    def spans(c):
        layer, part = lax.div(c, per), lax.rem(c, per)
        return layer, part * chunk, pl.multiple_of(layer * width + part * chunk, chunk)

    def piece(c, d):
        layer, start, target = spans(c)
        source = pl.multiple_of(lax.rem(mode + d, modes) * width + start, chunk)
        return pltpu.make_async_remote_copy(
            src_ref=x_ref.at[:, layer, pl.ds(source, chunk)],
            dst_ref=flat_ref.at[own_rows, pl.ds(target, chunk)],
            send_sem=piece_send.at[d - 1, c],
            recv_sem=piece_recv.at[d - 1, c],
            device_id=partners[d - 1],
            device_id_type=MESH,
        )

    def load(c):
        layer, part = lax.div(c, per * modes), lax.rem(c, per * modes)
        source = pl.multiple_of(part * chunk, chunk)
        target = pl.multiple_of(layer * length + part * chunk, chunk)
        return pltpu.make_async_copy(
            x_ref.at[:, layer, pl.ds(source, chunk)], local.at[:, pl.ds(target, chunk)], local_sem.at[c]
        ), target

    def begin(c, carry):
        for d in range(1, modes):
            piece(c, d).start()
        return carry

    def begin_load(c, carry):
        load(c)[0].start()
        return carry

    early = max(chunks // 2, 1)
    lax.fori_loop(0, early, begin, 0)
    lax.fori_loop(0, chunks * modes, begin_load, 0)

    main[...] = jnp.zeros_like(main)
    cross[...] = jnp.zeros_like(cross)

    def accumulate_in(c, carry):
        copy, target = load(c)
        copy.wait()
        if inner:
            high, low = halves(local[:, pl.ds(target, chunk)])
            main[0:rows, 0:rows] += contract(high, high, NT)
            cross[0:rows, 0:rows] += contract(high, low, NT)
        return carry

    lax.fori_loop(0, chunks * modes, accumulate_in, 0)
    for layer in range(depth):
        source = pl.multiple_of(layer * length + mode * width, chunk)
        flat_ref[own_rows, layer * width : (layer + 1) * width] = local[:, pl.ds(source, width)]

    def pack(acc, pairs, extent):
        for at, (i, k) in enumerate(pairs):
            tall, wide = slice(i * BLOCK, (i + 1) * BLOCK), slice(k * BLOCK, (k + 1) * BLOCK)
            acc[at * BLOCK : (at + 1) * BLOCK, :] = main[tall, wide] + (cross[tall, wide] + cross[wide, tall].T)
        used = len(pairs) * BLOCK
        if used < extent:
            acc[used:, :] = jnp.zeros((extent - used, BLOCK), jnp.float32)

    def scatter_sum(stages, acc, extent, slots, sems, target):
        base, bases = 0, []
        for g, stage in enumerate(stages):
            count = members(stage)
            part = extent // count
            copies = []
            for d in range(1, count):
                other, device = peer(stage, d)
                copy = pltpu.make_async_remote_copy(
                    src_ref=acc.at[pl.ds(pl.multiple_of(base + other * part, 8), part), :],
                    dst_ref=slots[g].at[d - 1],
                    send_sem=sems.at[0, g, d - 1],
                    recv_sem=sems.at[1, g, d - 1],
                    device_id=device,
                    device_id_type=MESH,
                )
                copy.start()
                copies.append(copy)
            base = base + position(stage) * part
            extent = part
            bases.append((base, part))
            for copy in copies:
                copy.wait()
            mine = pl.ds(pl.multiple_of(base, 8), part)
            added = acc[mine, :]
            for d in range(1, count):
                added = added + slots[g][d - 1]
            if g < len(stages) - 1:
                acc[mine, :] = added
            else:
                total_ref[pl.ds(pl.multiple_of(target + base, 8), part), :] = added
        return bases

    def share(stages, bases, targets, sems):
        for g in reversed(range(len(stages))):
            stage = stages[g]
            base, part = bases[g]
            copies = []
            for d in range(1, members(stage)):
                for t, target in enumerate(targets):
                    mine = pl.ds(pl.multiple_of(target + base, 8), part)
                    copy = pltpu.make_async_remote_copy(
                        src_ref=total_ref.at[mine, :],
                        dst_ref=total_ref.at[mine, :],
                        send_sem=sems.at[0, g, (d - 1) * len(targets) + t],
                        recv_sem=sems.at[1, g, (d - 1) * len(targets) + t],
                        device_id=peer(stage, d)[1],
                        device_id_type=MESH,
                    )
                    copy.start()
                    copies.append(copy)
            for copy in copies:
                copy.wait()

    def accumulate_out(c, carry):
        for d in range(1, modes):
            piece(c, d).wait_recv()
        high, low = halves(flat_ref[:, pl.ds(spans(c)[2], chunk)])
        if inner:
            for m in range(1, modes):
                tall, wide = slice(m * rows, (m + 1) * rows), slice(0, m * rows)
                main[tall, wide] += contract(high[tall, :], high[wide, :], NT) + contract(low[tall, :], high[wide, :], NT)
                cross[tall, wide] += contract(high[tall, :], low[wide, :], NT)
        else:
            main[...] += contract(high, high, NT)
            cross[...] += contract(high, low, NT)
        return carry

    swaps = []
    if inner:
        pack(acc_in, inner, in_extent)
        main[...] = jnp.zeros_like(main)
        cross[...] = jnp.zeros_like(cross)
        bases = scatter_sum(col_stages, acc_in, in_extent, slots_in, in_sems, mode * in_extent)
        base, part = bases[-1]
        mine = pl.ds(pl.multiple_of(mode * in_extent + base, 8), part)
        for d in range(1, modes):
            swap = pltpu.make_async_remote_copy(
                src_ref=total_ref.at[mine, :],
                dst_ref=total_ref.at[mine, :],
                send_sem=swap_send.at[d - 1],
                recv_sem=swap_recv.at[d - 1],
                device_id=partners[d - 1],
                device_id_type=MESH,
            )
            swap.start()
            swaps.append(swap)
    lax.fori_loop(early, chunks, begin, 0)
    lax.fori_loop(0, early, accumulate_out, 0)
    if inner:
        for swap in swaps:
            swap.wait()
        share(col_stages, bases, [m * in_extent for m in range(modes)], share_in)
    lax.fori_loop(early, chunks, accumulate_out, 0)

    pack(acc_out, outer, out_extent)
    bases = scatter_sum(all_stages, acc_out, out_extent, slots_out, out_sems, modes * in_extent)
    share(all_stages, bases, [modes * in_extent], share_out)

    def end(c, carry):
        for d in range(1, modes):
            piece(c, d).wait_send()
        return carry

    lax.fori_loop(0, chunks, end, 0)


def gather(tensor):
    modes, cols = lax.axis_size("mode"), lax.axis_size("col")
    rows, depth, length = tensor.shape
    size = rows * modes
    width = length // modes
    chunks = depth * (width // min(CHUNK, width))
    stages = stages_of(modes, cols)
    _, inner, in_extent, _, out_extent = layout_of(size, modes, cols)
    in_extent = max(in_extent, 8 * cols)
    slots_in, slots_out, extent_in, extent, most = [], [], in_extent, out_extent, 1
    for stride, count, with_mode in stages:
        extent_in = extent_in // count
        slots_in.append(pltpu.VMEM((max(count - 1, 1), extent_in, BLOCK), jnp.float32))
        count = count * (modes if with_mode else 1)
        extent = extent // count
        slots_out.append(pltpu.VMEM((max(count - 1, 1), extent, BLOCK), jnp.float32))
        most = max(most, count - 1)
    dma = pltpu.SemaphoreType.DMA
    vmem = pl.BlockSpec(memory_space=pltpu.VMEM)
    packed = (modes * in_extent if inner else 0) + out_extent
    return pl.pallas_call(
        functools.partial(gather_kernel, modes, cols),
        out_shape=(
            jax.ShapeDtypeStruct((size, depth * width), jnp.float32),
            jax.ShapeDtypeStruct((packed, BLOCK), jnp.float32),
        ),
        in_specs=[pl.BlockSpec(memory_space=pl.ANY)],
        out_specs=(vmem, vmem),
        scratch_shapes=[
            pltpu.VMEM((rows, depth * length), jnp.float32),
            pltpu.VMEM((in_extent, BLOCK), jnp.float32),
            pltpu.VMEM((out_extent, BLOCK), jnp.float32),
            pltpu.VMEM((size, size), jnp.float32),
            pltpu.VMEM((size, size), jnp.float32),
            *slots_in,
            *slots_out,
            dma((chunks * modes,)),
            *[dma((max(modes - 1, 1), chunks))] * 2,
            *[dma((max(modes - 1, 1),))] * 2,
            *[dma((2, len(stages), most))] * 2,
            dma((2, len(stages), most * modes)),
            dma((2, len(stages), most)),
        ],
        compiler_params=pltpu.CompilerParams(collective_id=0, has_side_effects=True),
        name="gather",
    )(tensor)


def linear_kernel(columns, where, packed_ref, start_ref, flat_ref, factor_ref, basis_ref, core_ref, gram, work, image, aug_f, aug_b, core, core_sem):
    size, rank = start_ref.shape
    blocks = size // BLOCK
    row = lax.broadcasted_iota(jnp.int32, (BLOCK, BLOCK), 0)
    column = lax.broadcasted_iota(jnp.int32, (BLOCK, BLOCK), 1)
    scale = 1.0 / columns
    for (i, k), at in where.items():
        scaled = packed_ref[at : at + BLOCK, :] * scale
        gram[i * BLOCK : (i + 1) * BLOCK, k * BLOCK : (k + 1) * BLOCK] = scaled
        work[i * BLOCK : (i + 1) * BLOCK, k * BLOCK : (k + 1) * BLOCK] = scaled
        if i != k:
            gram[k * BLOCK : (k + 1) * BLOCK, i * BLOCK : (i + 1) * BLOCK] = scaled.T

    for step in range(max(blocks, POWER)):
        augs = []
        if step < blocks:
            at = step * BLOCK
            load_augmented(aug_f, work[at : at + BLOCK, at : at + BLOCK])
            augs.append(aug_f)
        if step < POWER:
            source = start_ref if step == 0 else basis_ref
            image[...] = exact(gram[...], source[...], NN)
            load_augmented(aug_b, exact(image[...], image[...], TN))
            augs.append(aug_b)
        eliminate(augs)
        if step < POWER:
            basis_ref[...] = exact(image[...], aug_b[1], NT)
        if step < blocks:
            upper = jnp.where(row <= column, aug_f[0], 0.0)
            factor_ref[at : at + BLOCK, at : at + BLOCK] = upper.T
            if step > 0:
                factor_ref[0:at, at : at + BLOCK] = jnp.zeros((at, BLOCK), jnp.float32)
            below = at + BLOCK
            if below < size:
                inverse = aug_f[1]
                left = exact(work[below:size, at : at + BLOCK], inverse, NT)
                factor_ref[below:size, at : at + BLOCK] = left
                work[below:size, below:size] = work[below:size, below:size] - exact(left, left, NT)

    high, low = halves(basis_ref[...])
    depth, length = core_ref.shape[1:]
    width = min(CHUNK, length)
    copies = []
    for start in range(0, depth * length, width):
        part = slice(start, start + width)
        flat_high, flat_low = halves(flat_ref[:, part])
        core[:, part] = contract(high, flat_high, TN) + contract(high, flat_low, TN) + contract(low, flat_high, TN)
        layer, offset = divmod(start, length)
        copy = pltpu.make_async_copy(
            core.at[:, part], core_ref.at[:, layer, offset : offset + width], core_sem.at[len(copies)]
        )
        copy.start()
        copies.append(copy)
    for copy in copies:
        copy.wait()


def linear(columns, depth, packed, start_basis, flat):
    size, rank = start_basis.shape
    length = flat.shape[1] // depth
    where = layout_of(size, lax.axis_size("mode"), lax.axis_size("col"))[0]
    vmem = pl.BlockSpec(memory_space=pltpu.VMEM)
    return pl.pallas_call(
        functools.partial(linear_kernel, columns, where),
        out_shape=(
            jax.ShapeDtypeStruct((size, size), jnp.float32),
            jax.ShapeDtypeStruct((size, rank), jnp.float32),
            jax.ShapeDtypeStruct((rank, depth, length), jnp.float32),
        ),
        in_specs=[vmem] * 3,
        out_specs=(vmem, vmem, pl.BlockSpec(memory_space=pl.ANY)),
        scratch_shapes=[
            pltpu.VMEM((size, size), jnp.float32),
            pltpu.VMEM((size, size), jnp.float32),
            pltpu.VMEM((size, rank), jnp.float32),
            pltpu.VMEM((2, BLOCK, BLOCK), jnp.float32),
            pltpu.VMEM((2, rank, rank), jnp.float32),
            pltpu.VMEM((rank, flat.shape[1]), jnp.float32),
            pltpu.SemaphoreType.DMA((flat.shape[1] // min(CHUNK, length),)),
        ],
        name="linear",
    )(packed, start_basis, flat)


def fast_case(modes, cols, shape):
    rows, depth, length = shape
    return modes == 2 and depth == 1 and rows % (2 * BLOCK) == 0 and cols % 4 == 0 and length % (2 * BLOCK) == 0


STRIPS = 8
LATE = 4
EARLY = 3
HELD = 2
PIECES = STRIPS + 2


def fast_cuts(strip):
    return sorted([k * strip for k in range(STRIPS + 1)] + [2 * strip + strip // 2, 6 * strip + strip // 2])


def fast_layout(rows, cols):
    per = rows // BLOCK
    strip = rows // STRIPS
    first = rows - LATE * strip
    inner = lower_blocks(per)
    unit = 8 * cols
    extents = [round_up(len(inner) * BLOCK, unit), round_up(first * per, unit), round_up((rows - first) * per, unit)]
    starts, at = [], 0
    for extent in extents:
        starts.append(at)
        at += 2 * extent
    return per, strip, first, inner, extents, starts, at


def fast_gather_kernel(cols, columns, x_ref, high_out, low_out, early_out, lead_out, inverse_out, late_ref, local, recv, early_ref, lead_ref, inverse_ref, own_high, own_low, other_high, other_low, main, cross, work, aug, acc_in, acc_a, acc_b, *rest):
    slots, sems, hello = rest[:-2], rest[-2], rest[-1]
    mode, col = lax.axis_index("mode"), lax.axis_index("col")
    other_mode = 1 - mode
    rows, _, length = x_ref.shape
    width = length // 2
    chips = cols // 2
    per, strip, first, inner, extents, starts, _ = fast_layout(rows, cols)
    core, chip = lax.rem(col, 2), lax.div(col, 2)
    names = {}
    pending = {}

    def sem(*name):
        return sems.at[names.setdefault(name, len(names))]

    def drain(*kinds):
        for name in [name for name in pending if name[0] in kinds]:
            pending.pop(name).wait_send()

    def push(source, target, device, *name):
        if name in pending:
            pending.pop(name).wait_send()
        copy = pltpu.make_async_remote_copy(
            src_ref=source, dst_ref=target, send_sem=sem("send", *name), recv_sem=sem("recv", *name),
            device_id=device, device_id_type=MESH,
        )
        copy.start()
        pending[name] = copy
        return copy

    sibling = (mode, chip * 2 + 1 - core)
    partner = (other_mode, col)
    plane = []
    for d in range(1, chips):
        place = lax.rem(chip + d, chips)
        plane.append((place, (mode, place * 2 + core)))

    line = chips // 2
    place = lax.div(chip, 2)
    beside = (mode, (place * 2 + 1 - lax.rem(chip, 2)) * 2 + core)
    above, under = (mode, col + 4), (mode, col - 4)
    has_above, has_under = place < line - 1, place > 0

    def hail(semaphore, device):
        pl.semaphore_signal(semaphore, inc=1, device_id=device, device_id_type=MESH)

    barrier = pltpu.get_barrier_semaphore()
    for device in (partner, sibling, beside):
        hail(barrier, device)
    pl.when(has_above)(lambda: hail(barrier, above))
    pl.when(has_under)(lambda: hail(barrier, under))
    pl.semaphore_wait(barrier, 3 + has_above.astype(jnp.int32) + has_under.astype(jnp.int32))

    def meet_line():
        pl.when(has_under)(lambda: pl.semaphore_wait(hello.at[0], 1))
        pl.when(has_above)(lambda: hail(hello.at[0], above))
        pl.when(has_above)(lambda: pl.semaphore_wait(hello.at[1], 1))
        pl.when(has_under)(lambda: hail(hello.at[1], under))
        hail(hello.at[2], beside)

    def meet_beside():
        pl.semaphore_wait(hello.at[2], 1)
        hail(hello.at[3], partner)

    def meet_across():
        pl.semaphore_wait(hello.at[3], 1)

    pieces = []
    away = pl.ds(pl.multiple_of(other_mode * width, width), width)

    cuts = fast_cuts(strip)

    def send_piece(k):
        span = slice(cuts[k], cuts[k + 1])
        pieces.append(push(x_ref.at[span, 0, away], recv.at[span, :], partner, "piece", k))
        del pending["piece", k]

    for k in range(EARLY):
        send_piece(k)

    loads = []
    part = length // 4
    for c in range(4):
        span = slice(c * part, (c + 1) * part)
        copy = pltpu.make_async_copy(x_ref.at[:, 0, span], local.at[:, span], sem("local", c))
        copy.start()
        loads.append(copy)
    for c in range(4):
        if c == 1:
            meet_line()
        loads[c].wait()
        high, low = halves(local[:, c * part : (c + 1) * part])
        if c == 0:
            main[...] = contract(high, high, NT)
            cross[...] = contract(high, low, NT)
        else:
            main[...] += contract(high, high, NT)
            cross[...] += contract(high, low, NT)

    for at, (i, k) in enumerate(inner):
        tall, wide = slice(i * BLOCK, (i + 1) * BLOCK), slice(k * BLOCK, (k + 1) * BLOCK)
        acc_in[at * BLOCK : (at + 1) * BLOCK, :] = main[tall, wide] + (cross[tall, wide] + cross[wide, tall].T)

    def fill(acc, used):
        if used < acc.shape[0]:
            acc[used:, :] = jnp.zeros((acc.shape[0] - used, BLOCK), jnp.float32)

    def rows_at(base, count):
        return pl.ds(pl.multiple_of(base, 8), count)

    def core_send(acc, slot):
        half = acc.shape[0] // 2
        return push(acc.at[rows_at((1 - core) * half, half), :], slot.at[...], sibling, "core")

    def core_add(acc, slot, copy):
        half = acc.shape[0] // 2
        copy.wait_recv()
        mine = rows_at(core * half, half)
        acc[mine, :] = acc[mine, :] + slot[...]

    def plane_send(acc, slot):
        half = acc.shape[0] // 2
        share = half // chips
        copies = []
        for d, (place, device) in enumerate(plane):
            copies.append(push(acc.at[rows_at(core * half + place * share, share), :], slot.at[d], device, "plane", d))
        return copies

    def plane_add(acc, slot, copies, total, start):
        half = acc.shape[0] // 2
        share = half // chips
        base = core * half + chip * share
        for copy in copies:
            copy.wait_recv()
        added = acc[rows_at(base, share), :]
        for d in range(chips - 1):
            added = added + slot[d]
        total[rows_at(start + mode * acc.shape[0] + base, share), :] = added

    def swap(acc, total, start, phase):
        half = acc.shape[0] // 2
        share = half // chips
        mine = rows_at(start + mode * acc.shape[0] + core * half + chip * share, share)
        return push(total.at[mine, :], total.at[mine, :], partner, "swap", phase)

    def plane_share(acc, total, start, modes):
        half = acc.shape[0] // 2
        share = half // chips
        copies = []
        for d, (_, device) in enumerate(plane):
            for at, m in modes:
                mine = rows_at(start + m * acc.shape[0] + core * half + chip * share, share)
                copies.append(push(total.at[mine, :], total.at[mine, :], device, "share", d, at))
        return copies

    def direct_share(acc, total, start):
        half = acc.shape[0] // 2
        share = half // chips
        mine = rows_at(start + mode * acc.shape[0] + core * half + chip * share, share)
        copies = []
        for d in range(chips):
            device = (other_mode, lax.rem(chip + d, chips) * 2 + core)
            copies.append(push(total.at[mine, :], total.at[mine, :], device, "across", d))
        return copies

    def core_share(acc, total, start):
        half = acc.shape[0] // 2
        copies = []
        for m in range(2):
            mine = rows_at(start + m * acc.shape[0] + core * half, half)
            copies.append(push(total.at[mine, :], total.at[mine, :], sibling, "both", m))
        return copies

    def arrive(copies):
        for copy in copies:
            copy.wait_recv()

    outgoing = {}
    leaving = [0]
    both = [(0, 0), (1, 1)]

    def leave(source, target):
        lane = leaving[0] % len(loads)
        leaving[0] += 1
        if lane in outgoing:
            outgoing.pop(lane).wait()
        copy = pltpu.make_async_copy(source, target, sem("local", lane))
        copy.start()
        outgoing[lane] = copy

    def strips(begin, end, acc, offset, tall):
        span = slice(begin * strip, end * strip)
        arrive(pieces[cuts.index(begin * strip) : cuts.index(end * strip)])
        high, low = halves(recv[span, :])
        other_high[span, :] = high
        other_low[span, :] = low
        target = pl.ds(pl.multiple_of(other_mode * rows + begin * strip, strip), (end - begin) * strip)
        leave(other_high.at[span, :], high_out.at[target, :])
        leave(other_low.at[span, :], low_out.at[target, :])
        both = contract(own_high[...], jnp.concatenate([high, low], axis=0), NT)
        count = high.shape[0]
        value = both[:, 0:count] + (both[:, count:] + contract(own_low[...], high, NT))
        value = value.T
        for c in range(per):
            at = c * tall + begin * strip - offset
            acc[at : at + (end - begin) * strip, :] = value[:, c * BLOCK : (c + 1) * BLOCK]

    fill(acc_in, len(inner) * BLOCK)
    meet_beside()
    copy = core_send(acc_in, slots[0])
    mine = local[:, pl.ds(pl.multiple_of(mode * width, width), width)]
    high, low = halves(mine)
    own_high[...] = high
    own_low[...] = low
    core_add(acc_in, slots[0], copy)
    copies = plane_send(acc_in, slots[1])
    target = pl.ds(pl.multiple_of(mode * rows, rows), rows)
    leave(own_high, high_out.at[target, :])
    leave(own_low, low_out.at[target, :])
    plane_add(acc_in, slots[1], copies, early_ref, starts[0])
    meet_across()
    copy = swap(acc_in, early_ref, starts[0], 0)
    for k in range(EARLY, PIECES - HELD):
        send_piece(k)
    strips(0, 1, acc_a, 0, first)
    arrive([copy])
    copies = plane_share(acc_in, early_ref, starts[0], both)
    drain("core", "plane", "swap")
    strips(1, 2, acc_a, 0, first)
    arrive(copies)
    arrive(core_share(acc_in, early_ref, starts[0]))

    scale = 1.0 / columns
    for at, (i, k) in enumerate(inner):
        tall, wide = slice(i * BLOCK, (i + 1) * BLOCK), slice(k * BLOCK, (k + 1) * BLOCK)
        work[tall, wide] = early_ref[starts[0] + at * BLOCK : starts[0] + (at + 1) * BLOCK, :] * scale
    lead_ref[...] = jnp.zeros_like(lead_ref)
    inverse_ref[...] = jnp.zeros_like(inverse_ref)
    row = lax.broadcasted_iota(jnp.int32, (BLOCK, BLOCK), 0)
    column = lax.broadcasted_iota(jnp.int32, (BLOCK, BLOCK), 1)
    for step in range(per):
        at, below = step * BLOCK, (step + 1) * BLOCK
        load_augmented(aug, work[at:below, at:below])
        eliminate([aug])
        lead_ref[at:below, at:below] = jnp.where(row <= column, aug[0], 0.0).T
        inverse = aug[1]
        inverse_ref[at:below, at:below] = inverse
        if step > 0:
            inverse_ref[at:below, 0:at] = -exact(inverse, exact(lead_ref[at:below, 0:at], inverse_ref[0:at, 0:at], NN), NN)
        if below < rows:
            left = exact(work[below:rows, at:below], inverse, NT)
            lead_ref[below:rows, at:below] = left
            work[below:rows, below:rows] = work[below:rows, below:rows] - exact(left, left, NT)
        if step == 0:
            strips(2, STRIPS - LATE, acc_a, 0, first)
            fill(acc_a, first * per)
            core_add(acc_a, slots[2], core_send(acc_a, slots[2]))
            copies = plane_send(acc_a, slots[3])
    plane_add(acc_a, slots[3], copies, early_ref, starts[1])
    copy = swap(acc_a, early_ref, starts[1], 1)
    for k in range(PIECES - HELD, PIECES):
        send_piece(k)
    leave(lead_ref, lead_out)
    leave(inverse_ref, inverse_out)
    strips(STRIPS - LATE, STRIPS - 2, acc_b, first, rows - first)
    arrive([copy])
    copies = plane_share(acc_a, early_ref, starts[1], both)
    drain("core", "plane", "swap", "both")
    for copy in pieces[:-HELD]:
        copy.wait_send()
    strips(STRIPS - 2, STRIPS - 1, acc_b, first, rows - first)
    arrive(copies)
    copies = core_share(acc_a, early_ref, starts[1])
    drain("share")
    arrive(copies)
    leave(early_ref, early_out)
    strips(STRIPS - 1, STRIPS, acc_b, first, rows - first)
    fill(acc_b, (rows - first) * per)
    core_add(acc_b, slots[4], core_send(acc_b, slots[4]))
    plane_add(acc_b, slots[5], plane_send(acc_b, slots[5]), late_ref, 0)
    copies = direct_share(acc_b, late_ref, 0) + plane_share(acc_b, late_ref, 0, [(0, mode)])
    drain("core", "plane", "both")
    for copy in pieces[-HELD:]:
        copy.wait_send()
    for copy in outgoing.values():
        copy.wait()
    arrive(copies)
    copies = core_share(acc_b, late_ref, 0)
    drain("share", "across")
    arrive(copies)
    drain("both")


def fast_gather(tensor, columns):
    cols = lax.axis_size("col")
    rows, _, length = tensor.shape
    width = length // 2
    chips = cols // 2
    _, _, _, _, extents, starts, _ = fast_layout(rows, cols)
    slots = []
    for extent in extents:
        slots.append(pltpu.VMEM((extent // 2, BLOCK), jnp.float32))
        slots.append(pltpu.VMEM((chips - 1, extent // cols, BLOCK), jnp.float32))
    vmem = pl.BlockSpec(memory_space=pltpu.VMEM)
    anywhere = pl.BlockSpec(memory_space=pl.ANY)
    return pl.pallas_call(
        functools.partial(fast_gather_kernel, cols, columns),
        out_shape=(
            jax.ShapeDtypeStruct((2 * rows, width), jnp.bfloat16),
            jax.ShapeDtypeStruct((2 * rows, width), jnp.bfloat16),
            jax.ShapeDtypeStruct((starts[2], BLOCK), jnp.float32),
            jax.ShapeDtypeStruct((rows, rows), jnp.float32),
            jax.ShapeDtypeStruct((rows, rows), jnp.float32),
            jax.ShapeDtypeStruct((2 * extents[2], BLOCK), jnp.float32),
        ),
        in_specs=[anywhere],
        out_specs=(anywhere, anywhere, anywhere, anywhere, anywhere, vmem),
        scratch_shapes=[
            pltpu.VMEM((rows, length), jnp.float32),
            pltpu.VMEM((rows, width), jnp.float32),
            pltpu.VMEM((starts[2], BLOCK), jnp.float32),
            pltpu.VMEM((rows, rows), jnp.float32),
            pltpu.VMEM((rows, rows), jnp.float32),
            *[pltpu.VMEM((rows, width), jnp.bfloat16)] * 4,
            pltpu.VMEM((rows, rows), jnp.float32),
            pltpu.VMEM((rows, rows), jnp.float32),
            pltpu.VMEM((rows, rows), jnp.float32),
            pltpu.VMEM((2, BLOCK, BLOCK), jnp.float32),
            *[pltpu.VMEM((extent, BLOCK), jnp.float32) for extent in extents],
            *slots,
            pltpu.SemaphoreType.DMA((2 * PIECES + 16 + 8 * (chips - 1),)),
            pltpu.SemaphoreType.REGULAR((4,)),
        ],
        compiler_params=pltpu.CompilerParams(collective_id=0, has_side_effects=True),
        name="fast_gather",
    )(tensor)


def fast_linear_kernel(cols, columns, early_ref, late_ref, lead_ref, inverse_ref, start_ref, high_ref, low_ref, factor_out, basis_out, core_ref, factor_ref, basis_ref, gram, split, work, aug_f, aug_last, aug_b, flat_high, flat_low, core, flat_sem, out_sem, core_sem):
    size, rank = start_ref.shape
    rows = size // 2
    width = core_ref.shape[2]
    per, _, first, inner, extents, starts, _ = fast_layout(rows, cols)
    loads = [
        pltpu.make_async_copy(lead_ref, factor_ref.at[0:rows, 0:rows], flat_sem.at[0]),
        pltpu.make_async_copy(high_ref, flat_high, flat_sem.at[1]),
        pltpu.make_async_copy(low_ref, flat_low, flat_sem.at[2]),
    ]
    for load in loads:
        load.start()

    scale = 1.0 / columns
    for m in range(2):
        for at, (i, k) in enumerate(inner):
            begin = starts[0] + m * extents[0] + at * BLOCK
            block = early_ref[begin : begin + BLOCK, :] * scale
            tall = slice(m * rows + i * BLOCK, m * rows + (i + 1) * BLOCK)
            wide = slice(m * rows + k * BLOCK, m * rows + (k + 1) * BLOCK)
            gram[tall, wide] = block
            if i != k:
                gram[wide, tall] = block.T
    pair = []
    for m in range(2):
        blocks = []
        for c in range(per):
            a = starts[1] + m * extents[1] + c * first
            b = m * extents[2] + c * (rows - first)
            blocks.append(jnp.concatenate([early_ref[a : a + first, :], late_ref[b : b + rows - first, :]], axis=0))
        pair.append(jnp.concatenate(blocks, axis=1))
    lower = (pair[0] + pair[1].T) * scale
    gram[rows:size, 0:rows] = lower
    gram[0:rows, rows:size] = lower.T
    for p, part in enumerate(thirds(gram[...])):
        split[p] = part

    row = lax.broadcasted_iota(jnp.int32, (BLOCK, BLOCK), 0)
    column = lax.broadcasted_iota(jnp.int32, (BLOCK, BLOCK), 1)
    factor_ref[0:rows, rows:size] = jnp.zeros((rows, rows), jnp.float32)
    outgoing = []

    def leave(source, target, semaphore):
        copy = pltpu.make_async_copy(source, target, semaphore)
        copy.start()
        outgoing.append(copy)

    def basis_chain():
        basis = start_ref[...]
        for _ in range(POWER):
            image = thirds(six_terms([split[p] for p in range(3)], thirds(basis), NN))
            load_augmented(aug_b, self_product(image))
            yield
            for j in range(rank // PANEL):
                eliminate_panel(aug_b, j)
                yield
            basis = six_terms(image, thirds(aug_b[1]), NT)
            yield
        basis_ref[...] = basis
        leave(basis_ref, basis_out, out_sem.at[3])
        for load in loads[1:]:
            load.wait()
        high, low = halves(basis)
        both = jnp.concatenate([high, low], axis=1)
        piece = min(CHUNK, width)
        for n, start in enumerate(range(0, width, piece)):
            part = slice(start, start + piece)
            product = contract(both, flat_high[:, part], TN)
            core[:, part] = product[0:rank] + (product[rank:] + contract(high, flat_low[:, part], TN))
            leave(core.at[:, part], core_ref.at[:, 0, part], core_sem.at[n])
            yield

    def factor_chain():
        left = six_terms([split[p, rows:size, 0:rows] for p in range(3)], thirds(inverse_ref[...]), NT)
        factor_ref[rows:size, 0:rows] = left
        leave(factor_ref.at[rows:size, 0:rows], factor_out.at[rows:size, 0:rows], out_sem.at[0])
        yield
        parts = thirds(left)
        work[...] = gram[rows:size, rows:size] - six_terms(parts, parts, NT)
        yield
        for step in range(per):
            at, below = step * BLOCK, (step + 1) * BLOCK
            block = aug_f if below < rows else aug_last
            load_augmented(block, work[at:below, at:below])
            for j in range(BLOCK // PANEL):
                eliminate_panel(block, j)
                yield
            upper = jnp.where(row <= column, block[0], 0.0)
            factor_ref[rows + at : rows + below, rows + at : rows + below] = upper.T
            if step > 0:
                factor_ref[rows : rows + at, rows + at : rows + below] = jnp.zeros((at, BLOCK), jnp.float32)
            if below < rows:
                left = six_terms(thirds(work[below:rows, at:below]), thirds(aug_f[1]), NT)
                factor_ref[rows + below : size, rows + at : rows + below] = left
                parts = thirds(left)
                work[below:rows, below:rows] = work[below:rows, below:rows] - six_terms(parts, parts, NT)
            yield
        loads[0].wait()
        leave(factor_ref.at[0:rows, :], factor_out.at[0:rows, :], out_sem.at[1])
        leave(factor_ref.at[rows:size, rows:size], factor_out.at[rows:size, rows:size], out_sem.at[2])

    for _ in itertools.zip_longest(basis_chain(), factor_chain()):
        pass
    for copy in outgoing:
        copy.wait()


def fast_linear(columns, early, late, lead, inverse, start_basis, high, low):
    size, rank = start_basis.shape
    rows, width = size // 2, high.shape[1]
    vmem = pl.BlockSpec(memory_space=pltpu.VMEM)
    anywhere = pl.BlockSpec(memory_space=pl.ANY)
    return pl.pallas_call(
        functools.partial(fast_linear_kernel, lax.axis_size("col"), columns),
        out_shape=(
            jax.ShapeDtypeStruct((size, size), jnp.float32),
            jax.ShapeDtypeStruct((size, rank), jnp.float32),
            jax.ShapeDtypeStruct((rank, 1, width), jnp.float32),
        ),
        in_specs=[vmem, vmem, anywhere, vmem, vmem, anywhere, anywhere],
        out_specs=(anywhere, anywhere, anywhere),
        scratch_shapes=[
            pltpu.VMEM((size, size), jnp.float32),
            pltpu.VMEM((size, rank), jnp.float32),
            pltpu.VMEM((size, size), jnp.float32),
            pltpu.VMEM((3, size, size), jnp.bfloat16),
            pltpu.VMEM((rows, rows), jnp.float32),
            pltpu.VMEM((2, BLOCK, BLOCK), jnp.float32),
            pltpu.VMEM((1, BLOCK, BLOCK), jnp.float32),
            pltpu.VMEM((2, rank, rank), jnp.float32),
            pltpu.VMEM((size, width), jnp.bfloat16),
            pltpu.VMEM((size, width), jnp.bfloat16),
            pltpu.VMEM((rank, width), jnp.float32),
            pltpu.SemaphoreType.DMA((3,)),
            pltpu.SemaphoreType.DMA((4,)),
            pltpu.SemaphoreType.DMA((width // min(CHUNK, width),)),
        ],
        name="fast_linear",
    )(early, late, lead, inverse, start_basis, high, low)


def per_device(tensor, start_basis):
    modes, cols = lax.axis_size("mode"), lax.axis_size("col")
    depth = tensor.shape[1]
    columns = depth * tensor.shape[2] * cols
    if fast_case(modes, cols, tensor.shape):
        high, low, early, lead, inverse, late = fast_gather(tensor, columns)
        return fast_linear(columns, early, late, lead, inverse, start_basis, high, low)
    flat, packed = gather(tensor)
    return linear(columns, depth, packed, start_basis, flat)


def solution(mesh):
    in_specs = (P("mode", "col", None), P())
    out_specs = (P(), P(), P(None, "col", "mode"))
    return jax.shard_map(
        per_device, mesh=mesh, in_specs=in_specs, out_specs=out_specs, check_vma=False
    )
```

```python
import functools
import itertools

import jax
import jax.numpy as jnp
from jax import lax
from jax.experimental import pallas as pl
from jax.experimental.pallas import tpu as pltpu
from jax.sharding import PartitionSpec as P

POWER = 2
BLOCK = 128
PANEL = 8
CHUNK = 512
MESH = pl.DeviceIdType.MESH


def halves(value):
    high = value.astype(jnp.bfloat16)
    low = (value - high.astype(jnp.float32)).astype(jnp.bfloat16)
    return high, low


def contract(left, right, dims):
    return lax.dot_general(left, right, (dims, ((), ())), preferred_element_type=jnp.float32)


def exact(left, right, dims):
    return lax.dot_general(
        left, right, (dims, ((), ())), precision=lax.Precision.HIGHEST,
        preferred_element_type=jnp.float32,
    )


NN = ((1,), (0,))
NT = ((1,), (1,))
TN = ((0,), (0,))


def thirds(value):
    high = value.astype(jnp.bfloat16)
    rest = value - high.astype(jnp.float32)
    middle = rest.astype(jnp.bfloat16)
    low = (rest - middle.astype(jnp.float32)).astype(jnp.bfloat16)
    return high, middle, low


def six_terms(left, right, dims):
    high, middle, low = right
    beside, along = (1, 0) if dims == NN else (0, 1)
    wide = jnp.concatenate([high, middle], axis=beside)
    first = contract(
        jnp.concatenate([left[0], left[1]], axis=1), jnp.concatenate([wide, wide], axis=along), dims
    )
    second = contract(
        jnp.concatenate([left[2], left[0]], axis=1), jnp.concatenate([high, low], axis=along), dims
    )
    count = second.shape[1]
    return first[:, 0:count] + (first[:, count:] + second)


def self_product(parts):
    high, middle, low = parts
    pair = jnp.concatenate([high, middle], axis=1)
    product = contract(pair, pair, TN)
    small = contract(high, low, TN)
    count = small.shape[0]
    rest = (product[0:count, count:] + product[count:, 0:count]) + (product[count:, count:] + (small + small.T))
    return product[0:count, 0:count] + rest


def split3(value):
    high = value.astype(jnp.bfloat16).astype(jnp.float32)
    rest = value - high
    middle = rest.astype(jnp.bfloat16).astype(jnp.float32)
    return high, middle, rest - middle


def spread(tile, lane):
    return jnp.broadcast_to(tile[:, lane : lane + 1], tile.shape)


def eliminate_panel(aug, j):
    parts, size, _ = aug.shape
    first = PANEL * j
    after = first + PANEL
    below = after + PANEL
    rows = [[aug[p, pl.ds(first + t, PANEL, stride=0), :] for p in range(parts)] for t in range(PANEL)]
    entry = {}
    for s in range(PANEL):
        for t in range(s + 1):
            entry[s, t] = spread(rows[t][0], first + s)
    if after < size:
        following = [aug[p, after:below, :] for p in range(parts)]
        column = [spread(following[0], first + t) for t in range(PANEL)]
    for t in range(PANEL):
        inverse = 1.0 / entry[t, t]
        for s in range(t + 1, PANEL):
            ratio = entry[s, t] * inverse
            for u in range(s, PANEL):
                entry[u, s] = entry[u, s] - ratio * entry[u, t]
            rows[s] = [a - ratio * b for a, b in zip(rows[s], rows[t])]
        scale = lax.rsqrt(entry[t, t])
        for p in range(parts):
            aug[p, first + t : first + t + 1, :] = (rows[t][p] * scale)[0:1]
        if after < size:
            ratio = column[t] * inverse
            for u in range(t + 1, PANEL):
                column[u] = column[u] - ratio * entry[u, t]
            following = [a - ratio * b for a, b in zip(following, rows[t])]
    if after < size:
        for p in range(parts):
            aug[p, after:below, :] = following[p]
    if below < size:
        rights = []
        for p in range(parts):
            high, middle, low = split3(aug[p, first:after, :])
            if p == 0:
                left = jnp.concatenate([high, high, middle, high, low, middle], axis=0).astype(jnp.bfloat16)
            rights.append(jnp.concatenate([high, middle, high, low, high, middle], axis=0).astype(jnp.bfloat16))
        update = contract(left, jnp.concatenate(rights, axis=1), TN)
        for p in range(parts):
            aug[p, below:size, :] = aug[p, below:size, :] - update[below:size, p * size : (p + 1) * size]


def eliminate(augs):
    for j in range(BLOCK // PANEL):
        for aug in augs:
            eliminate_panel(aug, j)


def load_augmented(aug, matrix):
    size = matrix.shape[0]
    aug[0] = matrix
    if aug.shape[0] > 1:
        row = lax.broadcasted_iota(jnp.int32, (size, size), 0)
        column = lax.broadcasted_iota(jnp.int32, (size, size), 1)
        aug[1] = jnp.where(row == column, 1.0, 0.0).astype(jnp.float32)


def lower_blocks(blocks):
    return [(i, k) for i in range(blocks) for k in range(i + 1)]


def stages_of(modes, cols):
    stages, stride = [], 1
    first = 2 if cols % 2 == 0 else 1
    if first > 1:
        stages.append((1, first, False))
        stride = first
    second = 2 if (cols // stride) % 2 == 0 else 1
    stages.append((stride, second, True))
    stride *= second
    if cols // stride > 1:
        stages.append((stride, cols // stride, False))
    return stages


def round_up(value, unit):
    return -(-value // unit) * unit


def layout_of(size, modes, cols):
    pairs = lower_blocks(size // BLOCK)
    rows = size // modes
    inner = []
    if rows % BLOCK == 0 and modes > 1:
        inner = lower_blocks(rows // BLOCK)
    per = rows // BLOCK
    extent = round_up(len(inner) * BLOCK, 8 * cols)
    where = {}
    for m in range(modes):
        for n, (i, k) in enumerate(inner):
            where[m * per + i, m * per + k] = m * extent + n * BLOCK
    outer = [pair for pair in pairs if pair not in where]
    for n, pair in enumerate(outer):
        where[pair] = modes * extent + n * BLOCK
    return where, inner, extent, outer, round_up(len(outer) * BLOCK, 8 * modes * cols)


def members_of(stages, modes):
    return [count * (modes if with_mode else 1) for _, count, with_mode in stages]


def gather_kernel(modes, cols, x_ref, flat_ref, total_ref, local, acc_in, acc_out, main, cross, *rest):
    mode, col = lax.axis_index("mode"), lax.axis_index("col")
    all_stages = stages_of(modes, cols)
    col_stages = [(stride, count, False) for stride, count, _ in all_stages]
    n = len(all_stages)
    slots_in, slots_out = rest[:n], rest[n : 2 * n]
    local_sem, piece_send, piece_recv, swap_send, swap_recv, in_sems, out_sems, share_in, share_out = rest[2 * n :]
    rows, depth, length = x_ref.shape
    size = rows * modes
    width = length // modes
    chunk = min(CHUNK, width)
    per = width // chunk
    chunks = depth * per
    where, inner, in_extent, outer, out_extent = layout_of(size, modes, cols)

    def position(stage):
        stride, count, with_mode = stage
        place = lax.rem(lax.div(col, stride), count)
        return place * modes + mode if with_mode else place

    def members(stage):
        return stage[1] * (modes if stage[2] else 1)

    def peer(stage, offset):
        stride, count, with_mode = stage
        other = lax.rem(position(stage) + offset, members(stage))
        place = lax.div(other, modes) if with_mode else other
        there = col + (place - lax.rem(lax.div(col, stride), count)) * stride
        return other, (lax.rem(other, modes) if with_mode else mode, there)

    partners = [(lax.rem(mode + d, modes), col) for d in range(1, modes)]
    greeted = []
    for stage in all_stages:
        greeted += [peer(stage, d)[1] for d in range(1, members(stage))]
    barrier = pltpu.get_barrier_semaphore()
    for device in greeted:
        pl.semaphore_signal(barrier, inc=1, device_id=device, device_id_type=MESH)
    pl.semaphore_wait(barrier, len(greeted))

    own_rows = pl.ds(pl.multiple_of(mode * rows, rows), rows)

    def spans(c):
        layer, part = lax.div(c, per), lax.rem(c, per)
        return layer, part * chunk, pl.multiple_of(layer * width + part * chunk, chunk)

    def piece(c, d):
        layer, start, target = spans(c)
        source = pl.multiple_of(lax.rem(mode + d, modes) * width + start, chunk)
        return pltpu.make_async_remote_copy(
            src_ref=x_ref.at[:, layer, pl.ds(source, chunk)],
            dst_ref=flat_ref.at[own_rows, pl.ds(target, chunk)],
            send_sem=piece_send.at[d - 1, c],
            recv_sem=piece_recv.at[d - 1, c],
            device_id=partners[d - 1],
            device_id_type=MESH,
        )

    def load(c):
        layer, part = lax.div(c, per * modes), lax.rem(c, per * modes)
        source = pl.multiple_of(part * chunk, chunk)
        target = pl.multiple_of(layer * length + part * chunk, chunk)
        return pltpu.make_async_copy(
            x_ref.at[:, layer, pl.ds(source, chunk)], local.at[:, pl.ds(target, chunk)], local_sem.at[c]
        ), target

    def begin(c, carry):
        for d in range(1, modes):
            piece(c, d).start()
        return carry

    def begin_load(c, carry):
        load(c)[0].start()
        return carry

    early = max(chunks // 2, 1)
    lax.fori_loop(0, early, begin, 0)
    lax.fori_loop(0, chunks * modes, begin_load, 0)

    main[...] = jnp.zeros_like(main)
    cross[...] = jnp.zeros_like(cross)

    def accumulate_in(c, carry):
        copy, target = load(c)
        copy.wait()
        if inner:
            high, low = halves(local[:, pl.ds(target, chunk)])
            main[0:rows, 0:rows] += contract(high, high, NT)
            cross[0:rows, 0:rows] += contract(high, low, NT)
        return carry

    lax.fori_loop(0, chunks * modes, accumulate_in, 0)
    for layer in range(depth):
        source = pl.multiple_of(layer * length + mode * width, chunk)
        flat_ref[own_rows, layer * width : (layer + 1) * width] = local[:, pl.ds(source, width)]

    def pack(acc, pairs, extent):
        for at, (i, k) in enumerate(pairs):
            tall, wide = slice(i * BLOCK, (i + 1) * BLOCK), slice(k * BLOCK, (k + 1) * BLOCK)
            acc[at * BLOCK : (at + 1) * BLOCK, :] = main[tall, wide] + (cross[tall, wide] + cross[wide, tall].T)
        used = len(pairs) * BLOCK
        if used < extent:
            acc[used:, :] = jnp.zeros((extent - used, BLOCK), jnp.float32)

    def scatter_sum(stages, acc, extent, slots, sems, target):
        base, bases = 0, []
        for g, stage in enumerate(stages):
            count = members(stage)
            part = extent // count
            copies = []
            for d in range(1, count):
                other, device = peer(stage, d)
                copy = pltpu.make_async_remote_copy(
                    src_ref=acc.at[pl.ds(pl.multiple_of(base + other * part, 8), part), :],
                    dst_ref=slots[g].at[d - 1],
                    send_sem=sems.at[0, g, d - 1],
                    recv_sem=sems.at[1, g, d - 1],
                    device_id=device,
                    device_id_type=MESH,
                )
                copy.start()
                copies.append(copy)
            base = base + position(stage) * part
            extent = part
            bases.append((base, part))
            for copy in copies:
                copy.wait()
            mine = pl.ds(pl.multiple_of(base, 8), part)
            added = acc[mine, :]
            for d in range(1, count):
                added = added + slots[g][d - 1]
            if g < len(stages) - 1:
                acc[mine, :] = added
            else:
                total_ref[pl.ds(pl.multiple_of(target + base, 8), part), :] = added
        return bases

    def share(stages, bases, targets, sems):
        for g in reversed(range(len(stages))):
            stage = stages[g]
            base, part = bases[g]
            copies = []
            for d in range(1, members(stage)):
                for t, target in enumerate(targets):
                    mine = pl.ds(pl.multiple_of(target + base, 8), part)
                    copy = pltpu.make_async_remote_copy(
                        src_ref=total_ref.at[mine, :],
                        dst_ref=total_ref.at[mine, :],
                        send_sem=sems.at[0, g, (d - 1) * len(targets) + t],
                        recv_sem=sems.at[1, g, (d - 1) * len(targets) + t],
                        device_id=peer(stage, d)[1],
                        device_id_type=MESH,
                    )
                    copy.start()
                    copies.append(copy)
            for copy in copies:
                copy.wait()

    def accumulate_out(c, carry):
        for d in range(1, modes):
            piece(c, d).wait_recv()
        high, low = halves(flat_ref[:, pl.ds(spans(c)[2], chunk)])
        if inner:
            for m in range(1, modes):
                tall, wide = slice(m * rows, (m + 1) * rows), slice(0, m * rows)
                main[tall, wide] += contract(high[tall, :], high[wide, :], NT) + contract(low[tall, :], high[wide, :], NT)
                cross[tall, wide] += contract(high[tall, :], low[wide, :], NT)
        else:
            main[...] += contract(high, high, NT)
            cross[...] += contract(high, low, NT)
        return carry

    swaps = []
    if inner:
        pack(acc_in, inner, in_extent)
        main[...] = jnp.zeros_like(main)
        cross[...] = jnp.zeros_like(cross)
        bases = scatter_sum(col_stages, acc_in, in_extent, slots_in, in_sems, mode * in_extent)
        base, part = bases[-1]
        mine = pl.ds(pl.multiple_of(mode * in_extent + base, 8), part)
        for d in range(1, modes):
            swap = pltpu.make_async_remote_copy(
                src_ref=total_ref.at[mine, :],
                dst_ref=total_ref.at[mine, :],
                send_sem=swap_send.at[d - 1],
                recv_sem=swap_recv.at[d - 1],
                device_id=partners[d - 1],
                device_id_type=MESH,
            )
            swap.start()
            swaps.append(swap)
    lax.fori_loop(early, chunks, begin, 0)
    lax.fori_loop(0, early, accumulate_out, 0)
    if inner:
        for swap in swaps:
            swap.wait()
        share(col_stages, bases, [m * in_extent for m in range(modes)], share_in)
    lax.fori_loop(early, chunks, accumulate_out, 0)

    pack(acc_out, outer, out_extent)
    bases = scatter_sum(all_stages, acc_out, out_extent, slots_out, out_sems, modes * in_extent)
    share(all_stages, bases, [modes * in_extent], share_out)

    def end(c, carry):
        for d in range(1, modes):
            piece(c, d).wait_send()
        return carry

    lax.fori_loop(0, chunks, end, 0)


def gather(tensor):
    modes, cols = lax.axis_size("mode"), lax.axis_size("col")
    rows, depth, length = tensor.shape
    size = rows * modes
    width = length // modes
    chunks = depth * (width // min(CHUNK, width))
    stages = stages_of(modes, cols)
    _, inner, in_extent, _, out_extent = layout_of(size, modes, cols)
    in_extent = max(in_extent, 8 * cols)
    slots_in, slots_out, extent_in, extent, most = [], [], in_extent, out_extent, 1
    for stride, count, with_mode in stages:
        extent_in = extent_in // count
        slots_in.append(pltpu.VMEM((max(count - 1, 1), extent_in, BLOCK), jnp.float32))
        count = count * (modes if with_mode else 1)
        extent = extent // count
        slots_out.append(pltpu.VMEM((max(count - 1, 1), extent, BLOCK), jnp.float32))
        most = max(most, count - 1)
    dma = pltpu.SemaphoreType.DMA
    vmem = pl.BlockSpec(memory_space=pltpu.VMEM)
    packed = (modes * in_extent if inner else 0) + out_extent
    return pl.pallas_call(
        functools.partial(gather_kernel, modes, cols),
        out_shape=(
            jax.ShapeDtypeStruct((size, depth * width), jnp.float32),
            jax.ShapeDtypeStruct((packed, BLOCK), jnp.float32),
        ),
        in_specs=[pl.BlockSpec(memory_space=pl.ANY)],
        out_specs=(vmem, vmem),
        scratch_shapes=[
            pltpu.VMEM((rows, depth * length), jnp.float32),
            pltpu.VMEM((in_extent, BLOCK), jnp.float32),
            pltpu.VMEM((out_extent, BLOCK), jnp.float32),
            pltpu.VMEM((size, size), jnp.float32),
            pltpu.VMEM((size, size), jnp.float32),
            *slots_in,
            *slots_out,
            dma((chunks * modes,)),
            *[dma((max(modes - 1, 1), chunks))] * 2,
            *[dma((max(modes - 1, 1),))] * 2,
            *[dma((2, len(stages), most))] * 2,
            dma((2, len(stages), most * modes)),
            dma((2, len(stages), most)),
        ],
        compiler_params=pltpu.CompilerParams(collective_id=0, has_side_effects=True),
        name="gather",
    )(tensor)


def linear_kernel(columns, where, packed_ref, start_ref, flat_ref, factor_ref, basis_ref, core_ref, gram, work, image, aug_f, aug_b, core, core_sem):
    size, rank = start_ref.shape
    blocks = size // BLOCK
    row = lax.broadcasted_iota(jnp.int32, (BLOCK, BLOCK), 0)
    column = lax.broadcasted_iota(jnp.int32, (BLOCK, BLOCK), 1)
    scale = 1.0 / columns
    for (i, k), at in where.items():
        scaled = packed_ref[at : at + BLOCK, :] * scale
        gram[i * BLOCK : (i + 1) * BLOCK, k * BLOCK : (k + 1) * BLOCK] = scaled
        work[i * BLOCK : (i + 1) * BLOCK, k * BLOCK : (k + 1) * BLOCK] = scaled
        if i != k:
            gram[k * BLOCK : (k + 1) * BLOCK, i * BLOCK : (i + 1) * BLOCK] = scaled.T

    for step in range(max(blocks, POWER)):
        augs = []
        if step < blocks:
            at = step * BLOCK
            load_augmented(aug_f, work[at : at + BLOCK, at : at + BLOCK])
            augs.append(aug_f)
        if step < POWER:
            source = start_ref if step == 0 else basis_ref
            image[...] = exact(gram[...], source[...], NN)
            load_augmented(aug_b, exact(image[...], image[...], TN))
            augs.append(aug_b)
        eliminate(augs)
        if step < POWER:
            basis_ref[...] = exact(image[...], aug_b[1], NT)
        if step < blocks:
            upper = jnp.where(row <= column, aug_f[0], 0.0)
            factor_ref[at : at + BLOCK, at : at + BLOCK] = upper.T
            if step > 0:
                factor_ref[0:at, at : at + BLOCK] = jnp.zeros((at, BLOCK), jnp.float32)
            below = at + BLOCK
            if below < size:
                inverse = aug_f[1]
                left = exact(work[below:size, at : at + BLOCK], inverse, NT)
                factor_ref[below:size, at : at + BLOCK] = left
                work[below:size, below:size] = work[below:size, below:size] - exact(left, left, NT)

    high, low = halves(basis_ref[...])
    depth, length = core_ref.shape[1:]
    width = min(CHUNK, length)
    copies = []
    for start in range(0, depth * length, width):
        part = slice(start, start + width)
        flat_high, flat_low = halves(flat_ref[:, part])
        core[:, part] = contract(high, flat_high, TN) + contract(high, flat_low, TN) + contract(low, flat_high, TN)
        layer, offset = divmod(start, length)
        copy = pltpu.make_async_copy(
            core.at[:, part], core_ref.at[:, layer, offset : offset + width], core_sem.at[len(copies)]
        )
        copy.start()
        copies.append(copy)
    for copy in copies:
        copy.wait()


def linear(columns, depth, packed, start_basis, flat):
    size, rank = start_basis.shape
    length = flat.shape[1] // depth
    where = layout_of(size, lax.axis_size("mode"), lax.axis_size("col"))[0]
    vmem = pl.BlockSpec(memory_space=pltpu.VMEM)
    return pl.pallas_call(
        functools.partial(linear_kernel, columns, where),
        out_shape=(
            jax.ShapeDtypeStruct((size, size), jnp.float32),
            jax.ShapeDtypeStruct((size, rank), jnp.float32),
            jax.ShapeDtypeStruct((rank, depth, length), jnp.float32),
        ),
        in_specs=[vmem] * 3,
        out_specs=(vmem, vmem, pl.BlockSpec(memory_space=pl.ANY)),
        scratch_shapes=[
            pltpu.VMEM((size, size), jnp.float32),
            pltpu.VMEM((size, size), jnp.float32),
            pltpu.VMEM((size, rank), jnp.float32),
            pltpu.VMEM((2, BLOCK, BLOCK), jnp.float32),
            pltpu.VMEM((2, rank, rank), jnp.float32),
            pltpu.VMEM((rank, flat.shape[1]), jnp.float32),
            pltpu.SemaphoreType.DMA((flat.shape[1] // min(CHUNK, length),)),
        ],
        name="linear",
    )(packed, start_basis, flat)


def fast_case(modes, cols, shape):
    rows, depth, length = shape
    return modes == 2 and depth == 1 and rows % (2 * BLOCK) == 0 and cols % 4 == 0 and length % (2 * BLOCK) == 0


STRIPS = 8
LATE = 4
EARLY = 3
HELD = 3
PIECES = STRIPS + 3


def fast_cuts(strip):
    return sorted([k * strip for k in range(STRIPS + 1)] + [2 * strip + strip // 2, 6 * strip + strip // 2])


def fast_layout(rows, cols):
    per = rows // BLOCK
    strip = rows // STRIPS
    first = rows - LATE * strip
    inner = lower_blocks(per)
    unit = 8 * cols
    extents = [round_up(len(inner) * BLOCK, unit), round_up(first * per, unit), round_up((rows - first) * per, unit)]
    starts, at = [], 0
    for extent in extents:
        starts.append(at)
        at += 2 * extent
    return per, strip, first, inner, extents, starts, at


def fast_gather_kernel(cols, columns, x_ref, high_out, low_out, early_out, lead_out, inverse_out, late_ref, local, recv, early_ref, lead_ref, inverse_ref, own_high, own_low, other_high, other_low, main, cross, work, aug, acc_in, acc_a, acc_b, *rest):
    slots, sems, hello = rest[:-2], rest[-2], rest[-1]
    mode, col = lax.axis_index("mode"), lax.axis_index("col")
    other_mode = 1 - mode
    rows, _, length = x_ref.shape
    width = length // 2
    chips = cols // 2
    per, strip, first, inner, extents, starts, _ = fast_layout(rows, cols)
    core, chip = lax.rem(col, 2), lax.div(col, 2)
    names = {}
    pending = {}

    def sem(*name):
        return sems.at[names.setdefault(name, len(names))]

    def drain(*kinds):
        for name in [name for name in pending if name[0] in kinds]:
            pending.pop(name).wait_send()

    def push(source, target, device, *name):
        if name in pending:
            pending.pop(name).wait_send()
        copy = pltpu.make_async_remote_copy(
            src_ref=source, dst_ref=target, send_sem=sem("send", *name), recv_sem=sem("recv", *name),
            device_id=device, device_id_type=MESH,
        )
        copy.start()
        pending[name] = copy
        return copy

    def volley(name, triples, whole):
        if (name,) in pending:
            pending.pop((name,)).wait_send()

        def copy_of(source, target, device):
            return pltpu.make_async_remote_copy(
                src_ref=source, dst_ref=target, send_sem=sem("send", name), recv_sem=sem("recv", name),
                device_id=device, device_id_type=MESH,
            )

        for triple in triples:
            copy_of(*triple).start()
        pending[(name,)] = copy_of(whole, whole, sibling)
        return [pending[(name,)]]

    sibling = (mode, chip * 2 + 1 - core)
    partner = (other_mode, col)
    plane = []
    for d in range(1, chips):
        place = lax.rem(chip + d, chips)
        plane.append((place, (mode, place * 2 + core)))

    line = chips // 2
    place = lax.div(chip, 2)
    beside = (mode, (place * 2 + 1 - lax.rem(chip, 2)) * 2 + core)
    above, under = (mode, col + 4), (mode, col - 4)
    has_above, has_under = place < line - 1, place > 0

    def hail(semaphore, device):
        pl.semaphore_signal(semaphore, inc=1, device_id=device, device_id_type=MESH)

    barrier = pltpu.get_barrier_semaphore()
    for device in (partner, sibling, beside):
        hail(barrier, device)
    pl.when(has_above)(lambda: hail(barrier, above))
    pl.when(has_under)(lambda: hail(barrier, under))
    pl.semaphore_wait(barrier, 3 + has_above.astype(jnp.int32) + has_under.astype(jnp.int32))

    def meet_line():
        pl.when(has_under)(lambda: pl.semaphore_wait(hello.at[0], 1))
        pl.when(has_above)(lambda: hail(hello.at[0], above))
        pl.when(has_above)(lambda: pl.semaphore_wait(hello.at[1], 1))
        pl.when(has_under)(lambda: hail(hello.at[1], under))
        hail(hello.at[2], beside)

    def meet_beside():
        pl.semaphore_wait(hello.at[2], 1)
        hail(hello.at[3], partner)

    def meet_across():
        pl.semaphore_wait(hello.at[3], 1)

    pieces = []
    away = pl.ds(pl.multiple_of(other_mode * width, width), width)

    cuts = fast_cuts(strip)

    def piece_of(source, target, k):
        return pltpu.make_async_remote_copy(
            src_ref=source, dst_ref=target, send_sem=sem("pieces"), recv_sem=sem("piece", k),
            device_id=partner, device_id_type=MESH,
        )

    def send_piece(k):
        if k < PIECES - 2:
            span, start, count = slice(cuts[k], cuts[k + 1]), 0, width
        else:
            span, start, count = slice(rows - strip, rows), (k - PIECES + 2) * (width // 2), width // 2
        source = pl.ds(pl.multiple_of(other_mode * width + start, BLOCK), count)
        pieces.append(piece_of(x_ref.at[span, 0, source], recv.at[span, start : start + count], k))
        pieces[k].start()

    for k in range(EARLY):
        send_piece(k)

    loads = []
    part = length // 4
    for c in range(4):
        span = slice(c * part, (c + 1) * part)
        copy = pltpu.make_async_copy(x_ref.at[:, 0, span], local.at[:, span], sem("local", c))
        copy.start()
        loads.append(copy)
    for c in range(4):
        if c == 1:
            meet_line()
        loads[c].wait()
        high, low = halves(local[:, c * part : (c + 1) * part])
        if c == 0:
            main[...] = contract(high, high, NT)
            cross[...] = contract(high, low, NT)
        else:
            main[...] += contract(high, high, NT)
            cross[...] += contract(high, low, NT)

    for at, (i, k) in enumerate(inner):
        tall, wide = slice(i * BLOCK, (i + 1) * BLOCK), slice(k * BLOCK, (k + 1) * BLOCK)
        acc_in[at * BLOCK : (at + 1) * BLOCK, :] = main[tall, wide] + (cross[tall, wide] + cross[wide, tall].T)

    def fill(acc, used):
        if used < acc.shape[0]:
            acc[used:, :] = jnp.zeros((acc.shape[0] - used, BLOCK), jnp.float32)

    def rows_at(base, count):
        return pl.ds(pl.multiple_of(base, 8), count)

    def core_send(acc, slot):
        half = acc.shape[0] // 2
        return push(acc.at[rows_at((1 - core) * half, half), :], slot.at[...], sibling, "core")

    def core_add(acc, slot, copy):
        half = acc.shape[0] // 2
        copy.wait_recv()
        mine = rows_at(core * half, half)
        acc[mine, :] = acc[mine, :] + slot[...]

    def plane_send(acc, slot):
        half = acc.shape[0] // 2
        share = half // chips
        triples = []
        for d, (place, device) in enumerate(plane):
            triples.append((acc.at[rows_at(core * half + place * share, share), :], slot.at[d], device))
        return volley("plane", triples, slot)

    def plane_add(acc, slot, copies, total, start):
        half = acc.shape[0] // 2
        share = half // chips
        base = core * half + chip * share
        for copy in copies:
            copy.wait_recv()
        added = acc[rows_at(base, share), :]
        for d in range(chips - 1):
            added = added + slot[d]
        total[rows_at(start + mode * acc.shape[0] + base, share), :] = added

    def swap(acc, total, start, phase):
        half = acc.shape[0] // 2
        share = half // chips
        mine = rows_at(start + mode * acc.shape[0] + core * half + chip * share, share)
        return push(total.at[mine, :], total.at[mine, :], partner, "swap", phase)

    def plane_share(acc, total, start):
        half = acc.shape[0] // 2
        share = half // chips
        triples = []
        for _, device in plane:
            for m in range(2):
                mine = rows_at(start + m * acc.shape[0] + core * half + chip * share, share)
                triples.append((total.at[mine, :], total.at[mine, :], device))
        return volley("share", triples, total.at[0 : len(triples) * share, :])

    def direct_share(acc, total, start):
        half = acc.shape[0] // 2
        share = half // chips
        mine = rows_at(start + mode * acc.shape[0] + core * half + chip * share, share)
        devices = [(other_mode, lax.rem(chip + d, chips) * 2 + core) for d in range(chips)]
        devices += [device for _, device in plane]
        triples = [(total.at[mine, :], total.at[mine, :], device) for device in devices]
        return volley("direct", triples, total.at[0 : len(triples) * share, :])

    def core_share(acc, total, start):
        half = acc.shape[0] // 2
        triples = []
        for m in range(2):
            mine = rows_at(start + m * acc.shape[0] + core * half, half)
            triples.append((total.at[mine, :], total.at[mine, :], sibling))
        return volley("both", triples, total.at[0 : 2 * half, :])

    def arrive(copies):
        for copy in copies:
            copy.wait_recv()

    outgoing = {}
    leaving = [0]

    def leave(source, target):
        lane = leaving[0] % len(loads)
        leaving[0] += 1
        if lane in outgoing:
            outgoing.pop(lane).wait()
        copy = pltpu.make_async_copy(source, target, sem("local", lane))
        copy.start()
        outgoing[lane] = copy

    def strips(begin, end, acc, offset, tall):
        span = slice(begin * strip, end * strip)
        if end < STRIPS:
            steps = [(pieces[cuts.index(begin * strip) : cuts.index(end * strip)], 0, width)]
        else:
            steps = [([pieces[-2]], 0, width // 2), ([pieces[-1]], width // 2, width // 2)]
        count = (end - begin) * strip
        value = None
        for copies, start, wide in steps:
            arrive(copies)
            part = slice(start, start + wide)
            high, low = halves(recv[span, part])
            other_high[span, part] = high
            other_low[span, part] = low
            both = contract(own_high[:, part], jnp.concatenate([high, low], axis=0), NT)
            added = both[:, 0:count] + (both[:, count:] + contract(own_low[:, part], high, NT))
            value = added if value is None else value + added
        target = pl.ds(pl.multiple_of(other_mode * rows + begin * strip, strip), count)
        leave(other_high.at[span, :], high_out.at[target, :])
        leave(other_low.at[span, :], low_out.at[target, :])
        value = value.T
        for c in range(per):
            at = c * tall + begin * strip - offset
            acc[at : at + count, :] = value[:, c * BLOCK : (c + 1) * BLOCK]

    fill(acc_in, len(inner) * BLOCK)
    meet_beside()
    copy = core_send(acc_in, slots[0])
    mine = local[:, pl.ds(pl.multiple_of(mode * width, width), width)]
    high, low = halves(mine)
    own_high[...] = high
    own_low[...] = low
    core_add(acc_in, slots[0], copy)
    copies = plane_send(acc_in, slots[1])
    target = pl.ds(pl.multiple_of(mode * rows, rows), rows)
    leave(own_high, high_out.at[target, :])
    leave(own_low, low_out.at[target, :])
    plane_add(acc_in, slots[1], copies, early_ref, starts[0])
    meet_across()
    copy = swap(acc_in, early_ref, starts[0], 0)
    for k in range(EARLY, PIECES - HELD):
        send_piece(k)
    strips(0, 1, acc_a, 0, first)
    arrive([copy])
    copies = plane_share(acc_in, early_ref, starts[0])
    drain("core", "plane", "swap")
    strips(1, 2, acc_a, 0, first)
    arrive(copies)
    arrive(core_share(acc_in, early_ref, starts[0]))

    scale = 1.0 / columns
    for at, (i, k) in enumerate(inner):
        tall, wide = slice(i * BLOCK, (i + 1) * BLOCK), slice(k * BLOCK, (k + 1) * BLOCK)
        work[tall, wide] = early_ref[starts[0] + at * BLOCK : starts[0] + (at + 1) * BLOCK, :] * scale
    lead_ref[...] = jnp.zeros_like(lead_ref)
    inverse_ref[...] = jnp.zeros_like(inverse_ref)
    row = lax.broadcasted_iota(jnp.int32, (BLOCK, BLOCK), 0)
    column = lax.broadcasted_iota(jnp.int32, (BLOCK, BLOCK), 1)
    for step in range(per):
        at, below = step * BLOCK, (step + 1) * BLOCK
        load_augmented(aug, work[at:below, at:below])
        eliminate([aug])
        lead_ref[at:below, at:below] = jnp.where(row <= column, aug[0], 0.0).T
        inverse = aug[1]
        inverse_ref[at:below, at:below] = inverse
        if step > 0:
            inverse_ref[at:below, 0:at] = -exact(inverse, exact(lead_ref[at:below, 0:at], inverse_ref[0:at, 0:at], NN), NN)
        if below < rows:
            left = exact(work[below:rows, at:below], inverse, NT)
            lead_ref[below:rows, at:below] = left
            work[below:rows, below:rows] = work[below:rows, below:rows] - exact(left, left, NT)
        if step == 0:
            strips(2, STRIPS - LATE, acc_a, 0, first)
            fill(acc_a, first * per)
            core_add(acc_a, slots[2], core_send(acc_a, slots[2]))
            copies = plane_send(acc_a, slots[3])
    plane_add(acc_a, slots[3], copies, early_ref, starts[1])
    copy = swap(acc_a, early_ref, starts[1], 1)
    for k in range(PIECES - HELD, PIECES):
        send_piece(k)
    leave(lead_ref, lead_out)
    leave(inverse_ref, inverse_out)
    strips(STRIPS - LATE, STRIPS - 2, acc_b, first, rows - first)
    arrive([copy])
    copies = plane_share(acc_a, early_ref, starts[1])
    drain("core", "plane", "swap", "both")
    strips(STRIPS - 2, STRIPS - 1, acc_b, first, rows - first)
    arrive(copies)
    copies = core_share(acc_a, early_ref, starts[1])
    drain("share")
    arrive(copies)
    leave(early_ref, early_out)
    strips(STRIPS - 1, STRIPS, acc_b, first, rows - first)
    fill(acc_b, (rows - first) * per)
    core_add(acc_b, slots[4], core_send(acc_b, slots[4]))
    plane_add(acc_b, slots[5], plane_send(acc_b, slots[5]), late_ref, 0)
    copies = direct_share(acc_b, late_ref, 0)
    drain("core", "plane", "both")
    piece_of(x_ref.at[:, 0, away], recv, 0).wait_send()
    for copy in outgoing.values():
        copy.wait()
    arrive(copies)
    copies = core_share(acc_b, late_ref, 0)
    drain("direct")
    arrive(copies)
    drain("both")


def fast_gather(tensor, columns):
    cols = lax.axis_size("col")
    rows, _, length = tensor.shape
    width = length // 2
    chips = cols // 2
    _, _, _, _, extents, starts, _ = fast_layout(rows, cols)
    slots = []
    for extent in extents:
        slots.append(pltpu.VMEM((extent // 2, BLOCK), jnp.float32))
        slots.append(pltpu.VMEM((chips - 1, extent // cols, BLOCK), jnp.float32))
    vmem = pl.BlockSpec(memory_space=pltpu.VMEM)
    anywhere = pl.BlockSpec(memory_space=pl.ANY)
    return pl.pallas_call(
        functools.partial(fast_gather_kernel, cols, columns),
        out_shape=(
            jax.ShapeDtypeStruct((2 * rows, width), jnp.bfloat16),
            jax.ShapeDtypeStruct((2 * rows, width), jnp.bfloat16),
            jax.ShapeDtypeStruct((starts[2], BLOCK), jnp.float32),
            jax.ShapeDtypeStruct((rows, rows), jnp.float32),
            jax.ShapeDtypeStruct((rows, rows), jnp.float32),
            jax.ShapeDtypeStruct((2 * extents[2], BLOCK), jnp.float32),
        ),
        in_specs=[anywhere],
        out_specs=(anywhere, anywhere, anywhere, anywhere, anywhere, vmem),
        scratch_shapes=[
            pltpu.VMEM((rows, length), jnp.float32),
            pltpu.VMEM((rows, width), jnp.float32),
            pltpu.VMEM((starts[2], BLOCK), jnp.float32),
            pltpu.VMEM((rows, rows), jnp.float32),
            pltpu.VMEM((rows, rows), jnp.float32),
            *[pltpu.VMEM((rows, width), jnp.bfloat16)] * 4,
            pltpu.VMEM((rows, rows), jnp.float32),
            pltpu.VMEM((rows, rows), jnp.float32),
            pltpu.VMEM((rows, rows), jnp.float32),
            pltpu.VMEM((2, BLOCK, BLOCK), jnp.float32),
            *[pltpu.VMEM((extent, BLOCK), jnp.float32) for extent in extents],
            *slots,
            pltpu.SemaphoreType.DMA((PIECES + 19,)),
            pltpu.SemaphoreType.REGULAR((4,)),
        ],
        compiler_params=pltpu.CompilerParams(collective_id=0, has_side_effects=True),
        name="fast_gather",
    )(tensor)


def fast_linear_kernel(cols, columns, early_ref, late_ref, lead_ref, inverse_ref, start_ref, high_ref, low_ref, factor_out, basis_out, core_ref, factor_ref, basis_ref, gram, split, work, aug_b, flat_high, flat_low, core, flat_sem, out_sem, core_sem, *augs):
    size, rank = start_ref.shape
    rows = size // 2
    width = core_ref.shape[2]
    per, _, first, inner, extents, starts, _ = fast_layout(rows, cols)
    loads = [
        pltpu.make_async_copy(lead_ref, factor_ref.at[0:rows, 0:rows], flat_sem.at[0]),
        pltpu.make_async_copy(high_ref, flat_high, flat_sem.at[1]),
        pltpu.make_async_copy(low_ref, flat_low, flat_sem.at[2]),
    ]
    for load in loads:
        load.start()

    scale = 1.0 / columns
    for m in range(2):
        for at, (i, k) in enumerate(inner):
            begin = starts[0] + m * extents[0] + at * BLOCK
            block = early_ref[begin : begin + BLOCK, :] * scale
            tall = slice(m * rows + i * BLOCK, m * rows + (i + 1) * BLOCK)
            wide = slice(m * rows + k * BLOCK, m * rows + (k + 1) * BLOCK)
            gram[tall, wide] = block
            if i != k:
                gram[wide, tall] = block.T
    pair = []
    for m in range(2):
        blocks = []
        for c in range(per):
            a = starts[1] + m * extents[1] + c * first
            b = m * extents[2] + c * (rows - first)
            blocks.append(jnp.concatenate([early_ref[a : a + first, :], late_ref[b : b + rows - first, :]], axis=0))
        pair.append(jnp.concatenate(blocks, axis=1))
    lower = (pair[0] + pair[1].T) * scale
    gram[rows:size, 0:rows] = lower
    gram[0:rows, rows:size] = lower.T
    for p, part in enumerate(thirds(gram[...])):
        split[p] = part

    row = lax.broadcasted_iota(jnp.int32, (BLOCK, BLOCK), 0)
    column = lax.broadcasted_iota(jnp.int32, (BLOCK, BLOCK), 1)
    factor_ref[0:rows, rows:size] = jnp.zeros((rows, rows), jnp.float32)
    outgoing = []

    def leave(source, target, semaphore):
        copy = pltpu.make_async_copy(source, target, semaphore)
        copy.start()
        outgoing.append(copy)

    def basis_chain():
        basis = start_ref[...]
        for _ in range(POWER):
            image = thirds(six_terms([split[p] for p in range(3)], thirds(basis), NN))
            load_augmented(aug_b, self_product(image))
            yield
            for j in range(rank // PANEL):
                eliminate_panel(aug_b, j)
                yield
            basis = six_terms(image, thirds(aug_b[1]), NT)
            yield
        basis_ref[...] = basis
        leave(basis_ref, basis_out, out_sem.at[3])
        for load in loads[1:]:
            load.wait()
        high, low = halves(basis)
        both = jnp.concatenate([high, low], axis=1)
        piece = min(CHUNK, width)
        for n, start in enumerate(range(0, width, piece)):
            part = slice(start, start + piece)
            product = contract(both, flat_high[:, part], TN)
            core[:, part] = product[0:rank] + (product[rank:] + contract(high, flat_low[:, part], TN))
            leave(core.at[:, part], core_ref.at[:, 0, part], core_sem.at[n])
            yield

    def factor_chain():
        left = six_terms([split[p, rows:size, 0:rows] for p in range(3)], thirds(inverse_ref[...]), NT)
        factor_ref[rows:size, 0:rows] = left
        leave(factor_ref.at[rows:size, 0:rows], factor_out.at[rows:size, 0:rows], out_sem.at[0])
        yield
        parts = thirds(left)
        work[...] = gram[rows:size, rows:size] - six_terms(parts, parts, NT)
        yield
        for step in range(per):
            at, below = step * BLOCK, (step + 1) * BLOCK
            aug = augs[step]
            for p in range(per - step):
                aug[p] = work[at:below, at + p * BLOCK : below + p * BLOCK]
            for j in range(BLOCK // PANEL):
                eliminate_panel(aug, j)
                yield
            upper = jnp.where(row <= column, aug[0], 0.0)
            factor_ref[rows + at : rows + below, rows + at : rows + below] = upper.T
            if step > 0:
                factor_ref[rows : rows + at, rows + at : rows + below] = jnp.zeros((at, BLOCK), jnp.float32)
            if below < rows:
                across = jnp.concatenate([aug[p] for p in range(1, per - step)], axis=1)
                factor_ref[rows + below : size, rows + at : rows + below] = across.T
                work[below:rows, below:rows] = work[below:rows, below:rows] - self_product(thirds(across))
            yield
        loads[0].wait()
        leave(factor_ref.at[0:rows, :], factor_out.at[0:rows, :], out_sem.at[1])
        leave(factor_ref.at[rows:size, rows:size], factor_out.at[rows:size, rows:size], out_sem.at[2])

    for _ in itertools.zip_longest(basis_chain(), factor_chain()):
        pass
    for copy in outgoing:
        copy.wait()


def fast_linear(columns, early, late, lead, inverse, start_basis, high, low):
    size, rank = start_basis.shape
    rows, width = size // 2, high.shape[1]
    vmem = pl.BlockSpec(memory_space=pltpu.VMEM)
    anywhere = pl.BlockSpec(memory_space=pl.ANY)
    return pl.pallas_call(
        functools.partial(fast_linear_kernel, lax.axis_size("col"), columns),
        out_shape=(
            jax.ShapeDtypeStruct((size, size), jnp.float32),
            jax.ShapeDtypeStruct((size, rank), jnp.float32),
            jax.ShapeDtypeStruct((rank, 1, width), jnp.float32),
        ),
        in_specs=[vmem, vmem, anywhere, vmem, vmem, anywhere, anywhere],
        out_specs=(anywhere, anywhere, anywhere),
        scratch_shapes=[
            pltpu.VMEM((size, size), jnp.float32),
            pltpu.VMEM((size, rank), jnp.float32),
            pltpu.VMEM((size, size), jnp.float32),
            pltpu.VMEM((3, size, size), jnp.bfloat16),
            pltpu.VMEM((rows, rows), jnp.float32),
            pltpu.VMEM((2, rank, rank), jnp.float32),
            pltpu.VMEM((size, width), jnp.bfloat16),
            pltpu.VMEM((size, width), jnp.bfloat16),
            pltpu.VMEM((rank, width), jnp.float32),
            pltpu.SemaphoreType.DMA((3,)),
            pltpu.SemaphoreType.DMA((4,)),
            pltpu.SemaphoreType.DMA((width // min(CHUNK, width),)),
            *[pltpu.VMEM((rows // BLOCK - step, BLOCK, BLOCK), jnp.float32) for step in range(rows // BLOCK)],
        ],
        name="fast_linear",
    )(early, late, lead, inverse, start_basis, high, low)


def per_device(tensor, start_basis):
    modes, cols = lax.axis_size("mode"), lax.axis_size("col")
    depth = tensor.shape[1]
    columns = depth * tensor.shape[2] * cols
    if fast_case(modes, cols, tensor.shape):
        high, low, early, lead, inverse, late = fast_gather(tensor, columns)
        return fast_linear(columns, early, late, lead, inverse, start_basis, high, low)
    flat, packed = gather(tensor)
    return linear(columns, depth, packed, start_basis, flat)


def solution(mesh):
    in_specs = (P("mode", "col", None), P())
    out_specs = (P(), P(), P(None, "col", "mode"))
    return jax.shard_map(
        per_device, mesh=mesh, in_specs=in_specs, out_specs=out_specs, check_vma=False
    )
```

```python
import functools
import itertools

import jax
import jax.numpy as jnp
from jax import lax
from jax.experimental import pallas as pl
from jax.experimental.pallas import tpu as pltpu
from jax.sharding import PartitionSpec as P

POWER = 2
BLOCK = 128
PANEL = 8
CHUNK = 512
MESH = pl.DeviceIdType.MESH


def halves(value):
    high = value.astype(jnp.bfloat16)
    low = (value - high.astype(jnp.float32)).astype(jnp.bfloat16)
    return high, low


def contract(left, right, dims):
    return lax.dot_general(left, right, (dims, ((), ())), preferred_element_type=jnp.float32)


def exact(left, right, dims):
    return lax.dot_general(
        left, right, (dims, ((), ())), precision=lax.Precision.HIGHEST,
        preferred_element_type=jnp.float32,
    )


NN = ((1,), (0,))
NT = ((1,), (1,))
TN = ((0,), (0,))


def thirds(value):
    high = value.astype(jnp.bfloat16)
    rest = value - high.astype(jnp.float32)
    middle = rest.astype(jnp.bfloat16)
    low = (rest - middle.astype(jnp.float32)).astype(jnp.bfloat16)
    return high, middle, low


def six_terms(left, right, dims):
    high, middle, low = right
    beside, along = (1, 0) if dims == NN else (0, 1)
    wide = jnp.concatenate([high, middle], axis=beside)
    first = contract(
        jnp.concatenate([left[0], left[1]], axis=1), jnp.concatenate([wide, wide], axis=along), dims
    )
    second = contract(
        jnp.concatenate([left[2], left[0]], axis=1), jnp.concatenate([high, low], axis=along), dims
    )
    count = second.shape[1]
    return first[:, 0:count] + (first[:, count:] + second)


def self_product(parts):
    high, middle, low = parts
    pair = jnp.concatenate([high, middle], axis=1)
    product = contract(pair, pair, TN)
    small = contract(high, low, TN)
    count = small.shape[0]
    rest = (product[0:count, count:] + product[count:, 0:count]) + (product[count:, count:] + (small + small.T))
    return product[0:count, 0:count] + rest


def split3(value):
    high = value.astype(jnp.bfloat16).astype(jnp.float32)
    rest = value - high
    middle = rest.astype(jnp.bfloat16).astype(jnp.float32)
    return high, middle, rest - middle


def spread(tile, lane):
    return jnp.broadcast_to(tile[:, lane : lane + 1], tile.shape)


def eliminate_panel(aug, j):
    parts, size, _ = aug.shape
    first = PANEL * j
    after = first + PANEL
    below = after + PANEL
    rows = [[aug[p, pl.ds(first + t, PANEL, stride=0), :] for p in range(parts)] for t in range(PANEL)]
    entry = {}
    for s in range(PANEL):
        for t in range(s + 1):
            entry[s, t] = spread(rows[t][0], first + s)
    if after < size:
        following = [aug[p, after:below, :] for p in range(parts)]
        column = [spread(following[0], first + t) for t in range(PANEL)]
    for t in range(PANEL):
        inverse = 1.0 / entry[t, t]
        for s in range(t + 1, PANEL):
            ratio = entry[s, t] * inverse
            for u in range(s, PANEL):
                entry[u, s] = entry[u, s] - ratio * entry[u, t]
            rows[s] = [a - ratio * b for a, b in zip(rows[s], rows[t])]
        scale = lax.rsqrt(entry[t, t])
        for p in range(parts):
            aug[p, first + t : first + t + 1, :] = (rows[t][p] * scale)[0:1]
        if after < size:
            ratio = column[t] * inverse
            for u in range(t + 1, PANEL):
                column[u] = column[u] - ratio * entry[u, t]
            following = [a - ratio * b for a, b in zip(following, rows[t])]
    if after < size:
        for p in range(parts):
            aug[p, after:below, :] = following[p]
    if below < size:
        rights = []
        for p in range(parts):
            high, middle, low = split3(aug[p, first:after, :])
            if p == 0:
                left = jnp.concatenate([high, high, middle, high, low, middle], axis=0).astype(jnp.bfloat16)
            rights.append(jnp.concatenate([high, middle, high, low, high, middle], axis=0).astype(jnp.bfloat16))
        update = contract(left, jnp.concatenate(rights, axis=1), TN)
        for p in range(parts):
            aug[p, below:size, :] = aug[p, below:size, :] - update[below:size, p * size : (p + 1) * size]


def eliminate(augs):
    for j in range(BLOCK // PANEL):
        for aug in augs:
            eliminate_panel(aug, j)


def load_augmented(aug, matrix):
    size = matrix.shape[0]
    aug[0] = matrix
    if aug.shape[0] > 1:
        row = lax.broadcasted_iota(jnp.int32, (size, size), 0)
        column = lax.broadcasted_iota(jnp.int32, (size, size), 1)
        aug[1] = jnp.where(row == column, 1.0, 0.0).astype(jnp.float32)


def lower_blocks(blocks):
    return [(i, k) for i in range(blocks) for k in range(i + 1)]


def stages_of(modes, cols):
    stages, stride = [], 1
    first = 2 if cols % 2 == 0 else 1
    if first > 1:
        stages.append((1, first, False))
        stride = first
    second = 2 if (cols // stride) % 2 == 0 else 1
    stages.append((stride, second, True))
    stride *= second
    if cols // stride > 1:
        stages.append((stride, cols // stride, False))
    return stages


def round_up(value, unit):
    return -(-value // unit) * unit


def layout_of(size, modes, cols):
    pairs = lower_blocks(size // BLOCK)
    rows = size // modes
    inner = []
    if rows % BLOCK == 0 and modes > 1:
        inner = lower_blocks(rows // BLOCK)
    per = rows // BLOCK
    extent = round_up(len(inner) * BLOCK, 8 * cols)
    where = {}
    for m in range(modes):
        for n, (i, k) in enumerate(inner):
            where[m * per + i, m * per + k] = m * extent + n * BLOCK
    outer = [pair for pair in pairs if pair not in where]
    for n, pair in enumerate(outer):
        where[pair] = modes * extent + n * BLOCK
    return where, inner, extent, outer, round_up(len(outer) * BLOCK, 8 * modes * cols)


def members_of(stages, modes):
    return [count * (modes if with_mode else 1) for _, count, with_mode in stages]


def gather_kernel(modes, cols, x_ref, flat_ref, total_ref, local, acc_in, acc_out, main, cross, *rest):
    mode, col = lax.axis_index("mode"), lax.axis_index("col")
    all_stages = stages_of(modes, cols)
    col_stages = [(stride, count, False) for stride, count, _ in all_stages]
    n = len(all_stages)
    slots_in, slots_out = rest[:n], rest[n : 2 * n]
    local_sem, piece_send, piece_recv, swap_send, swap_recv, in_sems, out_sems, share_in, share_out = rest[2 * n :]
    rows, depth, length = x_ref.shape
    size = rows * modes
    width = length // modes
    chunk = min(CHUNK, width)
    per = width // chunk
    chunks = depth * per
    where, inner, in_extent, outer, out_extent = layout_of(size, modes, cols)

    def position(stage):
        stride, count, with_mode = stage
        place = lax.rem(lax.div(col, stride), count)
        return place * modes + mode if with_mode else place

    def members(stage):
        return stage[1] * (modes if stage[2] else 1)

    def peer(stage, offset):
        stride, count, with_mode = stage
        other = lax.rem(position(stage) + offset, members(stage))
        place = lax.div(other, modes) if with_mode else other
        there = col + (place - lax.rem(lax.div(col, stride), count)) * stride
        return other, (lax.rem(other, modes) if with_mode else mode, there)

    partners = [(lax.rem(mode + d, modes), col) for d in range(1, modes)]
    greeted = []
    for stage in all_stages:
        greeted += [peer(stage, d)[1] for d in range(1, members(stage))]
    barrier = pltpu.get_barrier_semaphore()
    for device in greeted:
        pl.semaphore_signal(barrier, inc=1, device_id=device, device_id_type=MESH)
    pl.semaphore_wait(barrier, len(greeted))

    own_rows = pl.ds(pl.multiple_of(mode * rows, rows), rows)

    def spans(c):
        layer, part = lax.div(c, per), lax.rem(c, per)
        return layer, part * chunk, pl.multiple_of(layer * width + part * chunk, chunk)

    def piece(c, d):
        layer, start, target = spans(c)
        source = pl.multiple_of(lax.rem(mode + d, modes) * width + start, chunk)
        return pltpu.make_async_remote_copy(
            src_ref=x_ref.at[:, layer, pl.ds(source, chunk)],
            dst_ref=flat_ref.at[own_rows, pl.ds(target, chunk)],
            send_sem=piece_send.at[d - 1, c],
            recv_sem=piece_recv.at[d - 1, c],
            device_id=partners[d - 1],
            device_id_type=MESH,
        )

    def load(c):
        layer, part = lax.div(c, per * modes), lax.rem(c, per * modes)
        source = pl.multiple_of(part * chunk, chunk)
        target = pl.multiple_of(layer * length + part * chunk, chunk)
        return pltpu.make_async_copy(
            x_ref.at[:, layer, pl.ds(source, chunk)], local.at[:, pl.ds(target, chunk)], local_sem.at[c]
        ), target

    def begin(c, carry):
        for d in range(1, modes):
            piece(c, d).start()
        return carry

    def begin_load(c, carry):
        load(c)[0].start()
        return carry

    early = max(chunks // 2, 1)
    lax.fori_loop(0, early, begin, 0)
    lax.fori_loop(0, chunks * modes, begin_load, 0)

    main[...] = jnp.zeros_like(main)
    cross[...] = jnp.zeros_like(cross)

    def accumulate_in(c, carry):
        copy, target = load(c)
        copy.wait()
        if inner:
            high, low = halves(local[:, pl.ds(target, chunk)])
            main[0:rows, 0:rows] += contract(high, high, NT)
            cross[0:rows, 0:rows] += contract(high, low, NT)
        return carry

    lax.fori_loop(0, chunks * modes, accumulate_in, 0)
    for layer in range(depth):
        source = pl.multiple_of(layer * length + mode * width, chunk)
        flat_ref[own_rows, layer * width : (layer + 1) * width] = local[:, pl.ds(source, width)]

    def pack(acc, pairs, extent):
        for at, (i, k) in enumerate(pairs):
            tall, wide = slice(i * BLOCK, (i + 1) * BLOCK), slice(k * BLOCK, (k + 1) * BLOCK)
            acc[at * BLOCK : (at + 1) * BLOCK, :] = main[tall, wide] + (cross[tall, wide] + cross[wide, tall].T)
        used = len(pairs) * BLOCK
        if used < extent:
            acc[used:, :] = jnp.zeros((extent - used, BLOCK), jnp.float32)

    def scatter_sum(stages, acc, extent, slots, sems, target):
        base, bases = 0, []
        for g, stage in enumerate(stages):
            count = members(stage)
            part = extent // count
            copies = []
            for d in range(1, count):
                other, device = peer(stage, d)
                copy = pltpu.make_async_remote_copy(
                    src_ref=acc.at[pl.ds(pl.multiple_of(base + other * part, 8), part), :],
                    dst_ref=slots[g].at[d - 1],
                    send_sem=sems.at[0, g, d - 1],
                    recv_sem=sems.at[1, g, d - 1],
                    device_id=device,
                    device_id_type=MESH,
                )
                copy.start()
                copies.append(copy)
            base = base + position(stage) * part
            extent = part
            bases.append((base, part))
            for copy in copies:
                copy.wait()
            mine = pl.ds(pl.multiple_of(base, 8), part)
            added = acc[mine, :]
            for d in range(1, count):
                added = added + slots[g][d - 1]
            if g < len(stages) - 1:
                acc[mine, :] = added
            else:
                total_ref[pl.ds(pl.multiple_of(target + base, 8), part), :] = added
        return bases

    def share(stages, bases, targets, sems):
        for g in reversed(range(len(stages))):
            stage = stages[g]
            base, part = bases[g]
            copies = []
            for d in range(1, members(stage)):
                for t, target in enumerate(targets):
                    mine = pl.ds(pl.multiple_of(target + base, 8), part)
                    copy = pltpu.make_async_remote_copy(
                        src_ref=total_ref.at[mine, :],
                        dst_ref=total_ref.at[mine, :],
                        send_sem=sems.at[0, g, (d - 1) * len(targets) + t],
                        recv_sem=sems.at[1, g, (d - 1) * len(targets) + t],
                        device_id=peer(stage, d)[1],
                        device_id_type=MESH,
                    )
                    copy.start()
                    copies.append(copy)
            for copy in copies:
                copy.wait()

    def accumulate_out(c, carry):
        for d in range(1, modes):
            piece(c, d).wait_recv()
        high, low = halves(flat_ref[:, pl.ds(spans(c)[2], chunk)])
        if inner:
            for m in range(1, modes):
                tall, wide = slice(m * rows, (m + 1) * rows), slice(0, m * rows)
                main[tall, wide] += contract(high[tall, :], high[wide, :], NT) + contract(low[tall, :], high[wide, :], NT)
                cross[tall, wide] += contract(high[tall, :], low[wide, :], NT)
        else:
            main[...] += contract(high, high, NT)
            cross[...] += contract(high, low, NT)
        return carry

    swaps = []
    if inner:
        pack(acc_in, inner, in_extent)
        main[...] = jnp.zeros_like(main)
        cross[...] = jnp.zeros_like(cross)
        bases = scatter_sum(col_stages, acc_in, in_extent, slots_in, in_sems, mode * in_extent)
        base, part = bases[-1]
        mine = pl.ds(pl.multiple_of(mode * in_extent + base, 8), part)
        for d in range(1, modes):
            swap = pltpu.make_async_remote_copy(
                src_ref=total_ref.at[mine, :],
                dst_ref=total_ref.at[mine, :],
                send_sem=swap_send.at[d - 1],
                recv_sem=swap_recv.at[d - 1],
                device_id=partners[d - 1],
                device_id_type=MESH,
            )
            swap.start()
            swaps.append(swap)
    lax.fori_loop(early, chunks, begin, 0)
    lax.fori_loop(0, early, accumulate_out, 0)
    if inner:
        for swap in swaps:
            swap.wait()
        share(col_stages, bases, [m * in_extent for m in range(modes)], share_in)
    lax.fori_loop(early, chunks, accumulate_out, 0)

    pack(acc_out, outer, out_extent)
    bases = scatter_sum(all_stages, acc_out, out_extent, slots_out, out_sems, modes * in_extent)
    share(all_stages, bases, [modes * in_extent], share_out)

    def end(c, carry):
        for d in range(1, modes):
            piece(c, d).wait_send()
        return carry

    lax.fori_loop(0, chunks, end, 0)


def gather(tensor):
    modes, cols = lax.axis_size("mode"), lax.axis_size("col")
    rows, depth, length = tensor.shape
    size = rows * modes
    width = length // modes
    chunks = depth * (width // min(CHUNK, width))
    stages = stages_of(modes, cols)
    _, inner, in_extent, _, out_extent = layout_of(size, modes, cols)
    in_extent = max(in_extent, 8 * cols)
    slots_in, slots_out, extent_in, extent, most = [], [], in_extent, out_extent, 1
    for stride, count, with_mode in stages:
        extent_in = extent_in // count
        slots_in.append(pltpu.VMEM((max(count - 1, 1), extent_in, BLOCK), jnp.float32))
        count = count * (modes if with_mode else 1)
        extent = extent // count
        slots_out.append(pltpu.VMEM((max(count - 1, 1), extent, BLOCK), jnp.float32))
        most = max(most, count - 1)
    dma = pltpu.SemaphoreType.DMA
    vmem = pl.BlockSpec(memory_space=pltpu.VMEM)
    packed = (modes * in_extent if inner else 0) + out_extent
    return pl.pallas_call(
        functools.partial(gather_kernel, modes, cols),
        out_shape=(
            jax.ShapeDtypeStruct((size, depth * width), jnp.float32),
            jax.ShapeDtypeStruct((packed, BLOCK), jnp.float32),
        ),
        in_specs=[pl.BlockSpec(memory_space=pl.ANY)],
        out_specs=(vmem, vmem),
        scratch_shapes=[
            pltpu.VMEM((rows, depth * length), jnp.float32),
            pltpu.VMEM((in_extent, BLOCK), jnp.float32),
            pltpu.VMEM((out_extent, BLOCK), jnp.float32),
            pltpu.VMEM((size, size), jnp.float32),
            pltpu.VMEM((size, size), jnp.float32),
            *slots_in,
            *slots_out,
            dma((chunks * modes,)),
            *[dma((max(modes - 1, 1), chunks))] * 2,
            *[dma((max(modes - 1, 1),))] * 2,
            *[dma((2, len(stages), most))] * 2,
            dma((2, len(stages), most * modes)),
            dma((2, len(stages), most)),
        ],
        compiler_params=pltpu.CompilerParams(collective_id=0, has_side_effects=True),
        name="gather",
    )(tensor)


def linear_kernel(columns, where, packed_ref, start_ref, flat_ref, factor_ref, basis_ref, core_ref, gram, work, image, aug_f, aug_b, core, core_sem):
    size, rank = start_ref.shape
    blocks = size // BLOCK
    row = lax.broadcasted_iota(jnp.int32, (BLOCK, BLOCK), 0)
    column = lax.broadcasted_iota(jnp.int32, (BLOCK, BLOCK), 1)
    scale = 1.0 / columns
    for (i, k), at in where.items():
        scaled = packed_ref[at : at + BLOCK, :] * scale
        gram[i * BLOCK : (i + 1) * BLOCK, k * BLOCK : (k + 1) * BLOCK] = scaled
        work[i * BLOCK : (i + 1) * BLOCK, k * BLOCK : (k + 1) * BLOCK] = scaled
        if i != k:
            gram[k * BLOCK : (k + 1) * BLOCK, i * BLOCK : (i + 1) * BLOCK] = scaled.T

    for step in range(max(blocks, POWER)):
        augs = []
        if step < blocks:
            at = step * BLOCK
            load_augmented(aug_f, work[at : at + BLOCK, at : at + BLOCK])
            augs.append(aug_f)
        if step < POWER:
            source = start_ref if step == 0 else basis_ref
            image[...] = exact(gram[...], source[...], NN)
            load_augmented(aug_b, exact(image[...], image[...], TN))
            augs.append(aug_b)
        eliminate(augs)
        if step < POWER:
            basis_ref[...] = exact(image[...], aug_b[1], NT)
        if step < blocks:
            upper = jnp.where(row <= column, aug_f[0], 0.0)
            factor_ref[at : at + BLOCK, at : at + BLOCK] = upper.T
            if step > 0:
                factor_ref[0:at, at : at + BLOCK] = jnp.zeros((at, BLOCK), jnp.float32)
            below = at + BLOCK
            if below < size:
                inverse = aug_f[1]
                left = exact(work[below:size, at : at + BLOCK], inverse, NT)
                factor_ref[below:size, at : at + BLOCK] = left
                work[below:size, below:size] = work[below:size, below:size] - exact(left, left, NT)

    high, low = halves(basis_ref[...])
    depth, length = core_ref.shape[1:]
    width = min(CHUNK, length)
    copies = []
    for start in range(0, depth * length, width):
        part = slice(start, start + width)
        flat_high, flat_low = halves(flat_ref[:, part])
        core[:, part] = contract(high, flat_high, TN) + contract(high, flat_low, TN) + contract(low, flat_high, TN)
        layer, offset = divmod(start, length)
        copy = pltpu.make_async_copy(
            core.at[:, part], core_ref.at[:, layer, offset : offset + width], core_sem.at[len(copies)]
        )
        copy.start()
        copies.append(copy)
    for copy in copies:
        copy.wait()


def linear(columns, depth, packed, start_basis, flat):
    size, rank = start_basis.shape
    length = flat.shape[1] // depth
    where = layout_of(size, lax.axis_size("mode"), lax.axis_size("col"))[0]
    vmem = pl.BlockSpec(memory_space=pltpu.VMEM)
    return pl.pallas_call(
        functools.partial(linear_kernel, columns, where),
        out_shape=(
            jax.ShapeDtypeStruct((size, size), jnp.float32),
            jax.ShapeDtypeStruct((size, rank), jnp.float32),
            jax.ShapeDtypeStruct((rank, depth, length), jnp.float32),
        ),
        in_specs=[vmem] * 3,
        out_specs=(vmem, vmem, pl.BlockSpec(memory_space=pl.ANY)),
        scratch_shapes=[
            pltpu.VMEM((size, size), jnp.float32),
            pltpu.VMEM((size, size), jnp.float32),
            pltpu.VMEM((size, rank), jnp.float32),
            pltpu.VMEM((2, BLOCK, BLOCK), jnp.float32),
            pltpu.VMEM((2, rank, rank), jnp.float32),
            pltpu.VMEM((rank, flat.shape[1]), jnp.float32),
            pltpu.SemaphoreType.DMA((flat.shape[1] // min(CHUNK, length),)),
        ],
        name="linear",
    )(packed, start_basis, flat)


def fast_case(modes, cols, shape):
    rows, depth, length = shape
    return modes == 2 and depth == 1 and rows % (2 * BLOCK) == 0 and cols % 4 == 0 and length % (2 * BLOCK) == 0


STRIPS = 8
LATE = 4
EARLY = 4
HELD = 3
PIECES = STRIPS + 3


def fast_cuts(strip):
    return sorted([k * strip for k in range(STRIPS + 1)] + [2 * strip + strip // 2, 6 * strip + strip // 2])


def fast_layout(rows, cols):
    per = rows // BLOCK
    strip = rows // STRIPS
    first = rows - LATE * strip
    inner = lower_blocks(per)
    unit = 8 * cols
    extents = [round_up(len(inner) * BLOCK, unit), round_up(first * per, unit), round_up((rows - first) * per, unit)]
    starts, at = [], 0
    for extent in extents:
        starts.append(at)
        at += 2 * extent
    return per, strip, first, inner, extents, starts, at


def fast_gather_kernel(cols, columns, x_ref, high_out, low_out, early_out, lead_out, inverse_out, late_ref, local, recv, early_ref, lead_ref, inverse_ref, own_high, own_low, other_high, other_low, main, cross, work, aug, acc_in, acc_a, acc_b, *rest):
    slots, sems, hello = rest[:-2], rest[-2], rest[-1]
    mode, col = lax.axis_index("mode"), lax.axis_index("col")
    other_mode = 1 - mode
    rows, _, length = x_ref.shape
    width = length // 2
    chips = cols // 2
    per, strip, first, inner, extents, starts, _ = fast_layout(rows, cols)
    core, chip = lax.rem(col, 2), lax.div(col, 2)
    names = {}
    pending = {}

    def sem(*name):
        return sems.at[names.setdefault(name, len(names))]

    def drain(*kinds):
        for name in [name for name in pending if name[0] in kinds]:
            pending.pop(name).wait_send()

    def push(source, target, device, *name):
        if name in pending:
            pending.pop(name).wait_send()
        copy = pltpu.make_async_remote_copy(
            src_ref=source, dst_ref=target, send_sem=sem("send", *name), recv_sem=sem("recv", *name),
            device_id=device, device_id_type=MESH,
        )
        copy.start()
        pending[name] = copy
        return copy

    def volley(name, triples, whole):
        if (name,) in pending:
            pending.pop((name,)).wait_send()

        def copy_of(source, target, device):
            return pltpu.make_async_remote_copy(
                src_ref=source, dst_ref=target, send_sem=sem("send", name), recv_sem=sem("recv", name),
                device_id=device, device_id_type=MESH,
            )

        for triple in triples:
            copy_of(*triple).start()
        pending[(name,)] = copy_of(whole, whole, sibling)
        return [pending[(name,)]]

    sibling = (mode, chip * 2 + 1 - core)
    partner = (other_mode, col)
    plane = []
    for d in range(1, chips):
        place = lax.rem(chip + d, chips)
        plane.append((place, (mode, place * 2 + core)))

    line = chips // 2
    place = lax.div(chip, 2)
    beside = (mode, (place * 2 + 1 - lax.rem(chip, 2)) * 2 + core)
    above, under = (mode, col + 4), (mode, col - 4)
    has_above, has_under = place < line - 1, place > 0

    def hail(semaphore, device):
        pl.semaphore_signal(semaphore, inc=1, device_id=device, device_id_type=MESH)

    barrier = pltpu.get_barrier_semaphore()
    for device in (partner, sibling, beside):
        hail(barrier, device)
    pl.when(has_above)(lambda: hail(barrier, above))
    pl.when(has_under)(lambda: hail(barrier, under))
    pl.semaphore_wait(barrier, 3 + has_above.astype(jnp.int32) + has_under.astype(jnp.int32))

    def meet_line():
        pl.when(has_under)(lambda: pl.semaphore_wait(hello.at[0], 1))
        pl.when(has_above)(lambda: hail(hello.at[0], above))
        pl.when(has_above)(lambda: pl.semaphore_wait(hello.at[1], 1))
        pl.when(has_under)(lambda: hail(hello.at[1], under))
        hail(hello.at[2], beside)

    def meet_beside():
        pl.semaphore_wait(hello.at[2], 1)
        hail(hello.at[3], partner)

    def meet_across():
        pl.semaphore_wait(hello.at[3], 1)

    pieces = []
    away = pl.ds(pl.multiple_of(other_mode * width, width), width)

    cuts = fast_cuts(strip)

    def piece_of(source, target, k):
        return pltpu.make_async_remote_copy(
            src_ref=source, dst_ref=target, send_sem=sem("pieces"), recv_sem=sem("piece", k),
            device_id=partner, device_id_type=MESH,
        )

    def send_piece(k):
        if k < PIECES - 2:
            span, start, count = slice(cuts[k], cuts[k + 1]), 0, width
        else:
            span, start, count = slice(rows - strip, rows), (k - PIECES + 2) * (width // 2), width // 2
        source = pl.ds(pl.multiple_of(other_mode * width + start, BLOCK), count)
        pieces.append(piece_of(x_ref.at[span, 0, source], recv.at[span, start : start + count], k))
        pieces[k].start()

    for k in range(EARLY):
        send_piece(k)

    loads = []
    part = length // 4
    for c in range(4):
        span = slice(c * part, (c + 1) * part)
        copy = pltpu.make_async_copy(x_ref.at[:, 0, span], local.at[:, span], sem("local", c))
        copy.start()
        loads.append(copy)
    for c in range(4):
        if c == 1:
            meet_line()
        loads[c].wait()
        high, low = halves(local[:, c * part : (c + 1) * part])
        if c == 0:
            main[...] = contract(high, high, NT)
            cross[...] = contract(high, low, NT)
        else:
            main[...] += contract(high, high, NT)
            cross[...] += contract(high, low, NT)

    for at, (i, k) in enumerate(inner):
        tall, wide = slice(i * BLOCK, (i + 1) * BLOCK), slice(k * BLOCK, (k + 1) * BLOCK)
        acc_in[at * BLOCK : (at + 1) * BLOCK, :] = main[tall, wide] + (cross[tall, wide] + cross[wide, tall].T)

    def fill(acc, used):
        if used < acc.shape[0]:
            acc[used:, :] = jnp.zeros((acc.shape[0] - used, BLOCK), jnp.float32)

    def rows_at(base, count):
        return pl.ds(pl.multiple_of(base, 8), count)

    def core_send(acc, slot):
        half = acc.shape[0] // 2
        return push(acc.at[rows_at((1 - core) * half, half), :], slot.at[...], sibling, "core")

    def core_add(acc, slot, copy):
        half = acc.shape[0] // 2
        copy.wait_recv()
        mine = rows_at(core * half, half)
        acc[mine, :] = acc[mine, :] + slot[...]

    def plane_send(acc, slot):
        half = acc.shape[0] // 2
        share = half // chips
        triples = []
        for d, (place, device) in enumerate(plane):
            triples.append((acc.at[rows_at(core * half + place * share, share), :], slot.at[d], device))
        return volley("plane", triples, slot)

    def plane_add(acc, slot, copies, total, start):
        half = acc.shape[0] // 2
        share = half // chips
        base = core * half + chip * share
        for copy in copies:
            copy.wait_recv()
        added = acc[rows_at(base, share), :]
        for d in range(chips - 1):
            added = added + slot[d]
        total[rows_at(start + mode * acc.shape[0] + base, share), :] = added

    def swap(acc, total, start, phase):
        half = acc.shape[0] // 2
        share = half // chips
        mine = rows_at(start + mode * acc.shape[0] + core * half + chip * share, share)
        return push(total.at[mine, :], total.at[mine, :], partner, "swap", phase)

    def plane_share(acc, total, start):
        half = acc.shape[0] // 2
        share = half // chips
        triples = []
        for _, device in plane:
            for m in range(2):
                mine = rows_at(start + m * acc.shape[0] + core * half + chip * share, share)
                triples.append((total.at[mine, :], total.at[mine, :], device))
        return volley("share", triples, total.at[0 : len(triples) * share, :])

    def direct_share(acc, total, start):
        half = acc.shape[0] // 2
        share = half // chips
        mine = rows_at(start + mode * acc.shape[0] + core * half + chip * share, share)
        devices = [(other_mode, lax.rem(chip + d, chips) * 2 + core) for d in range(chips)]
        devices += [device for _, device in plane]
        triples = [(total.at[mine, :], total.at[mine, :], device) for device in devices]
        return volley("direct", triples, total.at[0 : len(triples) * share, :])

    def core_share(acc, total, start):
        half = acc.shape[0] // 2
        triples = []
        for m in range(2):
            mine = rows_at(start + m * acc.shape[0] + core * half, half)
            triples.append((total.at[mine, :], total.at[mine, :], sibling))
        return volley("both", triples, total.at[0 : 2 * half, :])

    def arrive(copies):
        for copy in copies:
            copy.wait_recv()

    outgoing = {}
    leaving = [0]

    def leave(source, target):
        lane = leaving[0] % len(loads)
        leaving[0] += 1
        if lane in outgoing:
            outgoing.pop(lane).wait()
        copy = pltpu.make_async_copy(source, target, sem("local", lane))
        copy.start()
        outgoing[lane] = copy

    def strips(begin, end, acc, offset, tall):
        span = slice(begin * strip, end * strip)
        if end < STRIPS:
            steps = [(pieces[cuts.index(begin * strip) : cuts.index(end * strip)], 0, width)]
        else:
            steps = [([pieces[-2]], 0, width // 2), ([pieces[-1]], width // 2, width // 2)]
        count = (end - begin) * strip
        value = None
        for copies, start, wide in steps:
            arrive(copies)
            part = slice(start, start + wide)
            high, low = halves(recv[span, part])
            other_high[span, part] = high
            other_low[span, part] = low
            both = contract(own_high[:, part], jnp.concatenate([high, low], axis=0), NT)
            added = both[:, 0:count] + (both[:, count:] + contract(own_low[:, part], high, NT))
            value = added if value is None else value + added
        target = pl.ds(pl.multiple_of(other_mode * rows + begin * strip, strip), count)
        leave(other_high.at[span, :], high_out.at[target, :])
        leave(other_low.at[span, :], low_out.at[target, :])
        value = value.T
        for c in range(per):
            at = c * tall + begin * strip - offset
            acc[at : at + count, :] = value[:, c * BLOCK : (c + 1) * BLOCK]

    fill(acc_in, len(inner) * BLOCK)
    meet_beside()
    copy = core_send(acc_in, slots[0])
    mine = local[:, pl.ds(pl.multiple_of(mode * width, width), width)]
    high, low = halves(mine)
    own_high[...] = high
    own_low[...] = low
    core_add(acc_in, slots[0], copy)
    copies = plane_send(acc_in, slots[1])
    target = pl.ds(pl.multiple_of(mode * rows, rows), rows)
    leave(own_high, high_out.at[target, :])
    leave(own_low, low_out.at[target, :])
    plane_add(acc_in, slots[1], copies, early_ref, starts[0])
    meet_across()
    copy = swap(acc_in, early_ref, starts[0], 0)
    for k in range(EARLY, PIECES - HELD):
        send_piece(k)
    strips(0, 1, acc_a, 0, first)
    arrive([copy])
    copies = plane_share(acc_in, early_ref, starts[0])
    drain("core", "plane", "swap")
    strips(1, 2, acc_a, 0, first)
    arrive(copies)
    arrive(core_share(acc_in, early_ref, starts[0]))

    scale = 1.0 / columns
    for at, (i, k) in enumerate(inner):
        tall, wide = slice(i * BLOCK, (i + 1) * BLOCK), slice(k * BLOCK, (k + 1) * BLOCK)
        work[tall, wide] = early_ref[starts[0] + at * BLOCK : starts[0] + (at + 1) * BLOCK, :] * scale
    lead_ref[...] = jnp.zeros_like(lead_ref)
    inverse_ref[...] = jnp.zeros_like(inverse_ref)
    row = lax.broadcasted_iota(jnp.int32, (BLOCK, BLOCK), 0)
    column = lax.broadcasted_iota(jnp.int32, (BLOCK, BLOCK), 1)
    for step in range(per):
        at, below = step * BLOCK, (step + 1) * BLOCK
        load_augmented(aug, work[at:below, at:below])
        eliminate([aug])
        lead_ref[at:below, at:below] = jnp.where(row <= column, aug[0], 0.0).T
        inverse = aug[1]
        inverse_ref[at:below, at:below] = inverse
        if step > 0:
            inverse_ref[at:below, 0:at] = -exact(inverse, exact(lead_ref[at:below, 0:at], inverse_ref[0:at, 0:at], NN), NN)
        if below < rows:
            left = exact(work[below:rows, at:below], inverse, NT)
            lead_ref[below:rows, at:below] = left
            work[below:rows, below:rows] = work[below:rows, below:rows] - exact(left, left, NT)
        if step == 0:
            strips(2, STRIPS - LATE, acc_a, 0, first)
            fill(acc_a, first * per)
            core_add(acc_a, slots[2], core_send(acc_a, slots[2]))
            copies = plane_send(acc_a, slots[3])
    plane_add(acc_a, slots[3], copies, early_ref, starts[1])
    copy = swap(acc_a, early_ref, starts[1], 1)
    for k in range(PIECES - HELD, PIECES):
        send_piece(k)
    leave(lead_ref, lead_out)
    leave(inverse_ref, inverse_out)
    strips(STRIPS - LATE, STRIPS - 2, acc_b, first, rows - first)
    arrive([copy])
    copies = plane_share(acc_a, early_ref, starts[1])
    drain("core", "plane", "swap", "both")
    strips(STRIPS - 2, STRIPS - 1, acc_b, first, rows - first)
    arrive(copies)
    copies = core_share(acc_a, early_ref, starts[1])
    drain("share")
    arrive(copies)
    leave(early_ref, early_out)
    strips(STRIPS - 1, STRIPS, acc_b, first, rows - first)
    fill(acc_b, (rows - first) * per)
    core_add(acc_b, slots[4], core_send(acc_b, slots[4]))
    plane_add(acc_b, slots[5], plane_send(acc_b, slots[5]), late_ref, 0)
    copies = direct_share(acc_b, late_ref, 0)
    drain("core", "plane", "both")
    piece_of(x_ref.at[:, 0, away], recv, 0).wait_send()
    for copy in outgoing.values():
        copy.wait()
    arrive(copies)
    copies = core_share(acc_b, late_ref, 0)
    drain("direct")
    arrive(copies)
    drain("both")


def fast_gather(tensor, columns):
    cols = lax.axis_size("col")
    rows, _, length = tensor.shape
    width = length // 2
    chips = cols // 2
    _, _, _, _, extents, starts, _ = fast_layout(rows, cols)
    slots = []
    for extent in extents:
        slots.append(pltpu.VMEM((extent // 2, BLOCK), jnp.float32))
        slots.append(pltpu.VMEM((chips - 1, extent // cols, BLOCK), jnp.float32))
    vmem = pl.BlockSpec(memory_space=pltpu.VMEM)
    anywhere = pl.BlockSpec(memory_space=pl.ANY)
    return pl.pallas_call(
        functools.partial(fast_gather_kernel, cols, columns),
        out_shape=(
            jax.ShapeDtypeStruct((2 * rows, width), jnp.bfloat16),
            jax.ShapeDtypeStruct((2 * rows, width), jnp.bfloat16),
            jax.ShapeDtypeStruct((starts[2], BLOCK), jnp.float32),
            jax.ShapeDtypeStruct((rows, rows), jnp.float32),
            jax.ShapeDtypeStruct((rows, rows), jnp.float32),
            jax.ShapeDtypeStruct((2 * extents[2], BLOCK), jnp.float32),
        ),
        in_specs=[anywhere],
        out_specs=(anywhere, anywhere, anywhere, anywhere, anywhere, vmem),
        scratch_shapes=[
            pltpu.VMEM((rows, length), jnp.float32),
            pltpu.VMEM((rows, width), jnp.float32),
            pltpu.VMEM((starts[2], BLOCK), jnp.float32),
            pltpu.VMEM((rows, rows), jnp.float32),
            pltpu.VMEM((rows, rows), jnp.float32),
            *[pltpu.VMEM((rows, width), jnp.bfloat16)] * 4,
            pltpu.VMEM((rows, rows), jnp.float32),
            pltpu.VMEM((rows, rows), jnp.float32),
            pltpu.VMEM((rows, rows), jnp.float32),
            pltpu.VMEM((2, BLOCK, BLOCK), jnp.float32),
            *[pltpu.VMEM((extent, BLOCK), jnp.float32) for extent in extents],
            *slots,
            pltpu.SemaphoreType.DMA((PIECES + 19,)),
            pltpu.SemaphoreType.REGULAR((4,)),
        ],
        compiler_params=pltpu.CompilerParams(collective_id=0, has_side_effects=True),
        name="fast_gather",
    )(tensor)


def fast_linear_kernel(cols, columns, early_ref, late_ref, lead_ref, inverse_ref, start_ref, high_ref, low_ref, factor_out, basis_out, core_ref, factor_ref, basis_ref, gram, split, work, aug_b, flat_high, flat_low, core, flat_sem, out_sem, core_sem, *augs):
    size, rank = start_ref.shape
    rows = size // 2
    width = core_ref.shape[2]
    per, _, first, inner, extents, starts, _ = fast_layout(rows, cols)
    loads = [
        pltpu.make_async_copy(lead_ref, factor_ref.at[0:rows, 0:rows], flat_sem.at[0]),
        pltpu.make_async_copy(high_ref, flat_high, flat_sem.at[1]),
        pltpu.make_async_copy(low_ref, flat_low, flat_sem.at[2]),
    ]
    for load in loads:
        load.start()

    scale = 1.0 / columns
    for m in range(2):
        for at, (i, k) in enumerate(inner):
            begin = starts[0] + m * extents[0] + at * BLOCK
            block = early_ref[begin : begin + BLOCK, :] * scale
            tall = slice(m * rows + i * BLOCK, m * rows + (i + 1) * BLOCK)
            wide = slice(m * rows + k * BLOCK, m * rows + (k + 1) * BLOCK)
            gram[tall, wide] = block
            if i != k:
                gram[wide, tall] = block.T
    pair = []
    for m in range(2):
        blocks = []
        for c in range(per):
            a = starts[1] + m * extents[1] + c * first
            b = m * extents[2] + c * (rows - first)
            blocks.append(jnp.concatenate([early_ref[a : a + first, :], late_ref[b : b + rows - first, :]], axis=0))
        pair.append(jnp.concatenate(blocks, axis=1))
    lower = (pair[0] + pair[1].T) * scale
    gram[rows:size, 0:rows] = lower
    gram[0:rows, rows:size] = lower.T
    for p, part in enumerate(thirds(gram[...])):
        split[p] = part

    row = lax.broadcasted_iota(jnp.int32, (BLOCK, BLOCK), 0)
    column = lax.broadcasted_iota(jnp.int32, (BLOCK, BLOCK), 1)
    factor_ref[0:rows, rows:size] = jnp.zeros((rows, rows), jnp.float32)
    outgoing = []

    def leave(source, target, semaphore):
        copy = pltpu.make_async_copy(source, target, semaphore)
        copy.start()
        outgoing.append(copy)

    def basis_chain():
        basis = start_ref[...]
        for _ in range(POWER):
            image = thirds(six_terms([split[p] for p in range(3)], thirds(basis), NN))
            load_augmented(aug_b, self_product(image))
            yield
            for j in range(rank // PANEL):
                eliminate_panel(aug_b, j)
                yield
            basis = six_terms(image, thirds(aug_b[1]), NT)
            yield
        basis_ref[...] = basis
        leave(basis_ref, basis_out, out_sem.at[3])
        for load in loads[1:]:
            load.wait()
        high, low = halves(basis)
        both = jnp.concatenate([high, low], axis=1)
        piece = min(2 * CHUNK, width)
        for n, start in enumerate(range(0, width, piece)):
            part = slice(start, start + piece)
            product = contract(both, flat_high[:, part], TN)
            core[:, part] = product[0:rank] + (product[rank:] + contract(high, flat_low[:, part], TN))
            leave(core.at[:, part], core_ref.at[:, 0, part], core_sem.at[n])
            yield

    def factor_chain():
        left = six_terms([split[p, rows:size, 0:rows] for p in range(3)], thirds(inverse_ref[...]), NT)
        factor_ref[rows:size, 0:rows] = left
        leave(factor_ref.at[rows:size, 0:rows], factor_out.at[rows:size, 0:rows], out_sem.at[0])
        yield
        parts = thirds(left)
        work[...] = gram[rows:size, rows:size] - six_terms(parts, parts, NT)
        yield
        for step in range(per):
            at, below = step * BLOCK, (step + 1) * BLOCK
            aug = augs[step]
            for p in range(per - step):
                aug[p] = work[at:below, at + p * BLOCK : below + p * BLOCK]
            for j in range(BLOCK // PANEL):
                eliminate_panel(aug, j)
                yield
            upper = jnp.where(row <= column, aug[0], 0.0)
            factor_ref[rows + at : rows + below, rows + at : rows + below] = upper.T
            if step > 0:
                factor_ref[rows : rows + at, rows + at : rows + below] = jnp.zeros((at, BLOCK), jnp.float32)
            if below < rows:
                across = jnp.concatenate([aug[p] for p in range(1, per - step)], axis=1)
                factor_ref[rows + below : size, rows + at : rows + below] = across.T
                work[below:rows, below:rows] = work[below:rows, below:rows] - self_product(thirds(across))
            yield
        loads[0].wait()
        leave(factor_ref.at[0:rows, :], factor_out.at[0:rows, :], out_sem.at[1])
        leave(factor_ref.at[rows:size, rows:size], factor_out.at[rows:size, rows:size], out_sem.at[2])

    for _ in itertools.zip_longest(basis_chain(), factor_chain()):
        pass
    for copy in outgoing:
        copy.wait()


def fast_linear(columns, early, late, lead, inverse, start_basis, high, low):
    size, rank = start_basis.shape
    rows, width = size // 2, high.shape[1]
    vmem = pl.BlockSpec(memory_space=pltpu.VMEM)
    anywhere = pl.BlockSpec(memory_space=pl.ANY)
    return pl.pallas_call(
        functools.partial(fast_linear_kernel, lax.axis_size("col"), columns),
        out_shape=(
            jax.ShapeDtypeStruct((size, size), jnp.float32),
            jax.ShapeDtypeStruct((size, rank), jnp.float32),
            jax.ShapeDtypeStruct((rank, 1, width), jnp.float32),
        ),
        in_specs=[vmem, vmem, anywhere, vmem, vmem, anywhere, anywhere],
        out_specs=(anywhere, anywhere, anywhere),
        scratch_shapes=[
            pltpu.VMEM((size, size), jnp.float32),
            pltpu.VMEM((size, rank), jnp.float32),
            pltpu.VMEM((size, size), jnp.float32),
            pltpu.VMEM((3, size, size), jnp.bfloat16),
            pltpu.VMEM((rows, rows), jnp.float32),
            pltpu.VMEM((2, rank, rank), jnp.float32),
            pltpu.VMEM((size, width), jnp.bfloat16),
            pltpu.VMEM((size, width), jnp.bfloat16),
            pltpu.VMEM((rank, width), jnp.float32),
            pltpu.SemaphoreType.DMA((3,)),
            pltpu.SemaphoreType.DMA((4,)),
            pltpu.SemaphoreType.DMA((width // min(CHUNK, width),)),
            *[pltpu.VMEM((rows // BLOCK - step, BLOCK, BLOCK), jnp.float32) for step in range(rows // BLOCK)],
        ],
        name="fast_linear",
    )(early, late, lead, inverse, start_basis, high, low)


def per_device(tensor, start_basis):
    modes, cols = lax.axis_size("mode"), lax.axis_size("col")
    depth = tensor.shape[1]
    columns = depth * tensor.shape[2] * cols
    if fast_case(modes, cols, tensor.shape):
        high, low, early, lead, inverse, late = fast_gather(tensor, columns)
        return fast_linear(columns, early, late, lead, inverse, start_basis, high, low)
    flat, packed = gather(tensor)
    return linear(columns, depth, packed, start_basis, flat)


def solution(mesh):
    in_specs = (P("mode", "col", None), P())
    out_specs = (P(), P(), P(None, "col", "mode"))
    return jax.shard_map(
        per_device, mesh=mesh, in_specs=in_specs, out_specs=out_specs, check_vma=False
    )
```
